256 devices in a mesh: dp: 4 (over x_hi, core), ctx: 64 (over x_lo, y, z).
Axes of the slice: x: 4 (x_hi: 2, x_lo: 2; x = x_hi * 2 + x_lo), y: 4, z: 8, core: 2. Of those that a mesh axis runs over, the one named last changes fastest.
Arguments:
- residual: bfloat16 [4096, 16, 1024], P('ctx', 'dp'), may hold values from -10 to 10
- projections: bfloat16 [4096, 16, 3072], P('ctx', 'dp'), may hold values from -8 to 8
- out_weight: bfloat16 [1024, 1024], replicated, may hold values from -0.1875 to 0.1875
- gain_one: float32 [1024], replicated, may hold values from 0.1 to 1.9
- up_weight: bfloat16 [1024, 2048], replicated, may hold values from -0.1875 to 0.1875
- conv_kernel: float32 [31, 1024], replicated, may hold values from -1 to 1
- gain_two: float32 [1024], replicated, may hold values from 0.1 to 1.9
- down_weight: bfloat16 [1024, 1024], replicated, may hold values from -0.1875 to 0.1875
- lengths: int32 [16], P('dp'), may hold values from 1024 to 4096, as said below
- out_grad: bfloat16 [4096, 16, 1024], P('ctx', 'dp'), may hold values from -0.0625 to 0.0625
Outputs:
- block_out: bfloat16 [4096, 16, 1024], P('ctx', 'dp')
- up_grad: float32 [2048, 1024], P(('dp', 'ctx'))
- down_grad: float32 [1024, 1024], P(('dp', 'ctx'))
- kernel_grad: float32 [1024, 31], P(('dp', 'ctx'))
- gain_one_grad: float32 [1024], P(('dp', 'ctx'))
- gain_two_grad: float32 [1024], P(('dp', 'ctx'))
The draws below stay inside these ranges and needn't reach their ends.
Inputs may be any that keep to these rules, and one draw needn't show every extreme that they name: `lengths`: utterance 0 has all 4096 frames valid.
All inputs are finite; a program needn't handle non-finite values.
Results may differ from the reference program's by a relative error of at most 0.02.
Values may be sent and summed in bfloat16 or wider, within the bound.
A program may use at most 128 MiB of HBM per device.

```python
import math
import jax
import jax.numpy as jnp
from jax import lax

D = 1024
HEADS = 16
HD = 64
KERNEL = 31
HALF = 15
NUTT = 16
LEN = 4096


def draw_projections(key, part):
    shape = (LEN, NUTT, HEADS, 3, HD)
    base_key = jax.random.fold_in(key, 11)
    spread = jnp.array([1.6, 1.6, 1.0], jnp.float32)[None, None, None, :, None]
    values = jax.random.truncated_normal(base_key, -4.0, 4.0, shape, jnp.float32) * spread
    return values.reshape(LEN, NUTT, 3 * D).astype(jnp.bfloat16)


def draw_residual(key, part):
    shape = (LEN, NUTT, D)
    row_scale = jnp.exp(jax.random.uniform(jax.random.fold_in(key, 32), (LEN, NUTT, 1), jnp.float32, math.log(0.1), 0.0))
    col_scale = jnp.exp(jax.random.uniform(jax.random.fold_in(key, 33), (1, 1, D), jnp.float32, math.log(0.3), math.log(3.0)))
    values = jax.random.truncated_normal(jax.random.fold_in(key, 31), -3.0, 3.0, shape, jnp.float32) * row_scale * col_scale
    return values.astype(jnp.bfloat16)


def draw_lengths(key, part):
    counts = jax.random.randint(jax.random.fold_in(key, 21), (NUTT,), LEN // 4, LEN + 1, dtype=jnp.int32)
    return counts.at[0].set(LEN)


def spiked(values, own_key, source, target, parts, factor):
    owner, partner = [(jnp.arange(values.shape[axis_at]) // (values.shape[axis_at] // parts)).reshape([-1 if axis == axis_at else 1 for axis in range(values.ndim)]) for axis_at in (source, target)]
    chosen = jax.random.permutation(own_key, parts)[partner]
    strong = (owner == chosen) | (owner == (partner + parts // 2) % parts)
    return jnp.where(strong, factor * values, values)


def block_levels(rng, dims, split, smallest, largest):
    level, own = 1.0, jax.random.fold_in(rng, 6)
    for dim, parts in split:
        heights = jnp.exp(jax.random.uniform(jax.random.fold_in(own, dim), (parts,), jnp.float32, smallest / len(split), largest / len(split)))
        level = level * jnp.repeat(heights, dims[dim] // parts).reshape([-1 if axis == dim else 1 for axis in range(len(dims))])
    return level


def bell_draw(own_key, dims, deviation, reach, shards=(), held_as=jnp.bfloat16):
    values = jax.random.normal(own_key, dims, jnp.float32) * deviation
    if len(shards) > 0:
        values = block_levels(own_key, dims, shards, -0.22, 0.18) * values
    return jnp.clip(values, min=-reach, max=reach).astype(held_as)


def gaussian_with(key, shape, scale, reach, pieces, heavy, kind=jnp.bfloat16):
    values = scale * jax.random.normal(key, shape, jnp.float32)
    if pieces:
        values = values * block_levels(key, shape, pieces, -0.22, 0.18)
    return jnp.clip(spiked(values, jax.random.fold_in(key, 3), *heavy), -reach, reach).astype(kind)


def setup_inputs(seed: int = 0) -> dict:
    streams_of = jax.random.split(jax.random.key(seed), 11)
    return {
        "residual": draw_residual(jax.random.fold_in(streams_of[10], 71), 0),
        "projections": draw_projections(jax.random.fold_in(streams_of[10], 71), 0),
        "out_weight": bell_draw(streams_of[2], (D, D), D ** -0.5, 0.1875),
        "gain_one": jnp.clip(1.0 + 0.18 * jax.random.normal(streams_of[3], (D,), jnp.float32), 0.1, 1.9),
        "up_weight": bell_draw(streams_of[4], (D, 2 * D), D ** -0.5, 0.1875),
        "conv_kernel": bell_draw(streams_of[5], (KERNEL, D), KERNEL ** -0.5, 1.0, (), jnp.float32),
        "gain_two": jnp.clip(1.0 + 0.18 * jax.random.normal(streams_of[6], (D,), jnp.float32), 0.1, 1.9),
        "down_weight": bell_draw(streams_of[7], (D, D), D ** -0.5, 0.1875),
        "lengths": draw_lengths(jax.random.fold_in(streams_of[10], 71), 0),
        "out_grad": gaussian_with(streams_of[9], (LEN, NUTT, D), (1.0 / (LEN * NUTT) ** 0.5), 0.0625, ((0, 64), (1, 4)), (0, 2, 64, 4.0)),
    }


EPSILON = 1e-05

def normalize(values):
    center = values - lax.optimization_barrier(jnp.mean(values, axis=-1, keepdims=True))
    inverse = lax.rsqrt(lax.optimization_barrier(jnp.mean(center * center, axis=-1, keepdims=True)) + EPSILON)
    return (center * inverse, inverse)

def attend_item(item):
    packed, key_marks = item
    query_rows = packed[:, :HD]
    key_rows = packed[:, HD:2 * HD]
    value_rows = packed[:, 2 * HD:]
    scores = jnp.dot(query_rows, key_rows.T, preferred_element_type=jnp.float32) * HD ** (-0.5)
    scores = jnp.where(key_marks[None, :] > 0, scores, -jnp.inf)
    highest = lax.optimization_barrier(jnp.max(scores, axis=-1, keepdims=True))
    raised = jnp.exp(scores - highest)
    weights_bf = (raised / lax.optimization_barrier(jnp.sum(raised, axis=-1, keepdims=True))).astype(jnp.bfloat16)
    return jnp.dot(weights_bf, value_rows, preferred_element_type=jnp.float32).astype(jnp.bfloat16)

def reference(residual, projections, out_weight, gain_one, up_weight, conv_kernel, gain_two, down_weight, lengths, out_grad):
    row_total = LEN * NUTT
    positions = jnp.arange(LEN, dtype=jnp.int32)
    valid = (positions[:, None] < lengths[None, :]).astype(jnp.bfloat16)
    items = projections.reshape(LEN, NUTT * HEADS, 3 * HD).transpose(1, 0, 2)
    item_marks = jnp.broadcast_to(valid.T[:, None, :], (NUTT, HEADS, LEN)).reshape(NUTT * HEADS, LEN)
    attended = lax.map(attend_item, (items, item_marks))
    context = attended.transpose(1, 0, 2).reshape(row_total, D)
    hidden = residual.reshape(row_total, D).astype(jnp.float32) + jnp.dot(context, out_weight, preferred_element_type=jnp.float32)
    normed_one, inverse_one = normalize(hidden)
    scaled_one = (normed_one * gain_one).astype(jnp.bfloat16)
    lifted = jnp.dot(scaled_one, up_weight, preferred_element_type=jnp.float32)
    linear_part = lifted[:, :D]
    gate_part = jax.nn.sigmoid(lifted[:, D:])
    row_mask = valid.reshape(row_total, 1).astype(jnp.float32)
    glu_out = (linear_part * gate_part * row_mask).astype(jnp.bfloat16)
    glu_wide = jnp.pad(glu_out.reshape(LEN, NUTT, D).astype(jnp.float32), ((HALF, HALF), (0, 0), (0, 0)))
    conv_out = jnp.zeros((LEN, NUTT, D), jnp.float32)
    for offset in range(KERNEL):
        conv_out = conv_out + conv_kernel[offset] * glu_wide[offset:offset + LEN]
    normed_two, inverse_two = normalize(conv_out.reshape(row_total, D))
    pre_act = normed_two * gain_two
    gate_two = jax.nn.sigmoid(pre_act)
    activated = (pre_act * gate_two).astype(jnp.bfloat16)
    block_out = (hidden + jnp.dot(activated, down_weight, preferred_element_type=jnp.float32)).astype(jnp.bfloat16)
    block_out = block_out.reshape(LEN, NUTT, D)
    cotangent = (out_grad * valid[:, :, None]).reshape(row_total, D)
    down_grad = jnp.dot(cotangent.T, activated, preferred_element_type=jnp.float32)
    act_grad = jnp.dot(cotangent, down_weight.T, preferred_element_type=jnp.float32)
    pre_grad = act_grad * gate_two * (1.0 + pre_act * (1.0 - gate_two))
    gain_two_grad = lax.optimization_barrier(jnp.sum(pre_grad * normed_two, axis=0))
    scaled_grad = pre_grad * gain_two
    conv_grad = inverse_two * (scaled_grad - lax.optimization_barrier(jnp.mean(scaled_grad, axis=-1, keepdims=True)) - normed_two * lax.optimization_barrier(jnp.mean(scaled_grad * normed_two, axis=-1, keepdims=True)))
    conv_grad = conv_grad.astype(jnp.bfloat16)
    conv_full = conv_grad.reshape(LEN, NUTT, D).astype(jnp.float32)
    conv_wide = jnp.pad(conv_full, ((HALF, HALF), (0, 0), (0, 0)))
    kernel_cols = []
    glu_grad = jnp.zeros((LEN, NUTT, D), jnp.float32)
    for offset in range(KERNEL):
        kernel_cols.append(lax.optimization_barrier(jnp.sum(conv_full * glu_wide[offset:offset + LEN], axis=(0, 1))))
        start = 2 * HALF - offset
        glu_grad = glu_grad + conv_kernel[offset] * conv_wide[start:start + LEN]
    kernel_grad = jnp.stack(kernel_cols, axis=1)
    glu_grad = glu_grad.reshape(row_total, D) * row_mask
    linear_grad = glu_grad * gate_part
    gate_grad = glu_grad * linear_part * gate_part * (1.0 - gate_part)
    lifted_grad = jnp.concatenate([linear_grad, gate_grad], axis=1).astype(jnp.bfloat16)
    up_grad = jnp.dot(lifted_grad.T, scaled_one, preferred_element_type=jnp.float32)
    input_grad = jnp.dot(lifted_grad, up_weight.T, preferred_element_type=jnp.float32)
    gain_one_grad = lax.optimization_barrier(jnp.sum(input_grad * normed_one, axis=0))
    return (block_out, up_grad, down_grad, kernel_grad, gain_one_grad, gain_two_grad)
```

```python
import functools

import jax
import jax.numpy as jnp
from jax import lax
from jax.experimental import pallas as pl
from jax.experimental.pallas import tpu as pltpu
from jax.sharding import PartitionSpec as P

HEADS = 16
EPSILON = 1e-05
LOG2E = 1.4426950408889634
MESH = pl.DeviceIdType.MESH
BF16 = jnp.bfloat16
F32 = jnp.float32

PART_Z = (0, 384)
PART_Y = (384, 640)
PART_X = (1024, 640)
CHUNK = 1664


def lane_ids(shape):
    return lax.broadcasted_iota(jnp.int32, shape, len(shape) - 1)


def attend_kernel(
    proj, lengths, out,
    pbuf, rows32, kv_send, q_send, kv_recv, q_recv, o_send, o_recv, keys, values,
    load_sem, kv_ssem, q_ssem, o_ssem, kv_rsem, q_rsem, o_rsem,
):
    dp = lax.axis_index("dp")
    me = lax.axis_index("ctx")
    group, pair = me // 8, me // 2
    load = pltpu.make_async_copy(proj, pbuf, load_sem)
    load.start()
    barrier = pltpu.get_barrier_semaphore()

    def greet(step, carry):
        pl.semaphore_signal(
            barrier, inc=1, device_id=(dp, lax.rem(me + step, 64)), device_id_type=MESH
        )
        return carry

    lax.fori_loop(1, 64, greet, 0)
    load.wait()

    def widen(step, carry):
        both = jnp.concatenate([pbuf[step * 2 + i].astype(F32) for i in range(2)], axis=0)
        for tile in range(24):
            rows32[tile, pl.ds(pl.multiple_of(step * 8, 8), 8), :] = both[
                :, tile * 128 : tile * 128 + 128
            ]
        return carry

    lax.fori_loop(0, 32, widen, 0)
    pl.semaphore_wait(barrier, 63)

    def push(src, dst, ssem, rsem, target):
        @pl.when(target != me)
        def _():
            pltpu.make_async_remote_copy(
                src_ref=src, dst_ref=dst, send_sem=ssem, recv_sem=rsem,
                device_id=(dp, target), device_id_type=MESH,
            ).start()

        @pl.when(target == me)
        def _():
            pltpu.make_async_copy(src, dst, rsem).start()

    low = lane_ids((64, 128)) < 64
    low32 = lane_ids((32, 128)) < 64

    def pack(step, carry):
        which = lax.rem(pair + step, 32)
        utt, duo = which // 8, lax.rem(which, 8)
        rows = pl.ds(utt, 64, stride=4)
        first, second, third = [rows32[duo * 3 + i, rows, :] for i in range(3)]
        first_t, second_t = pltpu.roll(first, 64, 1), pltpu.roll(second, 64, 1)
        kv_send[which * 2] = jnp.where(low, first_t, second_t).astype(BF16)
        kv_send[which * 2 + 1] = third.astype(BF16)
        q_send[which * 2] = jnp.where(low32, first[:32], first_t[32:]).astype(BF16)
        q_send[which * 2 + 1] = jnp.where(low32, second_t[:32], second[32:]).astype(BF16)
        for side in range(2):
            target = which * 2 + side
            push(kv_send.at[target], kv_recv.at[me], kv_ssem, kv_rsem.at[group], target)
        return carry

    lax.fori_loop(0, 32, pack, 0)

    def ask(step, carry):
        which = lax.rem(pair + step, 32)
        for side in range(2):
            target = which * 2 + side
            push(q_send.at[target], q_recv.at[me], q_ssem, q_rsem.at[group], target)
        return carry

    lax.fori_loop(0, 32, ask, 0)

    length = lengths[me // 16]

    def take_keys(step, carry):
        src = lax.rem(group - step + 8, 8)
        eight = pl.ds(pl.multiple_of(src * 8, 8), 8)
        pltpu.make_async_copy(kv_recv.at[eight], kv_recv.at[eight], kv_rsem.at[src]).wait()
        kv = kv_recv[eight].reshape(512, 128).astype(F32)
        lane = lane_ids((512, 128))
        base = pl.multiple_of(src * 512, 512)
        frame = base + lax.broadcasted_iota(jnp.int32, (512, 128), 0)
        block = pl.ds(base, 512)
        keys[block, :128] = jnp.where(lane < 64, kv, pltpu.roll(kv, 64, 1)).astype(BF16)
        keys[block, 128:] = jnp.where((lane == 0) & (frame >= length), -30000.0, 0.0).astype(BF16)
        values[block, :] = jnp.where(lane < 64, 1.0, kv).astype(BF16)
        return carry

    lax.fori_loop(0, 8, take_keys, 0)

    def attend(step, carry):
        src = lax.rem(group - step + 8, 8)
        eight = pl.ds(pl.multiple_of(src * 8, 8), 8)
        pltpu.make_async_copy(q_recv.at[eight], q_recv.at[eight], q_rsem.at[src]).wait()
        half = lane_ids((256, 128))
        query = q_recv[eight].reshape(256, 128).astype(F32) * (0.125 * LOG2E)
        high = query.astype(BF16).astype(F32)
        rest = query - high
        one = jnp.where(half == 0, 1.0, 0.0)
        early = jnp.where(half < 64, high, pltpu.roll(rest, 64, 1))
        late = jnp.where(half < 64, pltpu.roll(high, 64, 1), rest)
        query = jnp.concatenate(
            [jnp.concatenate([early, one], axis=1), jnp.concatenate([late, one], axis=1)], axis=0
        ).astype(BF16)

        def scores(c):
            return lax.dot_general(
                query, keys[c * 512 : (c + 1) * 512, :], (((1,), (1,)), ((), ())),
                preferred_element_type=F32,
            )

        highest = jnp.full((512, 1), -1e30, F32)
        total = jnp.zeros((512, 128), F32)
        now = scores(0)
        for c in range(8):
            later = scores(c + 1) if c < 7 else None
            top = jnp.maximum(highest, jnp.max(now, axis=1, keepdims=True))
            probs = jnp.exp2(now - top).astype(BF16)
            total = total * jnp.exp2(highest - top) + jnp.dot(
                probs, values[c * 512 : (c + 1) * 512, :], preferred_element_type=F32
            )
            highest, now = top, later
        normed = total / pltpu.roll(total, 64, 1)
        context = jnp.where(half < 64, pltpu.roll(normed[:256], 64, 1), normed[256:])
        o_send[eight] = context.astype(BF16).reshape(8, 32, 128)

        def reply(item, inner):
            target = src * 8 + item
            push(o_send.at[target], o_recv.at[me], o_ssem, o_rsem.at[group], target)
            return inner

        lax.fori_loop(0, 8, reply, 0)
        return carry

    lax.fori_loop(0, 8, attend, 0)

    def gather(step, carry):
        src = lax.rem(group + step, 8)
        eight = pl.ds(pl.multiple_of(src * 8, 8), 8)
        pltpu.make_async_copy(o_recv.at[eight], o_recv.at[eight], o_rsem.at[src]).wait()
        for i in range(4):
            which = src * 4 + i
            utt, duo = which // 8, lax.rem(which, 8)
            left = o_recv[which * 2].astype(F32)
            right = o_recv[which * 2 + 1].astype(F32)
            upper = jnp.where(low32, left, pltpu.roll(right, 64, 1))
            lower = jnp.where(low32, pltpu.roll(left, 64, 1), right)
            rows32[duo, pl.ds(utt, 64, stride=4), :] = jnp.concatenate([upper, lower], axis=0)
        return carry

    lax.fori_loop(0, 8, gather, 0)
    for tile in range(8):
        out[:, tile * 128 : tile * 128 + 128] = rows32[tile].astype(BF16)
    for buf, sem in ((kv_send, kv_ssem), (q_send, q_ssem), (o_send, o_ssem)):
        sent = buf.at[pl.ds(0, 63)]
        pltpu.make_async_copy(sent, sent, sem).wait()


def attend(projections, lengths):
    dma = pltpu.SemaphoreType.DMA
    return pl.pallas_call(
        attend_kernel,
        out_shape=jax.ShapeDtypeStruct((256, 1024), BF16),
        in_specs=[
            pl.BlockSpec(memory_space=pl.ANY),
            pl.BlockSpec(memory_space=pltpu.SMEM),
        ],
        out_specs=pl.BlockSpec(memory_space=pltpu.VMEM),
        scratch_shapes=[
            pltpu.VMEM((64, 4, 3072), BF16),
            pltpu.VMEM((24, 256, 128), F32),
            pltpu.VMEM((64, 64, 128), BF16),
            pltpu.VMEM((64, 32, 128), BF16),
            pltpu.VMEM((64, 64, 128), BF16),
            pltpu.VMEM((64, 32, 128), BF16),
            pltpu.VMEM((64, 32, 128), BF16),
            pltpu.VMEM((64, 32, 128), BF16),
            pltpu.VMEM((4096, 256), BF16),
            pltpu.VMEM((4096, 128), BF16),
            dma, dma, dma, dma,
            dma((8,)), dma((8,)), dma((8,)),
        ],
        compiler_params=pltpu.CompilerParams(
            collective_id=1, has_side_effects=True, vmem_limit_bytes=48 << 20
        ),
        name="exchange_attend",
    )(projections, lengths)


def sum_kernel(
    grads, out,
    mine, other, y_recv, y_sum, yx_recv, yx_sum, yxz_recv,
    x_recv, x_sum, xy_recv, xy_sum, xyz_recv,
    z_recv, z_sum, zx_recv, zx_sum, zxy_recv,
    lsem, ssem, rsem,
):
    dp, ctx = lax.axis_index("dp"), lax.axis_index("ctx")
    x_hi, core = dp // 2, lax.rem(dp, 2)
    x_lo, y, z = ctx // 32, lax.rem(ctx // 8, 4), lax.rem(ctx, 8)
    x = x_hi * 2 + x_lo
    sibling = (x_hi * 2 + 1 - core, ctx)

    def along_x(k):
        to = lax.rem(x + k, 4)
        return (to // 2) * 2 + core, lax.rem(to, 2) * 32 + y * 8 + z

    def along_y(k):
        return dp, x_lo * 32 + lax.rem(y + k, 4) * 8 + z

    def along_z(k):
        return dp, x_lo * 32 + y * 8 + lax.rem(z + k, 8)

    locals_ = []
    for i, (start, width) in enumerate((PART_Y, PART_X, PART_Z)):
        part = pl.ds(start, width)
        copy = pltpu.make_async_copy(
            grads.at[:, core, :, :, :, :, part], mine.at[:, :, :, :, :, part], lsem.at[i]
        )
        copy.start()
        locals_.append(copy)

    barrier = pltpu.get_barrier_semaphore()
    peers = [sibling] + [along_x(k) for k in (1, 2, 3)] + [along_y(k) for k in (1, 2, 3)]
    peers += [along_z(k) for k in range(1, 8)]
    for peer in peers:
        pl.semaphore_signal(barrier, inc=1, device_id=peer, device_id_type=MESH)
    pl.semaphore_wait(barrier, len(peers))

    started = []

    def send(src, dst, peer):
        index = len(started)
        copy = pltpu.make_async_remote_copy(
            src_ref=src, dst_ref=dst, send_sem=ssem.at[index], recv_sem=rsem.at[index],
            device_id=peer, device_id_type=MESH,
        )
        copy.start()
        started.append(copy)
        return copy

    halves = []
    for start, width in (PART_Y, PART_X, PART_Z):
        part = pl.ds(start, width)
        halves.append(
            send(
                grads.at[:, 1 - core, :, :, :, :, part],
                other.at[:, :, :, :, :, part],
                sibling,
            )
        )

    def join(i, part):
        start, width = part
        locals_[i].wait()
        halves[i].wait_recv()
        cols = pl.ds(start, width)

        def body(step, carry):
            a, b, c = step // 8, lax.rem(step // 4, 2), lax.rem(step, 4)
            mine[a, b, c, :, :, cols] = (
                mine[a, b, c, :, :, cols].astype(F32) + other[a, b, c, :, :, cols].astype(F32)
            ).astype(BF16)
            return carry

        lax.fori_loop(0, 16, body, 0)

    def cols_of(part):
        return pl.ds(part[0], part[1])

    def split(k):
        to = lax.rem(x + k, 4)
        return to // 2, lax.rem(to, 2)

    join(0, PART_Y)
    y_one = [
        send(
            mine.at[:, :, lax.rem(y + k, 4), :, :, cols_of(PART_Y)], y_recv.at[k - 1], along_y(k)
        )
        for k in (1, 2, 3)
    ]
    join(1, PART_X)
    x_one = []
    for k in (1, 2, 3):
        hi, lo = split(k)
        x_one.append(send(mine.at[hi, lo, :, :, :, cols_of(PART_X)], x_recv.at[k - 1], along_x(k)))
    join(2, PART_Z)
    z_one = [
        send(
            mine.at[:, :, :, lax.rem(z + k, 8), :, cols_of(PART_Z)], z_recv.at[k - 1], along_z(k)
        )
        for k in range(1, 8)
    ]

    def wait_all(copies):
        for copy in copies:
            copy.wait_recv()

    wait_all(y_one)

    def y_body(step, carry):
        a, b = step // 2, lax.rem(step, 2)
        acc = mine[a, b, y, :, :, cols_of(PART_Y)].astype(F32)
        for k in range(3):
            acc = acc + y_recv[k, a, b].astype(F32)
        y_sum[a, b] = acc.astype(BF16)
        return carry

    lax.fori_loop(0, 4, y_body, 0)
    yx = []
    for k in (1, 2, 3):
        hi, lo = split(k)
        yx.append(send(y_sum.at[hi, lo], yx_recv.at[k - 1], along_x(k)))

    wait_all(x_one)

    def x_body(step, carry):
        acc = mine[x_hi, x_lo, step, :, :, cols_of(PART_X)].astype(F32)
        for k in range(3):
            acc = acc + x_recv[k, step].astype(F32)
        x_sum[step] = acc.astype(BF16)
        return carry

    lax.fori_loop(0, 4, x_body, 0)
    xy = [
        send(x_sum.at[lax.rem(y + k, 4)], xy_recv.at[k - 1], along_y(k)) for k in (1, 2, 3)
    ]

    wait_all(z_one)

    def z_body(step, carry):
        a, b = step // 2, lax.rem(step, 2)
        acc = mine[a, b, :, z, :, cols_of(PART_Z)].astype(F32)
        for k in range(7):
            acc = acc + z_recv[k, a, b].astype(F32)
        z_sum[a, b] = acc.astype(BF16)
        return carry

    lax.fori_loop(0, 4, z_body, 0)
    zx = []
    for k in (1, 2, 3):
        hi, lo = split(k)
        zx.append(send(z_sum.at[hi, lo], zx_recv.at[k - 1], along_x(k)))

    wait_all(yx)
    acc = y_sum[x_hi, x_lo].astype(F32)
    for k in range(3):
        acc = acc + yx_recv[k].astype(F32)
    yx_sum[...] = acc.astype(BF16)
    yxz = [
        send(yx_sum.at[lax.rem(z + k, 8)], yxz_recv.at[k - 1], along_z(k)) for k in range(1, 8)
    ]

    wait_all(xy)
    acc = x_sum[y].astype(F32)
    for k in range(3):
        acc = acc + xy_recv[k].astype(F32)
    xy_sum[...] = acc.astype(BF16)
    xyz = [
        send(xy_sum.at[lax.rem(z + k, 8)], xyz_recv.at[k - 1], along_z(k)) for k in range(1, 8)
    ]

    wait_all(zx)
    acc = z_sum[x_hi, x_lo].astype(F32)
    for k in range(3):
        acc = acc + zx_recv[k].astype(F32)
    zx_sum[...] = acc.astype(BF16)
    zxy = [
        send(zx_sum.at[lax.rem(y + k, 4)], zxy_recv.at[k - 1], along_y(k)) for k in (1, 2, 3)
    ]

    for copies, own, received, count, part in (
        (yxz, yx_sum.at[z], yxz_recv, 7, PART_Y),
        (xyz, xy_sum.at[z], xyz_recv, 7, PART_X),
        (zxy, zx_sum.at[y], zxy_recv, 3, PART_Z),
    ):
        wait_all(copies)
        acc = own[...].astype(F32)
        for k in range(count):
            acc = acc + received[k].astype(F32)
        out[:, cols_of(part)] = acc
    for copy in started:
        copy.wait_send()


def sum_everywhere(grads):
    dma = pltpu.SemaphoreType.DMA
    wide, narrow = PART_Y[1], PART_Z[1]

    def vmem(*shape):
        return pltpu.VMEM(shape, BF16)

    return pl.pallas_call(
        sum_kernel,
        out_shape=jax.ShapeDtypeStruct((8, CHUNK), F32),
        in_specs=[pl.BlockSpec(memory_space=pl.ANY)],
        out_specs=pl.BlockSpec(memory_space=pltpu.VMEM),
        scratch_shapes=[
            vmem(2, 2, 4, 8, 8, CHUNK), vmem(2, 2, 4, 8, 8, CHUNK),
            vmem(3, 2, 2, 8, 8, wide), vmem(2, 2, 8, 8, wide),
            vmem(3, 8, 8, wide), vmem(8, 8, wide), vmem(7, 8, wide),
            vmem(3, 4, 8, 8, wide), vmem(4, 8, 8, wide),
            vmem(3, 8, 8, wide), vmem(8, 8, wide), vmem(7, 8, wide),
            vmem(7, 2, 2, 4, 8, narrow), vmem(2, 2, 4, 8, narrow),
            vmem(3, 4, 8, narrow), vmem(4, 8, narrow), vmem(3, 8, narrow),
            dma((3,)), dma((48,)), dma((48,)),
        ],
        compiler_params=pltpu.CompilerParams(
            collective_id=2, has_side_effects=True, vmem_limit_bytes=48 << 20
        ),
        name="sum_everywhere",
    )(grads.reshape(2, 2, 2, 4, 8, 8, CHUNK))


def extended(x, sides, width):
    for axis, dim in sides:
        size, length = (lax.axis_size(axis), x.shape[dim])
        up = [(i, (i + 1) % size) for i in range(size - 1)]
        down = [(j, i) for i, j in up]
        last = lax.slice_in_dim(x, length - width, length, axis=dim)
        leading = lax.slice_in_dim(x, 0, width, axis=dim)
        before = lax.ppermute(last, axis, up)
        after = lax.ppermute(leading, axis, down)
        x = jnp.concatenate([before, x, after], axis=dim)
    return x


def normalize(values):
    center = values - jnp.mean(values, axis=-1, keepdims=True)
    inverse = lax.rsqrt(jnp.mean(center * center, axis=-1, keepdims=True) + EPSILON)
    return (center * inverse, inverse)


def on_device(
    residual,
    projections,
    out_weight,
    gain_one,
    up_weight,
    conv_kernel,
    gain_two,
    down_weight,
    lengths,
    out_grad,
):
    frames, utter_count, model_width = residual.shape
    kernel_len = conv_kernel.shape[0]
    half_width = (kernel_len - 1) // 2
    row_count = frames * utter_count
    first_frame = lax.axis_index("ctx") * frames
    positions = first_frame + jnp.arange(frames, dtype=jnp.int32)
    valid = (positions[:, None] < lengths[None, :]).astype(jnp.bfloat16)
    context = attend(projections, lengths)
    hidden = residual.reshape(row_count, model_width).astype(jnp.float32) + jnp.dot(
        context, out_weight, preferred_element_type=jnp.float32
    )
    normed_one, inverse_one = normalize(hidden)
    scaled_one = (normed_one * gain_one).astype(jnp.bfloat16)
    lifted = jnp.dot(scaled_one, up_weight, preferred_element_type=jnp.float32)
    linear_part = lifted[:, :model_width]
    gate_part = jax.nn.sigmoid(lifted[:, model_width:])
    row_mask = valid.reshape(row_count, 1).astype(jnp.float32)
    glu_out = (linear_part * gate_part * row_mask).astype(jnp.bfloat16)
    glu_rimmed = extended(
        glu_out.reshape(frames, utter_count, model_width), (("ctx", 0),), half_width
    )
    glu_wide = glu_rimmed.astype(jnp.float32)
    conv_out = jnp.zeros((frames, utter_count, model_width), jnp.float32)
    for offset in range(kernel_len):
        conv_out = conv_out + conv_kernel[offset] * glu_wide[offset : offset + frames]
    normed_two, inverse_two = normalize(conv_out.reshape(row_count, model_width))
    pre_act = normed_two * gain_two
    gate_two = jax.nn.sigmoid(pre_act)
    activated = (pre_act * gate_two).astype(jnp.bfloat16)
    block_out = (
        hidden + jnp.dot(activated, down_weight, preferred_element_type=jnp.float32)
    ).astype(jnp.bfloat16)
    block_out = block_out.reshape(frames, utter_count, model_width)
    cotangent = (out_grad * valid[:, :, None]).reshape(row_count, model_width)
    down_grad = jnp.einsum("ro,ri->oi", cotangent, activated, preferred_element_type=jnp.float32)
    act_grad = lax.dot_general(
        cotangent, down_weight, (((1,), (1,)), ((), ())), preferred_element_type=jnp.float32
    )
    pre_grad = act_grad * gate_two * (1.0 + pre_act * (1.0 - gate_two))
    gain_two_grad = jnp.sum(pre_grad * normed_two, axis=0)
    scaled_grad = pre_grad * gain_two
    conv_grad = inverse_two * (
        scaled_grad
        - jnp.mean(scaled_grad, axis=-1, keepdims=True)
        - normed_two * jnp.mean(scaled_grad * normed_two, axis=-1, keepdims=True)
    )
    conv_grad = conv_grad.astype(jnp.bfloat16).reshape(frames, utter_count, model_width)
    conv_rimmed = extended(conv_grad, (("ctx", 0),), half_width)
    conv_wide = conv_rimmed.astype(jnp.float32)
    conv_local = conv_wide[half_width : half_width + frames]
    kernel_cols = []
    glu_grad = jnp.zeros((frames, utter_count, model_width), jnp.float32)
    for offset in range(kernel_len):
        kernel_cols.append(jnp.sum(conv_local * glu_wide[offset : offset + frames], axis=(0, 1)))
        start_row = 2 * half_width - offset
        glu_grad = glu_grad + conv_kernel[offset] * conv_wide[start_row : start_row + frames]
    glu_grad = glu_grad.reshape(row_count, model_width) * row_mask
    linear_grad = glu_grad * gate_part
    gate_grad = glu_grad * linear_part * gate_part * (1.0 - gate_part)
    lifted_grad = jnp.concatenate([linear_grad, gate_grad], axis=1).astype(jnp.bfloat16)
    up_grad = jnp.einsum("rj,ri->ji", lifted_grad, scaled_one, preferred_element_type=jnp.float32)
    input_grad = lax.dot_general(
        lifted_grad, up_weight, (((1,), (1,)), ((), ())), preferred_element_type=jnp.float32
    )
    gain_one_grad = jnp.sum(input_grad * normed_one, axis=0)
    small = jnp.stack(kernel_cols + [gain_one_grad, gain_two_grad], axis=1).reshape(256, 4, 33)
    chunks = jnp.concatenate(
        [
            up_grad.astype(BF16).reshape(256, 8, 1024),
            down_grad.astype(BF16).reshape(256, 4, 2, 512).transpose(0, 2, 1, 3).reshape(256, 8, 512),
            jnp.pad(small.astype(BF16), ((0, 0), (0, 4), (0, 95))),
        ],
        axis=2,
    )
    total = sum_everywhere(chunks)
    return (
        block_out,
        total[:, :1024],
        total[:, 1024:1536].reshape(2, 4, 512).transpose(1, 0, 2).reshape(4, 1024),
        total[:4, 1536:1567],
        total[:4, 1567],
        total[:4, 1568],
    )


def solution(mesh):
    in_specs = (
        P("ctx", "dp", None),
        P("ctx", "dp", None),
        P(),
        P(),
        P(),
        P(),
        P(),
        P(),
        P("dp"),
        P("ctx", "dp", None),
    )
    out_specs = (
        P("ctx", "dp", None),
        P(("dp", "ctx"), None),
        P(("dp", "ctx"), None),
        P(("dp", "ctx"), None),
        P(("dp", "ctx")),
        P(("dp", "ctx")),
    )
    return jax.shard_map(
        on_device, mesh=mesh, in_specs=in_specs, out_specs=out_specs, check_vma=False
    )
```

```python
import functools

import jax
import jax.numpy as jnp
from jax import lax
from jax.experimental import pallas as pl
from jax.experimental.pallas import tpu as pltpu
from jax.sharding import PartitionSpec as P

HEADS = 16
EPSILON = 1e-05
LOG2E = 1.4426950408889634
MESH = pl.DeviceIdType.MESH
BF16 = jnp.bfloat16
F32 = jnp.float32

PART_Z = (0, 384)
PART_Y = (384, 640)
PART_X = (1024, 640)
CHUNK = 1664


def lane_ids(shape):
    return lax.broadcasted_iota(jnp.int32, shape, len(shape) - 1)


def attend_kernel(
    proj, lengths, out,
    pbuf, rows32, kv_send, q_send, kv_recv, q_recv, o_send, o_recv, keys, values,
    load_sem, kv_ssem, q_ssem, o_ssem, kv_rsem, q_rsem, o_rsem,
):
    dp = lax.axis_index("dp")
    me = lax.axis_index("ctx")
    group, pair = me // 8, me // 2
    load = pltpu.make_async_copy(proj, pbuf, load_sem)
    load.start()
    barrier = pltpu.get_barrier_semaphore()

    def greet(step, carry):
        pl.semaphore_signal(
            barrier, inc=1, device_id=(dp, lax.rem(me + step, 64)), device_id_type=MESH
        )
        return carry

    lax.fori_loop(1, 64, greet, 0)
    load.wait()

    def widen(step, carry):
        both = jnp.concatenate([pbuf[step * 2 + i].astype(F32) for i in range(2)], axis=0)
        for tile in range(24):
            rows32[tile, pl.ds(pl.multiple_of(step * 8, 8), 8), :] = both[
                :, tile * 128 : tile * 128 + 128
            ]
        return carry

    lax.fori_loop(0, 32, widen, 0)
    pl.semaphore_wait(barrier, 63)

    def push(src, dst, ssem, rsem, target):
        @pl.when(target != me)
        def _():
            pltpu.make_async_remote_copy(
                src_ref=src, dst_ref=dst, send_sem=ssem, recv_sem=rsem,
                device_id=(dp, target), device_id_type=MESH,
            ).start()

        @pl.when(target == me)
        def _():
            pltpu.make_async_copy(src, dst, rsem).start()

    low = lane_ids((64, 128)) < 64
    low32 = lane_ids((32, 128)) < 64

    def pack(step, carry):
        which = lax.rem(pair + step, 32)
        utt, duo = which // 8, lax.rem(which, 8)
        rows = pl.ds(utt, 64, stride=4)
        first, second, third = [rows32[duo * 3 + i, rows, :] for i in range(3)]
        first_t, second_t = pltpu.roll(first, 64, 1), pltpu.roll(second, 64, 1)
        kv_send[which * 2] = jnp.where(low, first_t, second_t).astype(BF16)
        kv_send[which * 2 + 1] = third.astype(BF16)
        q_send[which * 2] = jnp.where(low32, first[:32], first_t[32:]).astype(BF16)
        q_send[which * 2 + 1] = jnp.where(low32, second_t[:32], second[32:]).astype(BF16)
        for side in range(2):
            target = which * 2 + side
            push(kv_send.at[target], kv_recv.at[me], kv_ssem, kv_rsem.at[group], target)
        return carry

    lax.fori_loop(0, 32, pack, 0)

    def ask(step, carry):
        which = lax.rem(pair + step, 32)
        for side in range(2):
            target = which * 2 + side
            push(q_send.at[target], q_recv.at[me], q_ssem, q_rsem.at[group], target)
        return carry

    lax.fori_loop(0, 32, ask, 0)

    length = lengths[me // 16]

    def take_keys(step, carry):
        src = lax.rem(group - step + 8, 8)
        eight = pl.ds(pl.multiple_of(src * 8, 8), 8)
        pltpu.make_async_copy(kv_recv.at[eight], kv_recv.at[eight], kv_rsem.at[src]).wait()
        kv = kv_recv[eight].reshape(512, 128).astype(F32)
        lane = lane_ids((512, 128))
        base = pl.multiple_of(src * 512, 512)
        frame = base + lax.broadcasted_iota(jnp.int32, (512, 128), 0)
        block = pl.ds(base, 512)
        keys[block, :128] = jnp.where(lane < 64, kv, pltpu.roll(kv, 64, 1)).astype(BF16)
        keys[block, 128:] = jnp.where((lane == 0) & (frame >= length), -30000.0, 0.0).astype(BF16)
        values[block, :] = jnp.where(lane < 64, 1.0, kv).astype(BF16)
        return carry

    lax.fori_loop(0, 8, take_keys, 0)

    def attend(step, carry):
        src = lax.rem(group - step + 8, 8)
        eight = pl.ds(pl.multiple_of(src * 8, 8), 8)
        pltpu.make_async_copy(q_recv.at[eight], q_recv.at[eight], q_rsem.at[src]).wait()
        half = lane_ids((256, 128))
        query = q_recv[eight].reshape(256, 128).astype(F32) * (0.125 * LOG2E)
        high = query.astype(BF16).astype(F32)
        rest = query - high
        one = jnp.where(half == 0, 1.0, 0.0)
        early = jnp.where(half < 64, high, pltpu.roll(rest, 64, 1))
        late = jnp.where(half < 64, pltpu.roll(high, 64, 1), rest)
        query = jnp.concatenate(
            [jnp.concatenate([early, one], axis=1), jnp.concatenate([late, one], axis=1)], axis=0
        ).astype(BF16)

        def scores(c):
            return lax.dot_general(
                query, keys[c * 512 : (c + 1) * 512, :], (((1,), (1,)), ((), ())),
                preferred_element_type=F32,
            )

        highest = jnp.full((512, 1), -1e30, F32)
        total = jnp.zeros((512, 128), F32)
        now = scores(0)
        for c in range(8):
            later = scores(c + 1) if c < 7 else None
            top = jnp.maximum(highest, jnp.max(now, axis=1, keepdims=True))
            probs = jnp.exp2(now - top).astype(BF16)
            total = total * jnp.exp2(highest - top) + jnp.dot(
                probs, values[c * 512 : (c + 1) * 512, :], preferred_element_type=F32
            )
            highest, now = top, later
        normed = total / pltpu.roll(total, 64, 1)
        context = jnp.where(half < 64, pltpu.roll(normed[:256], 64, 1), normed[256:])
        o_send[eight] = context.astype(BF16).reshape(8, 32, 128)

        def reply(item, inner):
            target = src * 8 + item
            push(o_send.at[target], o_recv.at[me], o_ssem, o_rsem.at[group], target)
            return inner

        lax.fori_loop(0, 8, reply, 0)
        return carry

    lax.fori_loop(0, 8, attend, 0)

    def gather(step, carry):
        src = lax.rem(group + step, 8)
        eight = pl.ds(pl.multiple_of(src * 8, 8), 8)
        pltpu.make_async_copy(o_recv.at[eight], o_recv.at[eight], o_rsem.at[src]).wait()
        for i in range(4):
            which = src * 4 + i
            utt, duo = which // 8, lax.rem(which, 8)
            left = o_recv[which * 2].astype(F32)
            right = o_recv[which * 2 + 1].astype(F32)
            upper = jnp.where(low32, left, pltpu.roll(right, 64, 1))
            lower = jnp.where(low32, pltpu.roll(left, 64, 1), right)
            rows32[duo, pl.ds(utt, 64, stride=4), :] = jnp.concatenate([upper, lower], axis=0)
        return carry

    lax.fori_loop(0, 8, gather, 0)
    for tile in range(8):
        out[:, tile * 128 : tile * 128 + 128] = rows32[tile].astype(BF16)
    for buf, sem in ((kv_send, kv_ssem), (q_send, q_ssem), (o_send, o_ssem)):
        sent = buf.at[pl.ds(0, 63)]
        pltpu.make_async_copy(sent, sent, sem).wait()


def attend(projections, lengths):
    dma = pltpu.SemaphoreType.DMA
    return pl.pallas_call(
        attend_kernel,
        out_shape=jax.ShapeDtypeStruct((256, 1024), BF16),
        in_specs=[
            pl.BlockSpec(memory_space=pl.ANY),
            pl.BlockSpec(memory_space=pltpu.SMEM),
        ],
        out_specs=pl.BlockSpec(memory_space=pltpu.VMEM),
        scratch_shapes=[
            pltpu.VMEM((64, 4, 3072), BF16),
            pltpu.VMEM((24, 256, 128), F32),
            pltpu.VMEM((64, 64, 128), BF16),
            pltpu.VMEM((64, 32, 128), BF16),
            pltpu.VMEM((64, 64, 128), BF16),
            pltpu.VMEM((64, 32, 128), BF16),
            pltpu.VMEM((64, 32, 128), BF16),
            pltpu.VMEM((64, 32, 128), BF16),
            pltpu.VMEM((4096, 256), BF16),
            pltpu.VMEM((4096, 128), BF16),
            dma, dma, dma, dma,
            dma((8,)), dma((8,)), dma((8,)),
        ],
        compiler_params=pltpu.CompilerParams(
            collective_id=1, has_side_effects=True, vmem_limit_bytes=48 << 20
        ),
        name="exchange_attend",
    )(projections, lengths)


def sum_phase(
    where, send, grads, out,
    other, y_recv, y_sum, yx_recv, yx_sum, yxz_recv,
    x_recv, x_sum, xy_recv, xy_sum, xyz_recv,
    z_recv, z_sum, zx_recv, zx_sum, zxy_recv,
):
    x_hi, x_lo, core, y, z = where.x_hi, where.x_lo, where.core, where.y, where.z
    x = x_hi * 2 + x_lo
    along_x, along_y, along_z = where.along_x, where.along_y, where.along_z
    mine = grads.at[:, core]

    halves = []
    for start, width in (PART_Y, PART_X, PART_Z):
        part = pl.ds(start, width)
        halves.append(
            send(
                grads.at[:, 1 - core, :, :, :, :, part],
                other.at[:, :, :, :, :, part],
                where.sibling,
            )
        )

    def join(i, part):
        start, width = part
        halves[i].wait_recv()
        cols = pl.ds(start, width)

        def body(step, carry):
            a, b, c = step // 8, lax.rem(step // 4, 2), lax.rem(step, 4)
            mine[a, b, c, :, :, cols] = (
                mine[a, b, c, :, :, cols].astype(F32) + other[a, b, c, :, :, cols].astype(F32)
            ).astype(BF16)
            return carry

        lax.fori_loop(0, 16, body, 0)

    def cols_of(part):
        return pl.ds(part[0], part[1])

    def split(k):
        to = lax.rem(x + k, 4)
        return to // 2, lax.rem(to, 2)

    join(0, PART_Y)
    y_one = [
        send(
            mine.at[:, :, lax.rem(y + k, 4), :, :, cols_of(PART_Y)], y_recv.at[k - 1], along_y(k)
        )
        for k in (1, 2, 3)
    ]
    join(1, PART_X)
    x_one = []
    for k in (1, 2, 3):
        hi, lo = split(k)
        x_one.append(send(mine.at[hi, lo, :, :, :, cols_of(PART_X)], x_recv.at[k - 1], along_x(k)))
    join(2, PART_Z)
    z_one = [
        send(
            mine.at[:, :, :, lax.rem(z + k, 8), :, cols_of(PART_Z)], z_recv.at[k - 1], along_z(k)
        )
        for k in range(1, 8)
    ]

    def wait_all(copies):
        for copy in copies:
            copy.wait_recv()

    wait_all(y_one)

    def y_body(step, carry):
        a, b = step // 2, lax.rem(step, 2)
        acc = mine[a, b, y, :, :, cols_of(PART_Y)].astype(F32)
        for k in range(3):
            acc = acc + y_recv[k, a, b].astype(F32)
        y_sum[a, b] = acc.astype(BF16)
        return carry

    lax.fori_loop(0, 4, y_body, 0)
    yx = []
    for k in (1, 2, 3):
        hi, lo = split(k)
        yx.append(send(y_sum.at[hi, lo], yx_recv.at[k - 1], along_x(k)))

    wait_all(x_one)

    def x_body(step, carry):
        acc = mine[x_hi, x_lo, step, :, :, cols_of(PART_X)].astype(F32)
        for k in range(3):
            acc = acc + x_recv[k, step].astype(F32)
        x_sum[step] = acc.astype(BF16)
        return carry

    lax.fori_loop(0, 4, x_body, 0)
    xy = [
        send(x_sum.at[lax.rem(y + k, 4)], xy_recv.at[k - 1], along_y(k)) for k in (1, 2, 3)
    ]

    wait_all(z_one)

    def z_body(step, carry):
        a, b = step // 2, lax.rem(step, 2)
        acc = mine[a, b, :, z, :, cols_of(PART_Z)].astype(F32)
        for k in range(7):
            acc = acc + z_recv[k, a, b].astype(F32)
        z_sum[a, b] = acc.astype(BF16)
        return carry

    lax.fori_loop(0, 4, z_body, 0)
    zx = []
    for k in (1, 2, 3):
        hi, lo = split(k)
        zx.append(send(z_sum.at[hi, lo], zx_recv.at[k - 1], along_x(k)))

    wait_all(yx)
    acc = y_sum[x_hi, x_lo].astype(F32)
    for k in range(3):
        acc = acc + yx_recv[k].astype(F32)
    yx_sum[...] = acc.astype(BF16)
    yxz = [
        send(yx_sum.at[lax.rem(z + k, 8)], yxz_recv.at[k - 1], along_z(k)) for k in range(1, 8)
    ]

    wait_all(xy)
    acc = x_sum[y].astype(F32)
    for k in range(3):
        acc = acc + xy_recv[k].astype(F32)
    xy_sum[...] = acc.astype(BF16)
    xyz = [
        send(xy_sum.at[lax.rem(z + k, 8)], xyz_recv.at[k - 1], along_z(k)) for k in range(1, 8)
    ]

    wait_all(zx)
    acc = z_sum[x_hi, x_lo].astype(F32)
    for k in range(3):
        acc = acc + zx_recv[k].astype(F32)
    zx_sum[...] = acc.astype(BF16)
    zxy = [
        send(zx_sum.at[lax.rem(y + k, 4)], zxy_recv.at[k - 1], along_y(k)) for k in (1, 2, 3)
    ]

    for copies, own, received, count, part in (
        (yxz, yx_sum.at[z], yxz_recv, 7, PART_Y),
        (xyz, xy_sum.at[z], xyz_recv, 7, PART_X),
        (zxy, zx_sum.at[y], zxy_recv, 3, PART_Z),
    ):
        wait_all(copies)
        acc = own[...].astype(F32)
        for k in range(count):
            acc = acc + received[k].astype(F32)
        out[:, cols_of(part)] = acc


class Place:
    def __init__(self):
        dp, ctx = lax.axis_index("dp"), lax.axis_index("ctx")
        self.dp, self.ctx = dp, ctx
        self.x_hi, self.core = dp // 2, lax.rem(dp, 2)
        self.x_lo, self.y, self.z = ctx // 32, lax.rem(ctx // 8, 4), lax.rem(ctx, 8)
        self.sibling = (self.x_hi * 2 + 1 - self.core, ctx)

    def along_x(self, k):
        to = lax.rem(self.x_hi * 2 + self.x_lo + k, 4)
        return (to // 2) * 2 + self.core, lax.rem(to, 2) * 32 + self.y * 8 + self.z

    def along_y(self, k):
        return self.dp, self.x_lo * 32 + lax.rem(self.y + k, 4) * 8 + self.z

    def along_z(self, k):
        return self.dp, self.x_lo * 32 + self.y * 8 + lax.rem(self.z + k, 8)


def rowwise(body):
    def step(i, carry):
        body(pl.ds(pl.multiple_of(i * 16, 16), 16))
        return carry

    lax.fori_loop(0, 16, step, 0)


def colwise(body, count=4):
    def step(i, carry):
        body(i, pl.ds(pl.multiple_of(i * 256, 256), 256))
        return carry

    lax.fori_loop(0, count, step, 0)


def dot(a, b):
    return jnp.dot(a, b, preferred_element_type=F32)


def dot_t(a, b):
    return lax.dot_general(a, b, (((1,), (1,)), ((), ())), preferred_element_type=F32)


def t_dot(a, b):
    return lax.dot_general(a, b, (((0,), (0,)), ((), ())), preferred_element_type=F32)


def moments(values):
    center = values - jnp.mean(values, axis=-1, keepdims=True)
    inverse = lax.rsqrt(jnp.mean(center * center, axis=-1, keepdims=True) + EPSILON)
    return center * inverse, inverse


def sigmoid(x):
    return 1.0 / (1.0 + jnp.exp(-x))


def four_later(src, dst):
    def step(i, carry):
        base = pl.multiple_of(i * 8, 8)
        dst[pl.ds(base, 8), :] = jnp.concatenate(
            [src[pl.ds(base, 8), :][4:], src[pl.ds(base + 8, 8), :][:4]], axis=0
        )
        return carry

    lax.fori_loop(0, 47, step, 0)


def block_kernel(
    context, residual, out_grad, lengths, gain_one, gain_two, taps,
    out_w_hbm, up_w_hbm, down_w_hbm,
    block_out, total_out,
    out_w, up_w, down_w, mask, hidden, normed_one, scaled_one, linear, gate, glu,
    glu_even, glu_odd, grad_even, grad_odd, conv, normed_two, inverse_two, activated,
    cotangent, act_grad, conv_grad, lifted_grad, before, after, tap_sums, sums, turned, grads,
    *rest,
):
    sum_scratch, (wsem, ssem, rsem) = rest[:-3], rest[-3:]
    where = Place()
    ctx = where.ctx
    weights = []
    for i, (src, dst) in enumerate(((out_w_hbm, out_w), (up_w_hbm, up_w), (down_w_hbm, down_w))):
        copy = pltpu.make_async_copy(src, dst, wsem.at[i])
        copy.start()
        weights.append(copy)

    barrier = pltpu.get_barrier_semaphore()
    axis_peers = [where.along_x(k) for k in (1, 2, 3)] + [where.along_y(k) for k in (1, 2, 3)]
    axis_peers += [where.along_z(k) for k in range(1, 8)]
    left, right = (where.dp, lax.rem(ctx + 63, 64)), (where.dp, lax.rem(ctx + 1, 64))
    peers = [where.sibling, left, right] + axis_peers
    for peer in peers:
        pl.semaphore_signal(barrier, inc=1, device_id=peer, device_id_type=MESH)

    started = []

    def send(src, dst, peer):
        index = len(started)
        copy = pltpu.make_async_remote_copy(
            src_ref=src, dst_ref=dst, send_sem=ssem.at[index], recv_sem=rsem.at[index],
            device_id=peer, device_id_type=MESH,
        )
        copy.start()
        started.append(copy)
        return copy

    row = lax.broadcasted_iota(jnp.int32, (256, 128), 0)
    utt = lax.rem(row, 4)
    limit = jnp.where(
        utt < 2,
        jnp.where(utt == 0, lengths[0], lengths[1]),
        jnp.where(utt == 2, lengths[2], lengths[3]),
    )
    mask[...] = jnp.where(ctx * 64 + row // 4 < limit, 1.0, 0.0)

    weights[0].wait()

    def project(i, cols):
        hidden[:, cols] = residual[:, cols].astype(F32) + dot(context[...], out_w[:, cols])

    colwise(project)

    def first_norm(rows):
        normed, _ = moments(hidden[rows, :])
        normed_one[rows, :] = normed
        scaled_one[rows, :] = (normed * gain_one[...]).astype(BF16)
        keep = jnp.tile(mask[rows, :], (1, 8))
        cotangent[rows, :] = (out_grad[rows, :].astype(F32) * keep).astype(BF16)

    rowwise(first_norm)
    weights[1].wait()

    def lift(i, cols):
        lin = dot(scaled_one[...], up_w[:, cols])
        gated = sigmoid(dot(scaled_one[...], up_w[:, pl.ds(pl.multiple_of(i * 256 + 1024, 256), 256)]))
        keep = jnp.tile(mask[...], (1, 2))
        product = (lin * gated * keep).astype(BF16)
        linear[:, cols] = lin
        gate[:, cols] = gated
        glu[:, cols] = product
        glu_even[pl.ds(64, 256), cols] = product.astype(F32)

    colwise(lift)
    pl.semaphore_wait(barrier, len(peers))

    def swap_rims(src, dst):
        up = send(src.at[pl.ds(192, 64)], before.at[dst], right)
        down = send(src.at[pl.ds(0, 64)], after.at[dst], left)
        return up, down

    def take_rims(copies, slot, dst):
        for copy in copies:
            copy.wait_recv()
        dst[pl.ds(0, 64), :] = jnp.where(ctx > 0, before[slot].astype(F32), 0.0)
        dst[pl.ds(320, 64), :] = jnp.where(ctx < 63, after[slot].astype(F32), 0.0)

    rims = swap_rims(glu, 0)
    weights[2].wait()

    def lift_back(i, cols):
        act_grad[:, cols] = dot_t(cotangent[...], down_w[cols, :])

    colwise(lift_back)
    take_rims(rims, 0, glu_even)
    four_later(glu_even, glu_odd)

    def tiles(body):
        def step(i, carry):
            tile, block = i // 4, lax.rem(i, 4)
            body(pl.multiple_of(block * 64, 64), pl.ds(pl.multiple_of(tile * 128, 128), 128))
            return carry

        lax.fori_loop(0, 32, step, 0)

    def shifted(even, odd, base, ahead, cols):
        if ahead % 2 == 0:
            return even[pl.ds(base + ahead * 4, 64), cols]
        return odd[pl.ds(base + ahead * 4 - 4, 64), cols]

    def convolve(base, cols):
        acc = jnp.zeros((64, 128), F32)
        for j in range(31):
            acc = acc + taps[j : j + 1, cols] * shifted(glu_even, glu_odd, base, j + 1, cols)
        conv[pl.ds(base, 64), cols] = acc

    tiles(convolve)
    sums[...] = jnp.zeros_like(sums)

    def second_norm(rows):
        normed, inverse = moments(conv[rows, :])
        pre = normed * gain_two[...]
        s = sigmoid(pre)
        activated[rows, :] = (pre * s).astype(BF16)
        back = act_grad[rows, :] * s * (1.0 + pre * (1.0 - s))
        weighted = back * normed
        sums[0] += weighted[:8] + weighted[8:]
        q = back * gain_two[...]
        mean_q = jnp.mean(q, axis=-1, keepdims=True)
        mean_qn = jnp.mean(q * normed, axis=-1, keepdims=True)
        result = (inverse * (q - mean_q - normed * mean_qn)).astype(BF16)
        conv_grad[rows, :] = result
        grad_even[pl.ds(rows.start + 64, 16), :] = result.astype(F32)

    rowwise(second_norm)
    rims = swap_rims(conv_grad, 1)

    def finish(i, cols):
        block_out[:, cols] = (hidden[:, cols] + dot(activated[...], down_w[:, cols])).astype(BF16)

    colwise(finish)

    upper = lax.broadcasted_iota(jnp.int32, (32, 8, 512), 1) < 4

    def down_tile(i, cols):
        tile = t_dot(cotangent[:, cols], activated[...]).reshape(32, 8, 1024)
        first, second = tile[:, :, :512], tile[:, :, 512:]
        even = jnp.where(upper, first, pltpu.roll(second, 4, 1)).astype(BF16)
        odd = jnp.where(upper, pltpu.roll(first, 4, 1), second).astype(BF16)
        for n in range(32):
            x_lo, y, z = n // 16, (n // 4) % 4, 2 * (n % 4)
            grads[i // 2, lax.rem(i, 2), x_lo, y, z, :, pl.ds(1024, 512)] = even[n]
            grads[i // 2, lax.rem(i, 2), x_lo, y, z + 1, :, pl.ds(1024, 512)] = odd[n]

    colwise(down_tile)

    def tap_step(i, carry):
        cols = pl.ds(pl.multiple_of(i * 128, 128), 128)
        for block in range(4):
            local = grad_even[pl.ds(64 + block * 64, 64), cols]
            for j in range(31):
                product = local * shifted(glu_even, glu_odd, block * 64, j + 1, cols)
                part = jnp.sum(product.reshape(8, 8, 128), axis=0)
                if block == 0:
                    tap_sums[j, :, cols] = part
                else:
                    tap_sums[j, :, cols] += part
        return carry

    lax.fori_loop(0, 8, tap_step, 0)
    take_rims(rims, 1, grad_even)
    four_later(grad_even, grad_odd)

    def convolve_back(base, cols):
        acc = jnp.zeros((64, 128), F32)
        for j in range(31):
            acc = acc + taps[j : j + 1, cols] * shifted(grad_even, grad_odd, base, 31 - j, cols)
        rows = pl.ds(base, 64)
        acc = acc * mask[rows, :]
        g = gate[rows, cols]
        acc_g = acc * g
        lifted_grad[rows, cols] = acc_g.astype(BF16)
        other_cols = pl.ds(pl.multiple_of(cols.start + 1024, 128), 128)
        lifted_grad[rows, other_cols] = (acc_g * linear[rows, cols] * (1.0 - g)).astype(BF16)

    tiles(convolve_back)

    def up_tile(i, cols):
        tile = t_dot(lifted_grad[:, cols], scaled_one[...]).reshape(4, 8, 8, 1024).astype(BF16)
        grads[i // 4, lax.rem(i // 2, 2), lax.rem(i, 2), :, :, :, pl.ds(0, 1024)] = tile

    colwise(up_tile, 8)

    def input_tile(i, cols):
        grad = dot_t(lifted_grad[...], up_w[cols, :])
        product = grad * normed_one[:, cols]
        sums[1, :, cols] = jnp.sum(product.reshape(32, 8, 256), axis=0)

    colwise(input_tile)

    rows_33 = [jnp.sum(tap_sums[j], axis=0, keepdims=True) for j in range(31)]
    rows_33 += [jnp.sum(sums[1], axis=0, keepdims=True), jnp.sum(sums[0], axis=0, keepdims=True)]
    small = jnp.concatenate(rows_33 + [jnp.zeros((128 - 33, 1024), F32)], axis=0)
    for tile in range(8):
        turned[pl.ds(tile * 128, 128), :] = small[:, tile * 128 : tile * 128 + 128].T

    def scatter(i, carry):
        eight = turned[pl.ds(pl.multiple_of(i * 8, 8), 8), :]
        x_hi, core, x_lo = i // 64, lax.rem(i // 32, 2), lax.rem(i // 16, 2)
        y, z = lax.rem(i // 4, 4), lax.rem(i, 4) * 2
        grads[x_hi, core, x_lo, y, z, :, pl.ds(1536, 128)] = eight.astype(BF16)
        grads[x_hi, core, x_lo, y, z + 1, :, pl.ds(1536, 128)] = pltpu.roll(eight, 4, 0).astype(BF16)
        return carry

    lax.fori_loop(0, 128, scatter, 0)
    sum_phase(where, send, grads, total_out, *sum_scratch)
    for copy in started:
        copy.wait_send()


def on_device(
    residual, projections, out_weight, gain_one, up_weight, conv_kernel, gain_two, down_weight,
    lengths, out_grad,
):
    context = attend(projections, lengths)
    dma = pltpu.SemaphoreType.DMA
    wide, narrow = PART_Y[1], PART_Z[1]
    vmem_spec = pl.BlockSpec(memory_space=pltpu.VMEM)
    any_spec = pl.BlockSpec(memory_space=pl.ANY)

    def vmem(*shape):
        return pltpu.VMEM(shape, BF16)

    def wide_vmem(*shape):
        return pltpu.VMEM(shape, F32)

    block, total = pl.pallas_call(
        block_kernel,
        out_shape=(
            jax.ShapeDtypeStruct((256, 1024), BF16),
            jax.ShapeDtypeStruct((8, CHUNK), F32),
        ),
        in_specs=[vmem_spec] * 3
        + [pl.BlockSpec(memory_space=pltpu.SMEM)]
        + [vmem_spec] * 3
        + [any_spec] * 3,
        out_specs=(vmem_spec, vmem_spec),
        scratch_shapes=[
            vmem(1024, 1024), vmem(1024, 2048), vmem(1024, 1024),
            wide_vmem(256, 128), wide_vmem(256, 1024), wide_vmem(256, 1024),
            vmem(256, 1024), wide_vmem(256, 1024), wide_vmem(256, 1024), vmem(256, 1024),
            wide_vmem(384, 1024), wide_vmem(384, 1024), wide_vmem(384, 1024),
            wide_vmem(384, 1024), wide_vmem(256, 1024), wide_vmem(8, 128),
            wide_vmem(8, 128), vmem(256, 1024),
            vmem(256, 1024), wide_vmem(256, 1024), vmem(256, 1024), vmem(256, 2048),
            vmem(2, 64, 1024), vmem(2, 64, 1024),
            wide_vmem(31, 8, 1024), wide_vmem(2, 8, 1024), wide_vmem(1024, 128),
            vmem(2, 2, 2, 4, 8, 8, CHUNK),
            vmem(2, 2, 4, 8, 8, CHUNK),
            vmem(3, 2, 2, 8, 8, wide), vmem(2, 2, 8, 8, wide),
            vmem(3, 8, 8, wide), vmem(8, 8, wide), vmem(7, 8, wide),
            vmem(3, 4, 8, 8, wide), vmem(4, 8, 8, wide),
            vmem(3, 8, 8, wide), vmem(8, 8, wide), vmem(7, 8, wide),
            vmem(7, 2, 2, 4, 8, narrow), vmem(2, 2, 4, 8, narrow),
            vmem(3, 4, 8, narrow), vmem(4, 8, narrow), vmem(3, 8, narrow),
            dma((3,)), dma((56,)), dma((56,)),
        ],
        compiler_params=pltpu.CompilerParams(
            collective_id=2, has_side_effects=True, vmem_limit_bytes=58 << 20
        ),
        name="block_and_sums",
    )(
        context,
        residual.reshape(256, 1024),
        out_grad.reshape(256, 1024),
        lengths,
        gain_one.reshape(1, 1024),
        gain_two.reshape(1, 1024),
        conv_kernel,
        out_weight,
        up_weight,
        down_weight,
    )
    return (
        block.reshape(64, 4, 1024),
        total[:, :1024],
        total[:, 1024:1536].reshape(2, 4, 512).transpose(1, 0, 2).reshape(4, 1024),
        total[:4, 1536:1567],
        total[:4, 1567],
        total[:4, 1568],
    )


def solution(mesh):
    in_specs = (
        P("ctx", "dp", None),
        P("ctx", "dp", None),
        P(),
        P(),
        P(),
        P(),
        P(),
        P(),
        P("dp"),
        P("ctx", "dp", None),
    )
    out_specs = (
        P("ctx", "dp", None),
        P(("dp", "ctx"), None),
        P(("dp", "ctx"), None),
        P(("dp", "ctx"), None),
        P(("dp", "ctx")),
        P(("dp", "ctx")),
    )
    return jax.shard_map(
        on_device, mesh=mesh, in_specs=in_specs, out_specs=out_specs, check_vma=False
    )
```

```python
import functools

import jax
import jax.numpy as jnp
from jax import lax
from jax.experimental import pallas as pl
from jax.experimental.pallas import tpu as pltpu
from jax.sharding import PartitionSpec as P

EPSILON = 1e-05
LOG2E = 1.4426950408889634
MESH = pl.DeviceIdType.MESH
BF16 = jnp.bfloat16
F32 = jnp.float32

UP_PARTS = ((0, 256), (256, 512), (768, 384))
DOWN_PARTS = ((0, 128), (128, 128), (256, 256))


def lane_ids(shape):
    return lax.broadcasted_iota(jnp.int32, shape, len(shape) - 1)


def dot(a, b):
    return jnp.dot(a, b, preferred_element_type=F32)


def dot_t(a, b):
    return lax.dot_general(a, b, (((1,), (1,)), ((), ())), preferred_element_type=F32)


def t_dot(a, b):
    return lax.dot_general(a, b, (((0,), (0,)), ((), ())), preferred_element_type=F32)


def sigmoid(x):
    return 1.0 / (1.0 + jnp.exp(-x))


def moments(values):
    center = values - jnp.mean(values, axis=-1, keepdims=True)
    inverse = lax.rsqrt(jnp.mean(center * center, axis=-1, keepdims=True) + EPSILON)
    return center * inverse, inverse


def loop(count, body):
    def step(i, carry):
        body(i)
        return carry

    lax.fori_loop(0, count, step, 0)


def aligned(start, size):
    return pl.ds(pl.multiple_of(start, size), size)


class Place:
    def __init__(self):
        dp, ctx = lax.axis_index("dp"), lax.axis_index("ctx")
        self.dp, self.ctx = dp, ctx
        self.x_hi, self.core = dp // 2, lax.rem(dp, 2)
        self.x_lo, self.y, self.z = ctx // 32, lax.rem(ctx // 8, 4), lax.rem(ctx, 8)
        self.sibling = (self.x_hi * 2 + 1 - self.core, ctx)

    def x_split(self, k):
        to = lax.rem(self.x_hi * 2 + self.x_lo + k, 4)
        return to // 2, lax.rem(to, 2)

    def along_x(self, k):
        hi, lo = self.x_split(k)
        return hi * 2 + self.core, lo * 32 + self.y * 8 + self.z

    def along_y(self, k):
        return self.dp, self.x_lo * 32 + lax.rem(self.y + k, 4) * 8 + self.z

    def along_z(self, k):
        return self.dp, self.x_lo * 32 + self.y * 8 + lax.rem(self.z + k, 8)


class Mail:
    def __init__(self, ssem, rsem):
        self.ssem, self.rsem, self.used, self.sent = ssem, rsem, 0, []

    def send(self, src, dst, peer):
        copy = pltpu.make_async_remote_copy(
            src_ref=src, dst_ref=dst, send_sem=self.ssem.at[self.used],
            recv_sem=self.rsem.at[self.used], device_id=peer, device_id_type=MESH,
        )
        copy.start()
        self.used += 1
        self.sent.append(copy)
        return copy

    def reserve(self, count):
        base = self.used
        self.used += count
        return base

    def close(self):
        for copy in self.sent:
            copy.wait_send()


def receive(copies):
    for copy in copies:
        copy.wait_recv()


class Sum:
    def __init__(self, place, mail, mine, parts, scratch, out, offset):
        self.place, self.mail, self.mine, self.out, self.offset = place, mail, mine, out, offset
        self.parts = parts
        self.z_lanes, self.y_lanes, self.x_lanes = [pl.ds(a, n) for a, n in parts]
        (self.y_in, self.y_sum, self.yx_in, self.yx_sum, self.yxz_in,
         self.x_in, self.x_sum, self.xy_in, self.xy_sum, self.xyz_in,
         self.z_in, self.z_sum, self.zx_in, self.zx_sum, self.zxy_in) = scratch

    @staticmethod
    def scratch(parts):
        (_, wz), (_, wy), (_, wx) = parts
        shapes = [
            (3, 2, 2, 8, 8, wy), (2, 2, 8, 8, wy), (3, 8, 8, wy), (8, 8, wy), (7, 8, wy),
            (3, 4, 8, 8, wx), (4, 8, 8, wx), (3, 8, 8, wx), (8, 8, wx), (7, 8, wx),
            (7, 2, 2, 4, 8, wz), (2, 2, 4, 8, wz), (3, 4, 8, wz), (4, 8, wz), (3, 8, wz),
        ]
        return [pltpu.VMEM(shape, BF16) for shape in shapes]

    def first(self):
        p, mine, mail = self.place, self.mine, self.mail
        self.one_y = [
            mail.send(
                mine.at[:, :, lax.rem(p.y + k, 4), :, :, self.y_lanes],
                self.y_in.at[k - 1], p.along_y(k),
            )
            for k in (1, 2, 3)
        ]
        self.one_x = []
        for k in (1, 2, 3):
            hi, lo = p.x_split(k)
            self.one_x.append(
                mail.send(
                    mine.at[hi, lo, :, :, :, self.x_lanes], self.x_in.at[k - 1], p.along_x(k)
                )
            )
        self.one_z = [
            mail.send(
                mine.at[:, :, :, lax.rem(p.z + k, 8), :, self.z_lanes],
                self.z_in.at[k - 1], p.along_z(k),
            )
            for k in range(1, 8)
        ]

    def second(self):
        p, mine, mail = self.place, self.mine, self.mail
        receive(self.one_y)

        def y_body(i):
            a, b = i // 2, lax.rem(i, 2)
            acc = mine[a, b, p.y, :, :, self.y_lanes].astype(F32)
            for k in range(3):
                acc = acc + self.y_in[k, a, b].astype(F32)
            self.y_sum[a, b] = acc.astype(BF16)

        loop(4, y_body)
        self.two_y = []
        for k in (1, 2, 3):
            hi, lo = p.x_split(k)
            self.two_y.append(
                mail.send(self.y_sum.at[hi, lo], self.yx_in.at[k - 1], p.along_x(k))
            )
        receive(self.one_x)

        def x_body(i):
            acc = mine[p.x_hi, p.x_lo, i, :, :, self.x_lanes].astype(F32)
            for k in range(3):
                acc = acc + self.x_in[k, i].astype(F32)
            self.x_sum[i] = acc.astype(BF16)

        loop(4, x_body)
        self.two_x = [
            mail.send(self.x_sum.at[lax.rem(p.y + k, 4)], self.xy_in.at[k - 1], p.along_y(k))
            for k in (1, 2, 3)
        ]
        receive(self.one_z)

        def z_body(i):
            a, b = i // 2, lax.rem(i, 2)
            acc = mine[a, b, :, p.z, :, self.z_lanes].astype(F32)
            for k in range(7):
                acc = acc + self.z_in[k, a, b].astype(F32)
            self.z_sum[a, b] = acc.astype(BF16)

        loop(4, z_body)
        self.two_z = []
        for k in (1, 2, 3):
            hi, lo = p.x_split(k)
            self.two_z.append(
                mail.send(self.z_sum.at[hi, lo], self.zx_in.at[k - 1], p.along_x(k))
            )

    def third(self):
        p, mail = self.place, self.mail

        def add(copies, own, received, dst):
            receive(copies)
            acc = own[...].astype(F32)
            for k in range(3):
                acc = acc + received[k].astype(F32)
            dst[...] = acc.astype(BF16)

        add(self.two_y, self.y_sum.at[p.x_hi, p.x_lo], self.yx_in, self.yx_sum)
        self.three_y = [
            mail.send(self.yx_sum.at[lax.rem(p.z + k, 8)], self.yxz_in.at[k - 1], p.along_z(k))
            for k in range(1, 8)
        ]
        add(self.two_x, self.x_sum.at[p.y], self.xy_in, self.xy_sum)
        self.three_x = [
            mail.send(self.xy_sum.at[lax.rem(p.z + k, 8)], self.xyz_in.at[k - 1], p.along_z(k))
            for k in range(1, 8)
        ]
        add(self.two_z, self.z_sum.at[p.x_hi, p.x_lo], self.zx_in, self.zx_sum)
        self.three_z = [
            mail.send(self.zx_sum.at[lax.rem(p.y + k, 4)], self.zxy_in.at[k - 1], p.along_y(k))
            for k in (1, 2, 3)
        ]

    def last(self):
        p = self.place
        for copies, own, received, count, (start, width) in (
            (self.three_y, self.yx_sum.at[p.z], self.yxz_in, 7, self.parts[1]),
            (self.three_x, self.xy_sum.at[p.z], self.xyz_in, 7, self.parts[2]),
            (self.three_z, self.zx_sum.at[p.y], self.zxy_in, 3, self.parts[0]),
        ):
            receive(copies)
            acc = own[...].astype(F32)
            for k in range(count):
                acc = acc + received[k].astype(F32)
            self.out[:, pl.ds(self.offset + start, width)] = acc


def four_later(src, dst):
    def body(i):
        base = pl.multiple_of(i * 8, 8)
        dst[pl.ds(base, 8), :] = jnp.concatenate(
            [src[pl.ds(base, 8), :][4:], src[pl.ds(base + 8, 8), :][:4]], axis=0
        )

    loop(47, body)


def whole_kernel(
    projections, residual, out_grad, lengths, gain_one, gain_two, taps,
    out_w_hbm, up_w_hbm, down_w_hbm,
    block_out, total_out,
    pbuf, rbuf, gbuf, rows32, kv_send, q_send, kv_recv, q_recv, o_send, o_recv,
    queries, keys, values, running, totals, context,
    load_sem, kv_ssem, q_ssem, o_ssem, kv_rsem, q_rsem, o_rsem,
    out_w, up_w, down_w, mask, hidden, normed_one, scaled_one, linear, gate, glu,
    glu_even, glu_odd, grad_even, grad_odd, conv, activated,
    cotangent, act_grad, conv_grad, lifted_grad, before, after, tap_sums, sums, turned,
    up_grads, down_grads, up_other, down_other, wsem, ssem, rsem,
    *sum_scratch,
):
    place = Place()
    mail = Mail(ssem, rsem)
    dp, me, core = place.dp, place.ctx, place.core
    group = me // 8
    loads = []
    for i, (src, dst) in enumerate(
        (
            (projections, pbuf), (out_grad, gbuf), (down_w_hbm, down_w), (residual, rbuf),
            (out_w_hbm, out_w), (up_w_hbm, up_w),
        )
    ):
        copy = pltpu.make_async_copy(src, dst, wsem.at[i])
        copy.start()
        loads.append(copy)
    barrier = pltpu.get_barrier_semaphore()

    def greet(i):
        peer = (dp, lax.rem(me + i + 1, 64))
        pl.semaphore_signal(barrier, inc=1, device_id=peer, device_id_type=MESH)

    loop(63, greet)
    for peer in [place.sibling] + [place.along_x(k) for k in (1, 2, 3)]:
        pl.semaphore_signal(barrier, inc=1, device_id=peer, device_id_type=MESH)
    loads[0].wait()

    def widen(i):
        both = jnp.concatenate([pbuf[i * 2 + n].astype(F32) for n in range(2)], axis=0)
        for tile in range(24):
            rows32[tile, aligned(i * 8, 8), :] = both[:, tile * 128 : tile * 128 + 128]

    loop(32, widen)
    low = lane_ids((64, 128)) < 64
    low32 = lane_ids((32, 128)) < 64

    def pack(i):
        utt, duo = i // 8, lax.rem(i, 8)
        rows = pl.ds(utt, 64, stride=4)
        first, second, third = [rows32[duo * 3 + n, rows, :] for n in range(3)]
        first_t, second_t = pltpu.roll(first, 64, 1), pltpu.roll(second, 64, 1)
        kv_send[i * 2] = jnp.where(low, first_t, second_t).astype(BF16)
        kv_send[i * 2 + 1] = third.astype(BF16)
        q_send[i * 2] = jnp.where(low32, first[:32], first_t[32:]).astype(BF16)
        q_send[i * 2 + 1] = jnp.where(low32, second_t[:32], second[32:]).astype(BF16)

    loop(32, pack)
    pl.semaphore_wait(barrier, 67)

    def push(src, dst, send_sem, recv_sem, target):
        @pl.when(target != me)
        def _():
            pltpu.make_async_remote_copy(
                src_ref=src, dst_ref=dst, send_sem=send_sem, recv_sem=recv_sem,
                device_id=(dp, target), device_id_type=MESH,
            ).start()

        @pl.when(target == me)
        def _():
            pltpu.make_async_copy(src, dst, recv_sem).start()

    def nth_target(i):
        return lax.rem(group + i // 8, 8) * 8 + lax.rem(place.z + i, 8)

    def push_queries(i):
        target = nth_target(i)
        push(q_send.at[target], q_recv.at[me], q_ssem, q_rsem.at[group], target)

    def push_keys(i):
        target = nth_target(i)
        push(kv_send.at[target], kv_recv.at[me], kv_ssem, kv_rsem.at[group], target)

    loop(64, push_queries)
    loop(64, push_keys)

    row = lax.broadcasted_iota(jnp.int32, (256, 128), 0)
    utt = lax.rem(row, 4)
    limit = jnp.where(
        utt < 2,
        jnp.where(utt == 0, lengths[0], lengths[1]),
        jnp.where(utt == 2, lengths[2], lengths[3]),
    )
    mask[...] = jnp.where(me * 64 + row // 4 < limit, 1.0, 0.0)
    loads[1].wait()

    def take_cotangent(i):
        four = jnp.concatenate([gbuf[i * 4 + n].astype(F32) for n in range(4)], axis=0)
        rows = aligned(i * 16, 16)
        cotangent[rows, :] = (four * jnp.tile(mask[rows, :], (1, 8))).astype(BF16)

    loop(16, take_cotangent)
    loads[2].wait()

    def lift_back(i):
        cols = aligned(i * 256, 256)
        act_grad[:, cols] = dot_t(cotangent[...], down_w[cols, :])

    loop(4, lift_back)
    loads[3].wait()

    def take_residual(i):
        both = jnp.concatenate([rbuf[i * 2 + n].astype(F32) for n in range(2)], axis=0)
        hidden[aligned(i * 8, 8), :] = both

    loop(32, take_residual)
    loads[4].wait()
    loads[5].wait()

    def clear(i):
        rows = aligned(i * 512, 512)
        running[rows, :] = jnp.full((512, 128), -1e30, F32)
        totals[rows, :] = jnp.zeros((512, 128), F32)

    loop(8, clear)
    half = lane_ids((256, 128))

    def take_queries(i):
        src = lax.rem(group - i + 8, 8)
        eight = aligned(src * 8, 8)
        pltpu.make_async_copy(q_recv.at[eight], q_recv.at[eight], q_rsem.at[src]).wait()
        query = q_recv[eight].reshape(256, 128).astype(F32) * (0.125 * LOG2E)
        high = query.astype(BF16).astype(F32)
        rest = query - high
        one = jnp.where(half == 0, 1.0, 0.0)
        early = jnp.where(half < 64, high, pltpu.roll(rest, 64, 1))
        late = jnp.where(half < 64, pltpu.roll(high, 64, 1), rest)
        queries[aligned(src * 512, 512), :] = jnp.concatenate(
            [jnp.concatenate([early, one], axis=1), jnp.concatenate([late, one], axis=1)], axis=0
        ).astype(BF16)

    loop(8, take_queries)
    length = lengths[me // 16]

    def with_keys(i, finish):
        src = lax.rem(group - i + 8, 8)
        eight = aligned(src * 8, 8)
        pltpu.make_async_copy(kv_recv.at[eight], kv_recv.at[eight], kv_rsem.at[src]).wait()
        kv = kv_recv[eight].reshape(512, 128).astype(F32)
        lane = lane_ids((512, 128))
        frame = src * 512 + lax.broadcasted_iota(jnp.int32, (512, 128), 0)
        keys[:, :128] = jnp.where(lane < 64, kv, pltpu.roll(kv, 64, 1)).astype(BF16)
        keys[:, 128:] = jnp.where((lane == 0) & (frame >= length), -30000.0, 0.0).astype(BF16)
        values[...] = jnp.where(lane < 64, 1.0, kv).astype(BF16)

        def block_of(n):
            return aligned(lax.rem(group - n + 8, 8) * 512, 512)

        now = dot_t(queries[block_of(0), :], keys[...])
        for n in range(8):
            later = dot_t(queries[block_of(n + 1), :], keys[...]) if n < 7 else None
            rows = block_of(n)
            highest = running[rows, :]
            top = jnp.maximum(highest, jnp.max(now, axis=1, keepdims=True))
            probs = jnp.exp2(now - jnp.tile(top, (1, 4))).astype(BF16)
            total = totals[rows, :] * jnp.exp2(highest - top) + dot(probs, values[...])
            if finish is None:
                running[rows, :] = top
                totals[rows, :] = total
            else:
                finish(n, total)
            now = later

    loop(7, lambda i: with_keys(i, None))

    def reply(n, total):
        src = lax.rem(group - n + 8, 8)
        normed = total / pltpu.roll(total, 64, 1)
        result = jnp.where(half < 64, pltpu.roll(normed[:256], 64, 1), normed[256:])
        o_send[aligned(src * 8, 8)] = result.astype(BF16).reshape(8, 32, 128)

        def push_one(item):
            target = src * 8 + lax.rem(place.z + item, 8)
            push(o_send.at[target], o_recv.at[me], o_ssem, o_rsem.at[group], target)

        loop(8, push_one)

    with_keys(7, reply)

    def gather(i):
        src = lax.rem(group + i, 8)
        eight = aligned(src * 8, 8)
        pltpu.make_async_copy(o_recv.at[eight], o_recv.at[eight], o_rsem.at[src]).wait()
        for n in range(4):
            which = src * 4 + n
            utt, duo = which // 8, lax.rem(which, 8)
            left = o_recv[which * 2].astype(F32)
            right = o_recv[which * 2 + 1].astype(F32)
            upper = jnp.where(low32, left, pltpu.roll(right, 64, 1))
            lower = jnp.where(low32, pltpu.roll(left, 64, 1), right)
            rows32[duo, pl.ds(utt, 64, stride=4), :] = jnp.concatenate([upper, lower], axis=0)

    loop(8, gather)
    for tile in range(8):
        context[:, tile * 128 : tile * 128 + 128] = rows32[tile].astype(BF16)

    def project(i):
        cols = aligned(i * 256, 256)
        hidden[:, cols] = hidden[:, cols] + dot(context[...], out_w[:, cols])

    loop(4, project)

    def first_norm(i):
        rows = aligned(i * 16, 16)
        normed, _ = moments(hidden[rows, :])
        normed_one[rows, :] = normed
        scaled_one[rows, :] = (normed * gain_one[...]).astype(BF16)

    loop(16, first_norm)

    def lift(i):
        cols = aligned(i * 256, 256)
        lin = dot(scaled_one[...], up_w[:, cols])
        gated = sigmoid(dot(scaled_one[...], up_w[:, aligned(i * 256 + 1024, 256)]))
        product = (lin * gated * jnp.tile(mask[...], (1, 2))).astype(BF16)
        linear[:, cols] = lin
        gate[:, cols] = gated
        glu[:, cols] = product
        glu_even[pl.ds(64, 256), cols] = product.astype(F32)

    loop(4, lift)
    left_peer, right_peer = (dp, lax.rem(me + 63, 64)), (dp, lax.rem(me + 1, 64))

    def swap_rims(src, slot):
        return [
            mail.send(src.at[pl.ds(192, 64)], before.at[slot], right_peer),
            mail.send(src.at[pl.ds(0, 64)], after.at[slot], left_peer),
        ]

    def take_rims(copies, slot, dst):
        receive(copies)
        dst[pl.ds(0, 64), :] = jnp.where(me > 0, before[slot].astype(F32), 0.0)
        dst[pl.ds(320, 64), :] = jnp.where(me < 63, after[slot].astype(F32), 0.0)

    take_rims(swap_rims(glu, 0), 0, glu_even)
    four_later(glu_even, glu_odd)

    def tiles(body):
        def step(i):
            body(pl.multiple_of(lax.rem(i, 4) * 64, 64), aligned((i // 4) * 128, 128))

        loop(32, step)

    def shifted(even, odd, base, ahead, cols):
        if ahead % 2 == 0:
            return even[pl.ds(base + ahead * 4, 64), cols]
        return odd[pl.ds(base + ahead * 4 - 4, 64), cols]

    def convolve(base, cols):
        acc = jnp.zeros((64, 128), F32)
        for j in range(31):
            acc = acc + taps[j : j + 1, cols] * shifted(glu_even, glu_odd, base, j + 1, cols)
        conv[pl.ds(base, 64), cols] = acc

    tiles(convolve)
    sums[...] = jnp.zeros_like(sums)

    def second_norm(i):
        rows = aligned(i * 16, 16)
        normed, inverse = moments(conv[rows, :])
        pre = normed * gain_two[...]
        s = sigmoid(pre)
        activated[rows, :] = (pre * s).astype(BF16)
        back = act_grad[rows, :] * s * (1.0 + pre * (1.0 - s))
        weighted = back * normed
        sums[0] += weighted[:8] + weighted[8:]
        q = back * gain_two[...]
        mean_q = jnp.mean(q, axis=-1, keepdims=True)
        mean_qn = jnp.mean(q * normed, axis=-1, keepdims=True)
        result = (inverse * (q - mean_q - normed * mean_qn)).astype(BF16)
        conv_grad[rows, :] = result
        grad_even[pl.ds(rows.start + 64, 16), :] = result.astype(F32)

    loop(16, second_norm)
    rims = swap_rims(conv_grad, 1)

    upper = lax.broadcasted_iota(jnp.int32, (32, 8, 512), 1) < 4
    down_base = mail.reserve(2)

    def down_tile(hi, side):
        cols = aligned(hi * 512 + side * 256, 256)
        tile = t_dot(cotangent[:, cols], activated[...]).reshape(32, 8, 1024)
        first, second = tile[:, :, :512], tile[:, :, 512:]
        even = jnp.where(upper, first, pltpu.roll(second, 4, 1)).astype(BF16)
        odd = jnp.where(upper, pltpu.roll(first, 4, 1), second).astype(BF16)
        for n in range(32):
            at = (n // 16, (n // 4) % 4, 2 * (n % 4))
            down_grads[hi, side, at[0], at[1], at[2]] = even[n]
            down_grads[hi, side, at[0], at[1], at[2] + 1] = odd[n]

    def down_far(hi):
        down_tile(hi, 1 - core)
        pltpu.make_async_remote_copy(
            src_ref=down_grads.at[hi, 1 - core], dst_ref=down_other.at[hi],
            send_sem=ssem.at[down_base + hi], recv_sem=rsem.at[down_base + hi],
            device_id=place.sibling, device_id_type=MESH,
        ).start()

    loop(2, down_far)
    loop(2, lambda hi: down_tile(hi, core))

    def finish_block(i):
        cols = aligned(i * 256, 256)
        block_out[:, cols] = (hidden[:, cols] + dot(activated[...], down_w[:, cols])).astype(BF16)

    loop(4, finish_block)
    for hi in range(2):
        pltpu.make_async_copy(
            down_other.at[hi], down_other.at[hi], rsem.at[down_base + hi]
        ).wait()

    def down_join(i):
        at = (i // 8, core, lax.rem(i // 4, 2), lax.rem(i, 4))
        both = down_grads[at].astype(F32) + down_other[at[0], at[2], at[3]].astype(F32)
        down_grads[at] = both.astype(BF16)

    loop(16, down_join)
    down_sum = Sum(
        place, mail, down_grads.at[:, core], DOWN_PARTS, sum_scratch[15:], total_out, 1152
    )
    down_sum.first()

    def tap_step(i):
        cols = aligned(i * 128, 128)
        for block in range(4):
            local = grad_even[pl.ds(64 + block * 64, 64), cols]
            for j in range(31):
                product = local * shifted(glu_even, glu_odd, block * 64, j + 1, cols)
                part = jnp.sum(product.reshape(8, 8, 128), axis=0)
                if block == 0:
                    tap_sums[j, :, cols] = part
                else:
                    tap_sums[j, :, cols] += part

    loop(8, tap_step)
    take_rims(rims, 1, grad_even)
    four_later(grad_even, grad_odd)
    down_sum.second()

    def convolve_back(base, cols):
        acc = jnp.zeros((64, 128), F32)
        for j in range(31):
            acc = acc + taps[j : j + 1, cols] * shifted(grad_even, grad_odd, base, 31 - j, cols)
        rows = pl.ds(base, 64)
        g = gate[rows, cols]
        acc = acc * mask[rows, :] * g
        lifted_grad[rows, cols] = acc.astype(BF16)
        other_cols = pl.ds(pl.multiple_of(cols.start + 1024, 128), 128)
        lifted_grad[rows, other_cols] = (acc * linear[rows, cols] * (1.0 - g)).astype(BF16)

    tiles(convolve_back)
    down_sum.third()

    up_base = mail.reserve(4)
    up_lanes = pl.ds(0, 1024)

    def up_tile(i, side):
        hi, lo = i // 2, lax.rem(i, 2)
        cols = aligned(hi * 1024 + side * 512 + lo * 256, 256)
        return t_dot(lifted_grad[:, cols], scaled_one[...]).reshape(4, 8, 8, 1024)

    def up_far(i):
        hi, lo = i // 2, lax.rem(i, 2)
        up_grads[hi, 1 - core, lo, :, :, :, up_lanes] = up_tile(i, 1 - core).astype(BF16)
        pltpu.make_async_remote_copy(
            src_ref=up_grads.at[hi, 1 - core, lo, :, :, :, up_lanes],
            dst_ref=up_other.at[hi, lo, :, :, :, up_lanes],
            send_sem=ssem.at[up_base + i], recv_sem=rsem.at[up_base + i],
            device_id=place.sibling, device_id_type=MESH,
        ).start()

    loop(4, up_far)

    def input_tile(i):
        cols = aligned(i * 256, 256)
        product = dot_t(lifted_grad[...], up_w[cols, :]) * normed_one[:, cols]
        sums[1, :, cols] = jnp.sum(product.reshape(32, 8, 256), axis=0)

    loop(4, input_tile)

    rows_33 = [jnp.sum(tap_sums[j], axis=0, keepdims=True) for j in range(31)]
    rows_33 += [jnp.sum(sums[1], axis=0, keepdims=True), jnp.sum(sums[0], axis=0, keepdims=True)]
    small = jnp.concatenate(rows_33 + [jnp.zeros((128 - 33, 1024), F32)], axis=0)
    for tile in range(8):
        turned[pl.ds(tile * 128, 128), :] = small[:, tile * 128 : tile * 128 + 128].T
    small_lanes = pl.ds(1024, 128)

    def scatter(i):
        eight = turned[aligned(i * 8, 8), :]
        at = (i // 64, lax.rem(i // 32, 2), lax.rem(i // 16, 2), lax.rem(i // 4, 4))
        z = lax.rem(i, 4) * 2
        up_grads[(*at, z, slice(None), small_lanes)] = eight.astype(BF16)
        up_grads[(*at, z + 1, slice(None), small_lanes)] = pltpu.roll(eight, 4, 0).astype(BF16)

    loop(128, scatter)
    small_copy = mail.send(
        up_grads.at[:, 1 - core, :, :, :, :, small_lanes],
        up_other.at[:, :, :, :, :, small_lanes], place.sibling,
    )

    def up_near(i):
        hi, lo = i // 2, lax.rem(i, 2)
        tile = up_tile(i, core)
        arrived = up_other.at[hi, lo, :, :, :, up_lanes]
        pltpu.make_async_copy(arrived, arrived, rsem.at[up_base + i]).wait()
        up_grads[hi, core, lo, :, :, :, up_lanes] = (tile + arrived[...].astype(F32)).astype(BF16)

    loop(4, up_near)
    small_copy.wait_recv()

    def small_join(i):
        hi, lo = i // 2, lax.rem(i, 2)
        up_grads[hi, core, lo, :, :, :, small_lanes] = (
            up_grads[hi, core, lo, :, :, :, small_lanes].astype(F32)
            + up_other[hi, lo, :, :, :, small_lanes].astype(F32)
        ).astype(BF16)

    loop(4, small_join)
    up_sum = Sum(place, mail, up_grads.at[:, core], UP_PARTS, sum_scratch[:15], total_out, 0)
    up_sum.first()
    down_sum.last()
    up_sum.second()
    up_sum.third()
    up_sum.last()

    mail.close()
    for hi in range(2):
        sent = down_grads.at[hi, 1 - core]
        pltpu.make_async_copy(sent, sent, ssem.at[down_base + hi]).wait()
    for i in range(4):
        sent = up_grads.at[i // 2, 1 - core, i % 2, :, :, :, up_lanes]
        pltpu.make_async_copy(sent, sent, ssem.at[up_base + i]).wait()
    for buf, sem in ((kv_send, kv_ssem), (q_send, q_ssem), (o_send, o_ssem)):
        sent = buf.at[pl.ds(0, 63)]
        pltpu.make_async_copy(sent, sent, sem).wait()


def hand_out_kernel(block, total, block_out, up_grad, down_grad, kernel_grad, one_grad, two_grad):
    def body(i):
        eight = block[aligned(i * 16, 16), :].astype(F32)
        for n in range(4):
            block_out[i * 4 + n] = eight[n * 4 : n * 4 + 4].astype(BF16)

    loop(16, body)
    up_grad[...] = total[:, :1024]
    down = total[:, 1152:1664]
    down_grad[:, :512] = down[:4]
    down_grad[:, 512:] = down[4:]
    small = total[:, 1024:1152]
    kernel_grad[...] = small[:4, :31]
    turned = small.T
    one_grad[...] = turned[31:32, :4]
    two_grad[...] = turned[32:33, :4]


def on_device(
    residual, projections, out_weight, gain_one, up_weight, conv_kernel, gain_two, down_weight,
    lengths, out_grad,
):
    dma = pltpu.SemaphoreType.DMA
    vmem_spec = pl.BlockSpec(memory_space=pltpu.VMEM)
    any_spec = pl.BlockSpec(memory_space=pl.ANY)

    def half(*shape):
        return pltpu.VMEM(shape, BF16)

    def full(*shape):
        return pltpu.VMEM(shape, F32)

    block, total = pl.pallas_call(
        whole_kernel,
        out_shape=(
            jax.ShapeDtypeStruct((256, 1024), BF16),
            jax.ShapeDtypeStruct((8, 1664), F32),
        ),
        in_specs=[any_spec] * 3
        + [pl.BlockSpec(memory_space=pltpu.SMEM)]
        + [vmem_spec] * 3
        + [any_spec] * 3,
        out_specs=(vmem_spec, vmem_spec),
        scratch_shapes=[
            half(64, 4, 3072), half(64, 4, 1024), half(64, 4, 1024), full(24, 256, 128),
            half(64, 64, 128), half(64, 32, 128), half(64, 64, 128), half(64, 32, 128),
            half(64, 32, 128), half(64, 32, 128),
            half(4096, 256), half(512, 256), half(512, 128), full(4096, 128), full(4096, 128),
            half(256, 1024),
            dma, dma, dma, dma, dma((8,)), dma((8,)), dma((8,)),
            half(1024, 1024), half(1024, 2048), half(1024, 1024),
            full(256, 128), full(256, 1024), full(256, 1024), half(256, 1024),
            full(256, 1024), full(256, 1024), half(256, 1024),
            full(384, 1024), full(384, 1024), full(384, 1024), full(384, 1024),
            full(256, 1024), half(256, 1024),
            half(256, 1024), full(256, 1024), half(256, 1024), half(256, 2048),
            half(2, 64, 1024), half(2, 64, 1024),
            full(31, 8, 1024), full(2, 8, 1024), full(1024, 128),
            half(2, 2, 2, 4, 8, 8, 1152), half(2, 2, 2, 4, 8, 8, 512),
            half(2, 2, 4, 8, 8, 1152), half(2, 2, 4, 8, 8, 512),
            dma((6,)), dma((96,)), dma((96,)),
        ]
        + Sum.scratch(UP_PARTS)
        + Sum.scratch(DOWN_PARTS),
        compiler_params=pltpu.CompilerParams(
            collective_id=1, has_side_effects=True, vmem_limit_bytes=63 << 20
        ),
        name="whole_block",
    )(
        projections, residual, out_grad, lengths, gain_one.reshape(1, 1024),
        gain_two.reshape(1, 1024), conv_kernel, out_weight, up_weight, down_weight,
    )
    outs = pl.pallas_call(
        hand_out_kernel,
        out_shape=(
            jax.ShapeDtypeStruct((64, 4, 1024), BF16),
            jax.ShapeDtypeStruct((8, 1024), F32),
            jax.ShapeDtypeStruct((4, 1024), F32),
            jax.ShapeDtypeStruct((4, 31), F32),
            jax.ShapeDtypeStruct((1, 4), F32),
            jax.ShapeDtypeStruct((1, 4), F32),
        ),
        in_specs=[vmem_spec] * 2,
        out_specs=(vmem_spec,) * 6,
        name="hand_out",
    )(block, total)
    return (*outs[:4], outs[4].reshape(4), outs[5].reshape(4))


def solution(mesh):
    in_specs = (
        P("ctx", "dp", None),
        P("ctx", "dp", None),
        P(),
        P(),
        P(),
        P(),
        P(),
        P(),
        P("dp"),
        P("ctx", "dp", None),
    )
    out_specs = (
        P("ctx", "dp", None),
        P(("dp", "ctx"), None),
        P(("dp", "ctx"), None),
        P(("dp", "ctx"), None),
        P(("dp", "ctx")),
        P(("dp", "ctx")),
    )
    return jax.shard_map(
        on_device, mesh=mesh, in_specs=in_specs, out_specs=out_specs, check_vma=False
    )
```

```python
import functools

import jax
import jax.numpy as jnp
from jax import lax
from jax.experimental import pallas as pl
from jax.experimental.pallas import tpu as pltpu
from jax.sharding import PartitionSpec as P

EPSILON = 1e-05
LOG2E = 1.4426950408889634
MESH = pl.DeviceIdType.MESH
BF16 = jnp.bfloat16
F32 = jnp.float32

UP_PARTS = ((0, 256), (256, 384), (640, 384))
SMALL_PARTS = ((0, 0), (0, 0), (0, 128))
DOWN_PARTS = ((0, 128), (128, 128), (256, 256))


def lane_ids(shape):
    return lax.broadcasted_iota(jnp.int32, shape, len(shape) - 1)


def dot(a, b):
    return jnp.dot(a, b, preferred_element_type=F32)


def dot_t(a, b):
    return lax.dot_general(a, b, (((1,), (1,)), ((), ())), preferred_element_type=F32)


def t_dot(a, b):
    return lax.dot_general(a, b, (((0,), (0,)), ((), ())), preferred_element_type=F32)


def sigmoid(x):
    return 1.0 / (1.0 + jnp.exp(-x))


def moments(values):
    center = values - jnp.mean(values, axis=-1, keepdims=True)
    inverse = lax.rsqrt(jnp.mean(center * center, axis=-1, keepdims=True) + EPSILON)
    return center * inverse, inverse


def loop(count, body):
    def step(i, carry):
        body(i)
        return carry

    lax.fori_loop(0, count, step, 0)


def aligned(start, size):
    return pl.ds(pl.multiple_of(start, size), size)


class Place:
    def __init__(self):
        dp, ctx = lax.axis_index("dp"), lax.axis_index("ctx")
        self.dp, self.ctx = dp, ctx
        self.x_hi, self.core = dp // 2, lax.rem(dp, 2)
        self.x_lo, self.y, self.z = ctx // 32, lax.rem(ctx // 8, 4), lax.rem(ctx, 8)
        self.sibling = (self.x_hi * 2 + 1 - self.core, ctx)

    def x_split(self, k):
        to = lax.rem(self.x_hi * 2 + self.x_lo + k, 4)
        return to // 2, lax.rem(to, 2)

    def along_x(self, k):
        hi, lo = self.x_split(k)
        return hi * 2 + self.core, lo * 32 + self.y * 8 + self.z

    def along_y(self, k):
        return self.dp, self.x_lo * 32 + lax.rem(self.y + k, 4) * 8 + self.z

    def along_z(self, k):
        return self.dp, self.x_lo * 32 + self.y * 8 + lax.rem(self.z + k, 8)


class Mail:
    def __init__(self, ssem, rsem):
        self.ssem, self.rsem, self.used, self.sent = ssem, rsem, 0, []

    def send(self, src, dst, peer):
        copy = pltpu.make_async_remote_copy(
            src_ref=src, dst_ref=dst, send_sem=self.ssem.at[self.used],
            recv_sem=self.rsem.at[self.used], device_id=peer, device_id_type=MESH,
        )
        copy.start()
        self.used += 1
        self.sent.append(copy)
        return copy

    def reserve(self, count):
        base = self.used
        self.used += count
        return base

    def close(self):
        for copy in self.sent:
            copy.wait_send()


def receive(copies):
    for copy in copies:
        copy.wait_recv()


class Sum:
    def __init__(self, place, mail, mine, parts, scratch, out, offset):
        self.place, self.mail, self.mine, self.out, self.offset = place, mail, mine, out, offset
        self.parts = parts
        self.one_x, self.one_y, self.one_z = [], [], []
        self.z_lanes, self.y_lanes, self.x_lanes = [pl.ds(a, max(n, 1)) for a, n in parts]
        (self.y_in, self.y_sum, self.yx_in, self.yx_sum, self.yxz_in,
         self.x_in, self.x_sum, self.xy_in, self.xy_sum, self.xyz_in,
         self.z_in, self.z_sum, self.zx_in, self.zx_sum, self.zxy_in) = scratch

    @staticmethod
    def scratch(parts):
        wz, wy, wx = [max(n, 128) for _, n in parts]
        shapes = [
            (3, 2, 2, 8, 8, wy), (2, 2, 8, 8, wy), (3, 8, 8, wy), (8, 8, wy), (7, 8, wy),
            (3, 4, 8, 8, wx), (4, 8, 8, wx), (3, 8, 8, wx), (8, 8, wx), (7, 8, wx),
            (7, 2, 2, 4, 8, wz), (2, 2, 4, 8, wz), (3, 4, 8, wz), (4, 8, wz), (3, 8, wz),
        ]
        return [pltpu.VMEM(shape, BF16) for shape in shapes]

    def first(self, halves=(slice(None),)):
        self.one_x, self.one_y, self.one_z = [], [], []
        for at in halves:
            self.first_yz(at)
        self.first_x()

    def first_yz(self, at):
        p, mine, mail = self.place, self.mine, self.mail
        if self.parts[1][1]:
            for k in (1, 2, 3):
                self.one_y.append(
                    mail.send(
                        mine.at[at, :, lax.rem(p.y + k, 4), :, :, self.y_lanes],
                        self.y_in.at[k - 1, at], p.along_y(k),
                    )
                )
        if self.parts[0][1]:
            for k in range(1, 8):
                self.one_z.append(
                    mail.send(
                        mine.at[at, :, :, lax.rem(p.z + k, 8), :, self.z_lanes],
                        self.z_in.at[k - 1, at], p.along_z(k),
                    )
                )

    def first_x(self):
        p, mine, mail = self.place, self.mine, self.mail
        for k in (1, 2, 3):
            hi, lo = p.x_split(k)
            self.one_x.append(
                mail.send(
                    mine.at[hi, lo, :, :, :, self.x_lanes], self.x_in.at[k - 1], p.along_x(k)
                )
            )

    def second(self):
        if self.parts[1][1]:
            self.second_y()
        self.second_x()
        if self.parts[0][1]:
            self.second_z()

    def second_y(self):
        p, mine, mail = self.place, self.mine, self.mail
        receive(self.one_y)

        def y_body(i):
            a, b = i // 2, lax.rem(i, 2)
            acc = mine[a, b, p.y, :, :, self.y_lanes].astype(F32)
            for k in range(3):
                acc = acc + self.y_in[k, a, b].astype(F32)
            self.y_sum[a, b] = acc.astype(BF16)

        loop(4, y_body)
        self.two_y = []
        for k in (1, 2, 3):
            hi, lo = p.x_split(k)
            self.two_y.append(
                mail.send(self.y_sum.at[hi, lo], self.yx_in.at[k - 1], p.along_x(k))
            )

    def second_x(self):
        p, mine, mail = self.place, self.mine, self.mail
        receive(self.one_x)

        def x_body(i):
            acc = mine[p.x_hi, p.x_lo, i, :, :, self.x_lanes].astype(F32)
            for k in range(3):
                acc = acc + self.x_in[k, i].astype(F32)
            self.x_sum[i] = acc.astype(BF16)

        loop(4, x_body)
        self.two_x = [
            mail.send(self.x_sum.at[lax.rem(p.y + k, 4)], self.xy_in.at[k - 1], p.along_y(k))
            for k in (1, 2, 3)
        ]

    def second_z(self):
        p, mine, mail = self.place, self.mine, self.mail
        receive(self.one_z)

        def z_body(i):
            a, b = i // 2, lax.rem(i, 2)
            acc = mine[a, b, :, p.z, :, self.z_lanes].astype(F32)
            for k in range(7):
                acc = acc + self.z_in[k, a, b].astype(F32)
            self.z_sum[a, b] = acc.astype(BF16)

        loop(4, z_body)
        self.two_z = []
        for k in (1, 2, 3):
            hi, lo = p.x_split(k)
            self.two_z.append(
                mail.send(self.z_sum.at[hi, lo], self.zx_in.at[k - 1], p.along_x(k))
            )

    def third(self):
        p, mail = self.place, self.mail

        def add(copies, own, received, dst):
            receive(copies)
            acc = own[...].astype(F32)
            for k in range(3):
                acc = acc + received[k].astype(F32)
            dst[...] = acc.astype(BF16)

        if self.parts[1][1]:
            add(self.two_y, self.y_sum.at[p.x_hi, p.x_lo], self.yx_in, self.yx_sum)
            self.three_y = [
                mail.send(self.yx_sum.at[lax.rem(p.z + k, 8)], self.yxz_in.at[k - 1], p.along_z(k))
                for k in range(1, 8)
            ]
        add(self.two_x, self.x_sum.at[p.y], self.xy_in, self.xy_sum)
        self.three_x = [
            mail.send(self.xy_sum.at[lax.rem(p.z + k, 8)], self.xyz_in.at[k - 1], p.along_z(k))
            for k in range(1, 8)
        ]
        if self.parts[0][1]:
            add(self.two_z, self.z_sum.at[p.x_hi, p.x_lo], self.zx_in, self.zx_sum)
            self.three_z = [
                mail.send(self.zx_sum.at[lax.rem(p.y + k, 4)], self.zxy_in.at[k - 1], p.along_y(k))
                for k in (1, 2, 3)
            ]

    def last(self):
        p = self.place
        steps = [(self.three_x, self.xy_sum.at[p.z], self.xyz_in, 7, self.parts[2])]
        if self.parts[0][1]:
            steps += [
                (self.three_y, self.yx_sum.at[p.z], self.yxz_in, 7, self.parts[1]),
                (self.three_z, self.zx_sum.at[p.y], self.zxy_in, 3, self.parts[0]),
            ]
        for copies, own, received, count, (start, width) in steps:
            receive(copies)
            acc = own[...].astype(F32)
            for k in range(count):
                acc = acc + received[k].astype(F32)
            self.out[:, pl.ds(self.offset + start, width)] = acc


def four_later(src, dst, start, stop):
    def body(i):
        base = pl.multiple_of((start + i) * 8, 8)
        dst[pl.ds(base, 8), :] = jnp.concatenate(
            [src[pl.ds(base, 8), :][4:], src[pl.ds(base + 8, 8), :][:4]], axis=0
        )

    loop(stop - start, body)


def whole_kernel(
    projections, residual, out_grad, lengths, gain_one, gain_two, taps,
    out_w_hbm, up_w_hbm, down_w_hbm,
    block_out, total_out,
    pbuf, rbuf, gbuf, rows32, kv_send, q_send, kv_recv, q_recv, o_send, o_recv,
    queries, keys, values, running, totals, context,
    load_sem, kv_ssem, q_ssem, o_ssem, kv_rsem, q_rsem, o_rsem,
    out_w, up_w, down_w, mask, hidden, normed_one, scaled_one, linear, gate, glu,
    glu_even, glu_odd, grad_even, grad_odd, conv, activated,
    cotangent, act_grad, conv_grad, lifted_grad, before, after, tap_sums, sums, turned,
    up_grads, down_grads, small_grads, up_other, down_other, small_other, wsem, ssem, rsem,
    *sum_scratch,
):
    place = Place()
    mail = Mail(ssem, rsem)
    dp, me, core = place.dp, place.ctx, place.core
    group = me // 8
    loads = []
    for i, (src, dst) in enumerate(
        (
            (projections, pbuf), (out_grad, gbuf), (down_w_hbm, down_w), (residual, rbuf),
            (out_w_hbm, out_w), (up_w_hbm, up_w),
        )
    ):
        copy = pltpu.make_async_copy(src, dst, wsem.at[i])
        copy.start()
        loads.append(copy)
    barrier = pltpu.get_barrier_semaphore()

    def greet(i):
        peer = (dp, lax.rem(me + i + 1, 64))
        pl.semaphore_signal(barrier, inc=1, device_id=peer, device_id_type=MESH)

    loop(63, greet)
    for peer in [place.sibling] + [place.along_x(k) for k in (1, 2, 3)]:
        pl.semaphore_signal(barrier, inc=1, device_id=peer, device_id_type=MESH)
    loads[0].wait()

    def widen(i):
        both = jnp.concatenate([pbuf[i * 2 + n].astype(F32) for n in range(2)], axis=0)
        for tile in range(24):
            rows32[tile, aligned(i * 8, 8), :] = both[:, tile * 128 : tile * 128 + 128]

    loop(32, widen)
    low = lane_ids((64, 128)) < 64
    low32 = lane_ids((32, 128)) < 64

    def pack(i):
        utt, duo = i // 8, lax.rem(i, 8)
        rows = pl.ds(utt, 64, stride=4)
        first, second, third = [rows32[duo * 3 + n, rows, :] for n in range(3)]
        first_t, second_t = pltpu.roll(first, 64, 1), pltpu.roll(second, 64, 1)
        kv_send[i * 2] = jnp.where(low, first_t, second_t).astype(BF16)
        kv_send[i * 2 + 1] = third.astype(BF16)
        q_send[i * 2] = jnp.where(low32, first[:32], first_t[32:]).astype(BF16)
        q_send[i * 2 + 1] = jnp.where(low32, second_t[:32], second[32:]).astype(BF16)

    loop(32, pack)
    pl.semaphore_wait(barrier, 67)

    def push(src, dst, send_sem, recv_sem, target):
        @pl.when(target != me)
        def _():
            pltpu.make_async_remote_copy(
                src_ref=src, dst_ref=dst, send_sem=send_sem, recv_sem=recv_sem,
                device_id=(dp, target), device_id_type=MESH,
            ).start()

        @pl.when(target == me)
        def _():
            pltpu.make_async_copy(src, dst, recv_sem).start()

    def nth_target(i):
        return lax.rem(group + i // 8, 8) * 8 + lax.rem(place.z + i, 8)

    def push_queries(i):
        target = nth_target(i)
        push(q_send.at[target], q_recv.at[me], q_ssem, q_rsem.at[group], target)

    def push_keys(i):
        target = nth_target(i)
        push(kv_send.at[target], kv_recv.at[me], kv_ssem, kv_rsem.at[group], target)

    loop(64, push_queries)
    loop(64, push_keys)

    row = lax.broadcasted_iota(jnp.int32, (256, 128), 0)
    utt = lax.rem(row, 4)
    limit = jnp.where(
        utt < 2,
        jnp.where(utt == 0, lengths[0], lengths[1]),
        jnp.where(utt == 2, lengths[2], lengths[3]),
    )
    mask[...] = jnp.where(me * 64 + row // 4 < limit, 1.0, 0.0)
    loads[1].wait()

    def take_cotangent(i):
        four = jnp.concatenate([gbuf[i * 4 + n].astype(F32) for n in range(4)], axis=0)
        rows = aligned(i * 16, 16)
        cotangent[rows, :] = (four * jnp.tile(mask[rows, :], (1, 8))).astype(BF16)

    loop(16, take_cotangent)
    loads[2].wait()

    def lift_back(i):
        cols = aligned(i * 256, 256)
        act_grad[:, cols] = dot_t(cotangent[...], down_w[cols, :])

    loop(4, lift_back)
    loads[3].wait()

    def take_residual(i):
        both = jnp.concatenate([rbuf[i * 2 + n].astype(F32) for n in range(2)], axis=0)
        hidden[aligned(i * 8, 8), :] = both

    loop(32, take_residual)
    loads[4].wait()
    loads[5].wait()

    def clear(i):
        rows = aligned(i * 512, 512)
        running[rows, :] = jnp.full((512, 128), -1e30, F32)
        totals[rows, :] = jnp.zeros((512, 128), F32)

    loop(8, clear)
    half = lane_ids((256, 128))

    def take_queries(i):
        src = lax.rem(group - i + 8, 8)
        eight = aligned(src * 8, 8)
        pltpu.make_async_copy(q_recv.at[eight], q_recv.at[eight], q_rsem.at[src]).wait()
        query = q_recv[eight].reshape(256, 128).astype(F32) * (0.125 * LOG2E)
        high = query.astype(BF16).astype(F32)
        rest = query - high
        one = jnp.where(half == 0, 1.0, 0.0)
        early = jnp.where(half < 64, high, pltpu.roll(rest, 64, 1))
        late = jnp.where(half < 64, pltpu.roll(high, 64, 1), rest)
        queries[aligned(src * 512, 512), :] = jnp.concatenate(
            [jnp.concatenate([early, one], axis=1), jnp.concatenate([late, one], axis=1)], axis=0
        ).astype(BF16)

    loop(8, take_queries)
    length = lengths[me // 16]

    def with_keys(i, finish):
        src = lax.rem(group - i + 8, 8)
        eight = aligned(src * 8, 8)
        pltpu.make_async_copy(kv_recv.at[eight], kv_recv.at[eight], kv_rsem.at[src]).wait()
        kv = kv_recv[eight].reshape(512, 128).astype(F32)
        lane = lane_ids((512, 128))
        frame = src * 512 + lax.broadcasted_iota(jnp.int32, (512, 128), 0)
        keys[:, :128] = jnp.where(lane < 64, kv, pltpu.roll(kv, 64, 1)).astype(BF16)
        keys[:, 128:] = jnp.where((lane == 0) & (frame >= length), -30000.0, 0.0).astype(BF16)
        values[...] = jnp.where(lane < 64, 1.0, kv).astype(BF16)

        def block_of(n):
            return aligned(lax.rem(group - n + 8, 8) * 512, 512)

        now = dot_t(queries[block_of(0), :], keys[...])
        for n in range(8):
            later = dot_t(queries[block_of(n + 1), :], keys[...]) if n < 7 else None
            rows = block_of(n)
            highest = running[rows, :]
            top = jnp.maximum(highest, jnp.max(now, axis=1, keepdims=True))
            probs = jnp.exp2(now - jnp.tile(top, (1, 4))).astype(BF16)
            total = totals[rows, :] * jnp.exp2(highest - top) + dot(probs, values[...])
            if finish is None:
                running[rows, :] = top
                totals[rows, :] = total
            else:
                finish(n, total)
            now = later

    loop(7, lambda i: with_keys(i, None))

    def reply(n, total):
        src = lax.rem(group - n + 8, 8)
        normed = total / pltpu.roll(total, 64, 1)
        result = jnp.where(half < 64, pltpu.roll(normed[:256], 64, 1), normed[256:])
        o_send[aligned(src * 8, 8)] = result.astype(BF16).reshape(8, 32, 128)

        def push_one(item):
            target = src * 8 + lax.rem(place.z + item, 8)
            push(o_send.at[target], o_recv.at[me], o_ssem, o_rsem.at[group], target)

        loop(8, push_one)

    with_keys(7, reply)

    def gather(i):
        src = lax.rem(group + i, 8)
        eight = aligned(src * 8, 8)
        pltpu.make_async_copy(o_recv.at[eight], o_recv.at[eight], o_rsem.at[src]).wait()
        for n in range(4):
            which = src * 4 + n
            utt, duo = which // 8, lax.rem(which, 8)
            left = o_recv[which * 2].astype(F32)
            right = o_recv[which * 2 + 1].astype(F32)
            upper = jnp.where(low32, left, pltpu.roll(right, 64, 1))
            lower = jnp.where(low32, pltpu.roll(left, 64, 1), right)
            rows32[duo, pl.ds(utt, 64, stride=4), :] = jnp.concatenate([upper, lower], axis=0)

    loop(8, gather)
    for tile in range(8):
        context[:, tile * 128 : tile * 128 + 128] = rows32[tile].astype(BF16)

    def project(i):
        cols = aligned(i * 256, 256)
        hidden[:, cols] = hidden[:, cols] + dot(context[...], out_w[:, cols])

    loop(4, project)

    def first_norm(i):
        rows = aligned(i * 16, 16)
        normed, _ = moments(hidden[rows, :])
        normed_one[rows, :] = normed
        scaled_one[rows, :] = (normed * gain_one[...]).astype(BF16)

    loop(16, first_norm)

    def lift(i):
        cols = aligned(i * 256, 256)
        lin = dot(scaled_one[...], up_w[:, cols])
        gated = sigmoid(dot(scaled_one[...], up_w[:, aligned(i * 256 + 1024, 256)]))
        product = (lin * gated * jnp.tile(mask[...], (1, 2))).astype(BF16)
        linear[:, cols] = lin
        gate[:, cols] = gated
        glu[:, cols] = product
        glu_even[pl.ds(64, 256), cols] = product.astype(F32)

    loop(4, lift)
    left_peer, right_peer = (dp, lax.rem(me + 63, 64)), (dp, lax.rem(me + 1, 64))

    def swap_rims(src, slot):
        return [
            mail.send(src.at[pl.ds(192, 64)], before.at[slot], right_peer),
            mail.send(src.at[pl.ds(0, 64)], after.at[slot], left_peer),
        ]

    def take_rims(copies, slot, dst):
        receive(copies)
        dst[pl.ds(0, 64), :] = jnp.where(me > 0, before[slot].astype(F32), 0.0)
        dst[pl.ds(320, 64), :] = jnp.where(me < 63, after[slot].astype(F32), 0.0)

    rims = swap_rims(glu, 0)
    four_later(glu_even, glu_odd, 8, 39)

    def tiles(blocks, body):
        def step(i):
            cols = aligned((i // len(blocks)) * 128, 128)
            which = lax.rem(i, len(blocks))
            block = blocks[0] + which * (blocks[1] - blocks[0])
            body(pl.multiple_of(block * 64, 64), cols)

        loop(8 * len(blocks), step)

    def windows(even, odd, base, cols):
        both = even[pl.ds(base, 192), cols], odd[pl.ds(base, 192), cols]

        def shifted(ahead):
            start = (ahead - ahead % 2) * 4
            return both[ahead % 2][start : start + 64]

        return shifted

    def convolve(base, cols):
        acc = jnp.zeros((64, 128), F32)
        shifted = windows(glu_even, glu_odd, base, cols)
        for j in range(31):
            acc = acc + taps[j : j + 1, cols] * shifted(j + 1)
        conv[pl.ds(base, 64), cols] = acc

    tiles((1, 2), convolve)
    take_rims(rims, 0, glu_even)
    four_later(glu_even, glu_odd, 0, 8)
    four_later(glu_even, glu_odd, 39, 47)
    tiles((0, 3), convolve)
    sums[...] = jnp.zeros_like(sums)

    def second_norm(i):
        rows = aligned(i * 16, 16)
        normed, inverse = moments(conv[rows, :])
        pre = normed * gain_two[...]
        s = sigmoid(pre)
        activated[rows, :] = (pre * s).astype(BF16)
        back = act_grad[rows, :] * s * (1.0 + pre * (1.0 - s))
        weighted = back * normed
        sums[0] += weighted[:8] + weighted[8:]
        q = back * gain_two[...]
        mean_q = jnp.mean(q, axis=-1, keepdims=True)
        mean_qn = jnp.mean(q * normed, axis=-1, keepdims=True)
        result = (inverse * (q - mean_q - normed * mean_qn)).astype(BF16)
        conv_grad[rows, :] = result
        grad_even[pl.ds(rows.start + 64, 16), :] = result.astype(F32)

    loop(16, second_norm)
    rims = swap_rims(conv_grad, 1)

    upper = lax.broadcasted_iota(jnp.int32, (32, 8, 512), 1) < 4
    down_base = mail.reserve(2)

    def down_tile(hi, side):
        cols = aligned(hi * 512 + side * 256, 256)
        tile = t_dot(cotangent[:, cols], activated[...]).reshape(32, 8, 1024)
        first, second = tile[:, :, :512], tile[:, :, 512:]
        even = jnp.where(upper, first, pltpu.roll(second, 4, 1)).astype(BF16)
        odd = jnp.where(upper, pltpu.roll(first, 4, 1), second).astype(BF16)
        for n in range(32):
            at = (n // 16, (n // 4) % 4, 2 * (n % 4))
            down_grads[hi, side, at[0], at[1], at[2]] = even[n]
            down_grads[hi, side, at[0], at[1], at[2] + 1] = odd[n]

    def down_far(hi):
        down_tile(hi, 1 - core)
        pltpu.make_async_remote_copy(
            src_ref=down_grads.at[hi, 1 - core], dst_ref=down_other.at[hi],
            send_sem=ssem.at[down_base + hi], recv_sem=rsem.at[down_base + hi],
            device_id=place.sibling, device_id_type=MESH,
        ).start()

    loop(2, down_far)
    loop(2, lambda hi: down_tile(hi, core))

    for hi in range(2):
        pltpu.make_async_copy(
            down_other.at[hi], down_other.at[hi], rsem.at[down_base + hi]
        ).wait()

    def down_join(i):
        at = (i // 8, core, lax.rem(i // 4, 2), lax.rem(i, 4))
        both = down_grads[at].astype(F32) + down_other[at[0], at[2], at[3]].astype(F32)
        down_grads[at] = both.astype(BF16)

    loop(16, down_join)
    down_sum = Sum(
        place, mail, down_grads.at[:, core], DOWN_PARTS, sum_scratch[15:30], total_out, 1152
    )
    down_sum.first()

    def tap_step(i):
        cols = aligned(i * 128, 128)
        for block in range(4):
            local = grad_even[pl.ds(64 + block * 64, 64), cols]
            shifted = windows(glu_even, glu_odd, block * 64, cols)
            for j in range(31):
                product = local * shifted(j + 1)
                part = jnp.sum(product.reshape(8, 8, 128), axis=0)
                if block == 0:
                    tap_sums[j, :, cols] = part
                else:
                    tap_sums[j, :, cols] += part

    loop(8, tap_step)
    take_rims(rims, 1, grad_even)
    four_later(grad_even, grad_odd, 0, 47)
    down_sum.second()

    def convolve_back(base, cols):
        acc = jnp.zeros((64, 128), F32)
        shifted = windows(grad_even, grad_odd, base, cols)
        for j in range(31):
            acc = acc + taps[j : j + 1, cols] * shifted(31 - j)
        rows = pl.ds(base, 64)
        g = gate[rows, cols]
        acc = acc * mask[rows, :] * g
        lifted_grad[rows, cols] = acc.astype(BF16)
        other_cols = pl.ds(pl.multiple_of(cols.start + 1024, 128), 128)
        lifted_grad[rows, other_cols] = (acc * linear[rows, cols] * (1.0 - g)).astype(BF16)

    tiles((0, 1, 2, 3), convolve_back)
    down_sum.third()

    up_base = mail.reserve(4)
    up_sum = Sum(place, mail, up_grads.at[:, core], UP_PARTS, sum_scratch[:15], total_out, 0)

    def up_tile(hi, lo, side):
        cols = aligned(hi * 1024 + side * 512 + lo * 256, 256)
        return t_dot(lifted_grad[:, cols], scaled_one[...]).reshape(4, 8, 8, 1024)

    def up_far(i):
        hi, lo = i // 2, lax.rem(i, 2)
        up_grads[hi, 1 - core, lo] = up_tile(hi, lo, 1 - core).astype(BF16)
        pltpu.make_async_remote_copy(
            src_ref=up_grads.at[hi, 1 - core, lo], dst_ref=up_other.at[hi, lo],
            send_sem=ssem.at[up_base + i], recv_sem=rsem.at[up_base + i],
            device_id=place.sibling, device_id_type=MESH,
        ).start()

    loop(4, up_far)

    for hi in range(2):

        def up_near(lo):
            tile = up_tile(hi, lo, core)
            arrived = up_other.at[hi, lo]
            pltpu.make_async_copy(arrived, arrived, rsem.at[up_base + hi * 2 + lo]).wait()
            up_grads[hi, core, lo] = (tile + arrived[...].astype(F32)).astype(BF16)

        loop(2, up_near)
        up_sum.first_yz(hi)
    up_sum.first_x()

    def input_tile(i):
        cols = aligned(i * 256, 256)
        product = dot_t(lifted_grad[...], up_w[cols, :]) * normed_one[:, cols]
        sums[1, :, cols] = jnp.sum(product.reshape(32, 8, 256), axis=0)

    loop(4, input_tile)

    rows_33 = [jnp.sum(tap_sums[j], axis=0, keepdims=True) for j in range(31)]
    rows_33 += [jnp.sum(sums[1], axis=0, keepdims=True), jnp.sum(sums[0], axis=0, keepdims=True)]
    small = jnp.concatenate(rows_33 + [jnp.zeros((128 - 33, 1024), F32)], axis=0)
    for tile in range(8):
        turned[pl.ds(tile * 128, 128), :] = small[:, tile * 128 : tile * 128 + 128].T

    def scatter(i):
        at = (i // 4, lax.rem(i // 2, 2), lax.rem(i, 2))
        for n in range(16):
            eight = turned[pl.ds(pl.multiple_of(i * 128 + n * 8, 8), 8), :]
            y, z = n // 4, 2 * (n % 4)
            small_grads[(*at, y, z)] = eight.astype(BF16)
            small_grads[(*at, y, z + 1)] = pltpu.roll(eight, 4, 0).astype(BF16)

    loop(8, scatter)
    small_copy = mail.send(small_grads.at[:, 1 - core], small_other, place.sibling)

    def finish_block(i):
        cols = aligned(i * 256, 256)
        block_out[:, cols] = (hidden[:, cols] + dot(activated[...], down_w[:, cols])).astype(BF16)

    loop(4, finish_block)
    small_copy.wait_recv()

    def small_join(i):
        at = i // 2, lax.rem(i, 2)
        both = small_grads[at[0], core, at[1]].astype(F32) + small_other[at].astype(F32)
        small_grads[at[0], core, at[1]] = both.astype(BF16)

    loop(4, small_join)
    small_sum = Sum(
        place, mail, small_grads.at[:, core], SMALL_PARTS, sum_scratch[30:], total_out, 1024
    )
    small_sum.first()
    down_sum.last()
    up_sum.second()
    small_sum.second()
    up_sum.third()
    small_sum.third()
    up_sum.last()
    small_sum.last()

    mail.close()
    for hi in range(2):
        sent = down_grads.at[hi, 1 - core]
        pltpu.make_async_copy(sent, sent, ssem.at[down_base + hi]).wait()
    for i in range(4):
        sent = up_grads.at[i // 2, 1 - core, i % 2]
        pltpu.make_async_copy(sent, sent, ssem.at[up_base + i]).wait()
    for buf, sem in ((kv_send, kv_ssem), (q_send, q_ssem), (o_send, o_ssem)):
        sent = buf.at[pl.ds(0, 63)]
        pltpu.make_async_copy(sent, sent, sem).wait()


def hand_out_kernel(block, total, block_out, up_grad, down_grad, kernel_grad, one_grad, two_grad):
    def body(i):
        eight = block[aligned(i * 16, 16), :].astype(F32)
        for n in range(4):
            block_out[i * 4 + n] = eight[n * 4 : n * 4 + 4].astype(BF16)

    loop(16, body)
    up_grad[...] = total[:, :1024]
    down = total[:, 1152:1664]
    down_grad[:, :512] = down[:4]
    down_grad[:, 512:] = down[4:]
    small = total[:, 1024:1152]
    kernel_grad[...] = small[:4, :31]
    turned = small.T
    one_grad[...] = turned[31:32, :4]
    two_grad[...] = turned[32:33, :4]


def on_device(
    residual, projections, out_weight, gain_one, up_weight, conv_kernel, gain_two, down_weight,
    lengths, out_grad,
):
    dma = pltpu.SemaphoreType.DMA
    vmem_spec = pl.BlockSpec(memory_space=pltpu.VMEM)
    any_spec = pl.BlockSpec(memory_space=pl.ANY)

    def half(*shape):
        return pltpu.VMEM(shape, BF16)

    def full(*shape):
        return pltpu.VMEM(shape, F32)

    block, total = pl.pallas_call(
        whole_kernel,
        out_shape=(
            jax.ShapeDtypeStruct((256, 1024), BF16),
            jax.ShapeDtypeStruct((8, 1664), F32),
        ),
        in_specs=[any_spec] * 3
        + [pl.BlockSpec(memory_space=pltpu.SMEM)]
        + [vmem_spec] * 3
        + [any_spec] * 3,
        out_specs=(vmem_spec, vmem_spec),
        scratch_shapes=[
            half(64, 4, 3072), half(64, 4, 1024), half(64, 4, 1024), full(24, 256, 128),
            half(64, 64, 128), half(64, 32, 128), half(64, 64, 128), half(64, 32, 128),
            half(64, 32, 128), half(64, 32, 128),
            half(4096, 256), half(512, 256), half(512, 128), full(4096, 128), full(4096, 128),
            half(256, 1024),
            dma, dma, dma, dma, dma((8,)), dma((8,)), dma((8,)),
            half(1024, 1024), half(1024, 2048), half(1024, 1024),
            full(256, 128), full(256, 1024), full(256, 1024), half(256, 1024),
            full(256, 1024), full(256, 1024), half(256, 1024),
            full(384, 1024), full(384, 1024), full(384, 1024), full(384, 1024),
            full(256, 1024), half(256, 1024),
            half(256, 1024), full(256, 1024), half(256, 1024), half(256, 2048),
            half(2, 64, 1024), half(2, 64, 1024),
            full(31, 8, 1024), full(2, 8, 1024), full(1024, 128),
            half(2, 2, 2, 4, 8, 8, 1024), half(2, 2, 2, 4, 8, 8, 512),
            half(2, 2, 2, 4, 8, 8, 128),
            half(2, 2, 4, 8, 8, 1024), half(2, 2, 4, 8, 8, 512), half(2, 2, 4, 8, 8, 128),
            dma((6,)), dma((128,)), dma((128,)),
        ]
        + Sum.scratch(UP_PARTS)
        + Sum.scratch(DOWN_PARTS)
        + Sum.scratch(SMALL_PARTS),
        compiler_params=pltpu.CompilerParams(
            collective_id=1, has_side_effects=True, vmem_limit_bytes=63 << 20
        ),
        name="whole_block",
    )(
        projections, residual, out_grad, lengths, gain_one.reshape(1, 1024),
        gain_two.reshape(1, 1024), conv_kernel, out_weight, up_weight, down_weight,
    )
    outs = pl.pallas_call(
        hand_out_kernel,
        out_shape=(
            jax.ShapeDtypeStruct((64, 4, 1024), BF16),
            jax.ShapeDtypeStruct((8, 1024), F32),
            jax.ShapeDtypeStruct((4, 1024), F32),
            jax.ShapeDtypeStruct((4, 31), F32),
            jax.ShapeDtypeStruct((1, 4), F32),
            jax.ShapeDtypeStruct((1, 4), F32),
        ),
        in_specs=[vmem_spec] * 2,
        out_specs=(vmem_spec,) * 6,
        name="hand_out",
    )(block, total)
    return (*outs[:4], outs[4].reshape(4), outs[5].reshape(4))


def solution(mesh):
    in_specs = (
        P("ctx", "dp", None),
        P("ctx", "dp", None),
        P(),
        P(),
        P(),
        P(),
        P(),
        P(),
        P("dp"),
        P("ctx", "dp", None),
    )
    out_specs = (
        P("ctx", "dp", None),
        P(("dp", "ctx"), None),
        P(("dp", "ctx"), None),
        P(("dp", "ctx"), None),
        P(("dp", "ctx")),
        P(("dp", "ctx")),
    )
    return jax.shard_map(
        on_device, mesh=mesh, in_specs=in_specs, out_specs=out_specs, check_vma=False
    )
```

```python
import functools

import jax
import jax.numpy as jnp
from jax import lax
from jax.experimental import pallas as pl
from jax.experimental.pallas import tpu as pltpu
from jax.sharding import PartitionSpec as P

EPSILON = 1e-05
LOG2E = 1.4426950408889634
MESH = pl.DeviceIdType.MESH
BF16 = jnp.bfloat16
F32 = jnp.float32

UP_PARTS = ((0, 256), (256, 384), (640, 384))
SMALL_PARTS = ((0, 0), (0, 0), (0, 128))
DOWN_PARTS = ((0, 128), (128, 128), (256, 256))


def lane_ids(shape):
    return lax.broadcasted_iota(jnp.int32, shape, len(shape) - 1)


def dot(a, b):
    return jnp.dot(a, b, preferred_element_type=F32)


def dot_t(a, b):
    return lax.dot_general(a, b, (((1,), (1,)), ((), ())), preferred_element_type=F32)


def t_dot(a, b):
    return lax.dot_general(a, b, (((0,), (0,)), ((), ())), preferred_element_type=F32)


def sigmoid(x):
    return 1.0 / (1.0 + jnp.exp(-x))


def moments(values):
    center = values - jnp.mean(values, axis=-1, keepdims=True)
    inverse = lax.rsqrt(jnp.mean(center * center, axis=-1, keepdims=True) + EPSILON)
    return center * inverse, inverse


def loop(count, body):
    def step(i, carry):
        body(i)
        return carry

    lax.fori_loop(0, count, step, 0)


def aligned(start, size):
    return pl.ds(pl.multiple_of(start, size), size)


class Place:
    def __init__(self):
        dp, ctx = lax.axis_index("dp"), lax.axis_index("ctx")
        self.dp, self.ctx = dp, ctx
        self.x_hi, self.core = dp // 2, lax.rem(dp, 2)
        self.x_lo, self.y, self.z = ctx // 32, lax.rem(ctx // 8, 4), lax.rem(ctx, 8)
        self.sibling = (self.x_hi * 2 + 1 - self.core, ctx)

    def x_split(self, k):
        to = lax.rem(self.x_hi * 2 + self.x_lo + k, 4)
        return to // 2, lax.rem(to, 2)

    def along_x(self, k):
        hi, lo = self.x_split(k)
        return hi * 2 + self.core, lo * 32 + self.y * 8 + self.z

    def along_y(self, k):
        return self.dp, self.x_lo * 32 + lax.rem(self.y + k, 4) * 8 + self.z

    def along_z(self, k):
        return self.dp, self.x_lo * 32 + self.y * 8 + lax.rem(self.z + k, 8)


class Mail:
    def __init__(self, ssem, rsem):
        self.ssem, self.rsem, self.used, self.sent = ssem, rsem, 0, []

    def send(self, src, dst, peer):
        copy = pltpu.make_async_remote_copy(
            src_ref=src, dst_ref=dst, send_sem=self.ssem.at[self.used],
            recv_sem=self.rsem.at[self.used], device_id=peer, device_id_type=MESH,
        )
        copy.start()
        self.used += 1
        self.sent.append(copy)
        return copy

    def reserve(self, count):
        base = self.used
        self.used += count
        return base

    def close(self):
        for copy in self.sent:
            copy.wait_send()


def receive(copies):
    for copy in copies:
        copy.wait_recv()


class Sum:
    def __init__(self, place, mail, mine, parts, scratch, out, offset):
        self.place, self.mail, self.mine, self.out, self.offset = place, mail, mine, out, offset
        self.parts = parts
        self.one_x, self.one_y, self.one_z = [], [], []
        self.z_lanes, self.y_lanes, self.x_lanes = [pl.ds(a, max(n, 1)) for a, n in parts]
        (self.y_in, self.y_sum, self.yx_in, self.yx_sum, self.yxz_in,
         self.x_in, self.x_sum, self.xy_in, self.xy_sum, self.xyz_in,
         self.z_in, self.z_sum, self.zx_in, self.zx_sum, self.zxy_in) = scratch

    @staticmethod
    def scratch(parts):
        wz, wy, wx = [max(n, 128) for _, n in parts]
        shapes = [
            (3, 2, 2, 8, 8, wy), (2, 2, 8, 8, wy), (3, 8, 8, wy), (8, 8, wy), (7, 8, wy),
            (3, 4, 8, 8, wx), (4, 8, 8, wx), (3, 8, 8, wx), (8, 8, wx), (7, 8, wx),
            (7, 2, 2, 4, 8, wz), (2, 2, 4, 8, wz), (3, 4, 8, wz), (4, 8, wz), (3, 8, wz),
        ]
        return [pltpu.VMEM(shape, BF16) for shape in shapes]

    def first(self, halves=(slice(None),)):
        self.one_x, self.one_y, self.one_z = [], [], []
        for at in halves:
            self.first_yz(at)
        self.first_x()

    def first_yz(self, at):
        p, mine, mail = self.place, self.mine, self.mail
        if self.parts[1][1]:
            for k in (1, 2, 3):
                self.one_y.append(
                    mail.send(
                        mine.at[at, :, lax.rem(p.y + k, 4), :, :, self.y_lanes],
                        self.y_in.at[k - 1, at], p.along_y(k),
                    )
                )
        if self.parts[0][1]:
            for k in range(1, 8):
                self.one_z.append(
                    mail.send(
                        mine.at[at, :, :, lax.rem(p.z + k, 8), :, self.z_lanes],
                        self.z_in.at[k - 1, at], p.along_z(k),
                    )
                )

    def first_x(self):
        p, mine, mail = self.place, self.mine, self.mail
        for k in (1, 2, 3):
            hi, lo = p.x_split(k)
            self.one_x.append(
                mail.send(
                    mine.at[hi, lo, :, :, :, self.x_lanes], self.x_in.at[k - 1], p.along_x(k)
                )
            )

    def second(self):
        if self.parts[1][1]:
            self.second_y()
        self.second_x()
        if self.parts[0][1]:
            self.second_z()

    def second_y(self):
        p, mine, mail = self.place, self.mine, self.mail
        receive(self.one_y)

        def y_body(i):
            a, b = i // 2, lax.rem(i, 2)
            acc = mine[a, b, p.y, :, :, self.y_lanes].astype(F32)
            for k in range(3):
                acc = acc + self.y_in[k, a, b].astype(F32)
            self.y_sum[a, b] = acc.astype(BF16)

        loop(4, y_body)
        self.two_y = []
        for k in (1, 2, 3):
            hi, lo = p.x_split(k)
            self.two_y.append(
                mail.send(self.y_sum.at[hi, lo], self.yx_in.at[k - 1], p.along_x(k))
            )

    def second_x(self):
        p, mine, mail = self.place, self.mine, self.mail
        receive(self.one_x)

        def x_body(i):
            acc = mine[p.x_hi, p.x_lo, i, :, :, self.x_lanes].astype(F32)
            for k in range(3):
                acc = acc + self.x_in[k, i].astype(F32)
            self.x_sum[i] = acc.astype(BF16)

        loop(4, x_body)
        self.two_x = [
            mail.send(self.x_sum.at[lax.rem(p.y + k, 4)], self.xy_in.at[k - 1], p.along_y(k))
            for k in (1, 2, 3)
        ]

    def second_z(self):
        p, mine, mail = self.place, self.mine, self.mail
        receive(self.one_z)

        def z_body(i):
            a, b = i // 2, lax.rem(i, 2)
            acc = mine[a, b, :, p.z, :, self.z_lanes].astype(F32)
            for k in range(7):
                acc = acc + self.z_in[k, a, b].astype(F32)
            self.z_sum[a, b] = acc.astype(BF16)

        loop(4, z_body)
        self.two_z = []
        for k in (1, 2, 3):
            hi, lo = p.x_split(k)
            self.two_z.append(
                mail.send(self.z_sum.at[hi, lo], self.zx_in.at[k - 1], p.along_x(k))
            )

    def third(self):
        p, mail = self.place, self.mail

        def add(copies, own, received, dst):
            receive(copies)
            acc = own[...].astype(F32)
            for k in range(3):
                acc = acc + received[k].astype(F32)
            dst[...] = acc.astype(BF16)

        if self.parts[1][1]:
            add(self.two_y, self.y_sum.at[p.x_hi, p.x_lo], self.yx_in, self.yx_sum)
            self.three_y = [
                mail.send(self.yx_sum.at[lax.rem(p.z + k, 8)], self.yxz_in.at[k - 1], p.along_z(k))
                for k in range(1, 8)
            ]
        add(self.two_x, self.x_sum.at[p.y], self.xy_in, self.xy_sum)
        self.three_x = [
            mail.send(self.xy_sum.at[lax.rem(p.z + k, 8)], self.xyz_in.at[k - 1], p.along_z(k))
            for k in range(1, 8)
        ]
        if self.parts[0][1]:
            add(self.two_z, self.z_sum.at[p.x_hi, p.x_lo], self.zx_in, self.zx_sum)
            self.three_z = [
                mail.send(self.zx_sum.at[lax.rem(p.y + k, 4)], self.zxy_in.at[k - 1], p.along_y(k))
                for k in (1, 2, 3)
            ]

    def last(self):
        p = self.place
        steps = [(self.three_x, self.xy_sum.at[p.z], self.xyz_in, 7, self.parts[2])]
        if self.parts[0][1]:
            steps += [
                (self.three_y, self.yx_sum.at[p.z], self.yxz_in, 7, self.parts[1]),
                (self.three_z, self.zx_sum.at[p.y], self.zxy_in, 3, self.parts[0]),
            ]
        for copies, own, received, count, (start, width) in steps:
            receive(copies)
            acc = own[...].astype(F32)
            for k in range(count):
                acc = acc + received[k].astype(F32)
            self.out[:, pl.ds(self.offset + start, width)] = acc


def four_later(src, dst, start, stop):
    def body(i):
        base = pl.multiple_of((start + i) * 8, 8)
        dst[pl.ds(base, 8), :] = jnp.concatenate(
            [src[pl.ds(base, 8), :][4:], src[pl.ds(base + 8, 8), :][:4]], axis=0
        )

    loop(stop - start, body)


def whole_kernel(
    projections, residual, out_grad, lengths, gain_one, gain_two, taps,
    out_w_hbm, up_w_hbm, down_w_hbm,
    block_out, total_out,
    pbuf, rbuf, gbuf, rows32, kv_send, q_send, kv_recv, q_recv, o_send, o_recv,
    queries, keys, values, running, totals, context,
    load_sem, kv_ssem, q_ssem, o_ssem, kv_rsem, q_rsem, o_rsem,
    out_w, up_w, down_w, mask, hidden, normed_one, scaled_one, linear, gate, glu,
    glu_even, glu_odd, grad_even, grad_odd, conv, activated,
    cotangent, act_grad, conv_grad, lifted_grad, before, after, tap_sums, sums, turned,
    up_grads, down_grads, small_grads, up_other, down_other, small_other, wsem, ssem, rsem,
    *sum_scratch,
):
    place = Place()
    mail = Mail(ssem, rsem)
    dp, me, core = place.dp, place.ctx, place.core
    group = me // 8
    loads = []
    for i, (src, dst) in enumerate(
        (
            (projections, pbuf), (out_grad, gbuf), (down_w_hbm, down_w), (residual, rbuf),
            (out_w_hbm, out_w), (up_w_hbm, up_w),
        )
    ):
        copy = pltpu.make_async_copy(src, dst, wsem.at[i])
        copy.start()
        loads.append(copy)
    barrier = pltpu.get_barrier_semaphore()

    def greet(i):
        peer = (dp, lax.rem(me + i + 1, 64))
        pl.semaphore_signal(barrier, inc=1, device_id=peer, device_id_type=MESH)

    loop(63, greet)
    for peer in [place.sibling] + [place.along_x(k) for k in (1, 2, 3)]:
        pl.semaphore_signal(barrier, inc=1, device_id=peer, device_id_type=MESH)
    loads[0].wait()

    def widen(i):
        both = jnp.concatenate([pbuf[i * 2 + n].astype(F32) for n in range(2)], axis=0)
        for tile in range(24):
            rows32[tile, aligned(i * 8, 8), :] = both[:, tile * 128 : tile * 128 + 128]

    loop(32, widen)
    low = lane_ids((64, 128)) < 64
    low32 = lane_ids((32, 128)) < 64

    pl.semaphore_wait(barrier, 67)

    def push(src, dst, send_sem, recv_sem, target):
        @pl.when(target != me)
        def _():
            pltpu.make_async_remote_copy(
                src_ref=src, dst_ref=dst, send_sem=send_sem, recv_sem=recv_sem,
                device_id=(dp, target), device_id_type=MESH,
            ).start()

        @pl.when(target == me)
        def _():
            pltpu.make_async_copy(src, dst, recv_sem).start()

    def pack_and_push(step):
        i = lax.rem(group + step // 4, 8) * 4 + lax.rem(place.z // 2 + step, 4)
        utt, duo = i // 8, lax.rem(i, 8)
        rows = pl.ds(utt, 64, stride=4)
        first, second, third = [rows32[duo * 3 + n, rows, :] for n in range(3)]
        first_t, second_t = pltpu.roll(first, 64, 1), pltpu.roll(second, 64, 1)
        kv_send[i * 2] = jnp.where(low, first_t, second_t).astype(BF16)
        kv_send[i * 2 + 1] = third.astype(BF16)
        q_send[i * 2] = jnp.where(low32, first[:32], first_t[32:]).astype(BF16)
        q_send[i * 2 + 1] = jnp.where(low32, second_t[:32], second[32:]).astype(BF16)
        for side in range(2):
            target = i * 2 + side
            push(q_send.at[target], q_recv.at[me], q_ssem, q_rsem.at[group], target)

    loop(32, pack_and_push)

    def push_keys(i):
        target = lax.rem(group + i // 8, 8) * 8 + lax.rem(place.z + i, 8)
        push(kv_send.at[target], kv_recv.at[me], kv_ssem, kv_rsem.at[group], target)

    loop(64, push_keys)

    row = lax.broadcasted_iota(jnp.int32, (256, 128), 0)
    utt = lax.rem(row, 4)
    limit = jnp.where(
        utt < 2,
        jnp.where(utt == 0, lengths[0], lengths[1]),
        jnp.where(utt == 2, lengths[2], lengths[3]),
    )
    mask[...] = jnp.where(me * 64 + row // 4 < limit, 1.0, 0.0)
    loads[1].wait()

    def take_cotangent(i):
        four = jnp.concatenate([gbuf[i * 4 + n].astype(F32) for n in range(4)], axis=0)
        rows = aligned(i * 16, 16)
        cotangent[rows, :] = (four * jnp.tile(mask[rows, :], (1, 8))).astype(BF16)

    loop(16, take_cotangent)
    loads[2].wait()

    def lift_back(i):
        cols = aligned(i * 256, 256)
        act_grad[:, cols] = dot_t(cotangent[...], down_w[cols, :])

    loop(4, lift_back)
    loads[3].wait()

    def take_residual(i):
        both = jnp.concatenate([rbuf[i * 2 + n].astype(F32) for n in range(2)], axis=0)
        hidden[aligned(i * 8, 8), :] = both

    loop(32, take_residual)
    loads[4].wait()
    loads[5].wait()

    def clear(i):
        rows = aligned(i * 512, 512)
        running[rows, :] = jnp.full((512, 128), -1e30, F32)
        totals[rows, :] = jnp.zeros((512, 128), F32)

    loop(8, clear)
    half = lane_ids((256, 128))

    def take_queries(i):
        src = lax.rem(group - i + 8, 8)
        eight = aligned(src * 8, 8)
        pltpu.make_async_copy(q_recv.at[eight], q_recv.at[eight], q_rsem.at[src]).wait()
        query = q_recv[eight].reshape(256, 128).astype(F32) * (0.125 * LOG2E)
        high = query.astype(BF16).astype(F32)
        rest = query - high
        one = jnp.where(half == 0, 1.0, 0.0)
        early = jnp.where(half < 64, high, pltpu.roll(rest, 64, 1))
        late = jnp.where(half < 64, pltpu.roll(high, 64, 1), rest)
        queries[aligned(src * 512, 512), :] = jnp.concatenate(
            [jnp.concatenate([early, one], axis=1), jnp.concatenate([late, one], axis=1)], axis=0
        ).astype(BF16)

    loop(8, take_queries)
    length = lengths[me // 16]

    def with_keys(i, finish):
        src = lax.rem(group - i + 8, 8)
        eight = aligned(src * 8, 8)
        pltpu.make_async_copy(kv_recv.at[eight], kv_recv.at[eight], kv_rsem.at[src]).wait()
        kv = kv_recv[eight].reshape(512, 128).astype(F32)
        lane = lane_ids((512, 128))
        frame = src * 512 + lax.broadcasted_iota(jnp.int32, (512, 128), 0)
        keys[:, :128] = jnp.where(lane < 64, kv, pltpu.roll(kv, 64, 1)).astype(BF16)
        keys[:, 128:] = jnp.where((lane == 0) & (frame >= length), -30000.0, 0.0).astype(BF16)
        values[...] = jnp.where(lane < 64, 1.0, kv).astype(BF16)

        def block_of(n):
            return aligned(lax.rem(group - n + 8, 8) * 512, 512)

        now = dot_t(queries[block_of(0), :], keys[...])
        for n in range(8):
            later = dot_t(queries[block_of(n + 1), :], keys[...]) if n < 7 else None
            rows = block_of(n)
            highest = running[rows, :]
            top = jnp.maximum(highest, jnp.max(now, axis=1, keepdims=True))
            probs = jnp.exp2(now - jnp.tile(top, (1, 4))).astype(BF16)
            total = totals[rows, :] * jnp.exp2(highest - top) + dot(probs, values[...])
            if finish is None:
                running[rows, :] = top
                totals[rows, :] = total
            else:
                finish(n, total)
            now = later

    loop(7, lambda i: with_keys(i, None))

    def reply(n, total):
        src = lax.rem(group - n + 8, 8)
        normed = total / pltpu.roll(total, 64, 1)
        result = jnp.where(half < 64, pltpu.roll(normed[:256], 64, 1), normed[256:])
        o_send[aligned(src * 8, 8)] = result.astype(BF16).reshape(8, 32, 128)

        def push_one(item):
            target = src * 8 + lax.rem(place.z + item, 8)
            push(o_send.at[target], o_recv.at[me], o_ssem, o_rsem.at[group], target)

        loop(8, push_one)

    with_keys(7, reply)

    def gather(i):
        src = lax.rem(group + i, 8)
        eight = aligned(src * 8, 8)
        pltpu.make_async_copy(o_recv.at[eight], o_recv.at[eight], o_rsem.at[src]).wait()
        for n in range(4):
            which = src * 4 + n
            utt, duo = which // 8, lax.rem(which, 8)
            left = o_recv[which * 2].astype(F32)
            right = o_recv[which * 2 + 1].astype(F32)
            upper = jnp.where(low32, left, pltpu.roll(right, 64, 1))
            lower = jnp.where(low32, pltpu.roll(left, 64, 1), right)
            rows32[duo, pl.ds(utt, 64, stride=4), :] = jnp.concatenate([upper, lower], axis=0)

    loop(8, gather)
    for tile in range(8):
        context[:, tile * 128 : tile * 128 + 128] = rows32[tile].astype(BF16)

    def project(i):
        cols = aligned(i * 512, 512)
        hidden[:, cols] = hidden[:, cols] + dot(context[...], out_w[:, cols])

    loop(2, project)

    def first_norm(i):
        rows = aligned(i * 32, 32)
        normed, _ = moments(hidden[rows, :])
        normed_one[rows, :] = normed
        scaled_one[rows, :] = (normed * gain_one[...]).astype(BF16)

    loop(8, first_norm)

    def lift(i):
        cols = aligned(i * 256, 256)
        lin = dot(scaled_one[...], up_w[:, cols])
        gated = sigmoid(dot(scaled_one[...], up_w[:, aligned(i * 256 + 1024, 256)]))
        product = (lin * gated * jnp.tile(mask[...], (1, 2))).astype(BF16)
        linear[:, cols] = lin
        gate[:, cols] = gated
        glu[:, cols] = product
        glu_even[pl.ds(64, 256), cols] = product.astype(F32)

    loop(4, lift)
    left_peer, right_peer = (dp, lax.rem(me + 63, 64)), (dp, lax.rem(me + 1, 64))

    def swap_rims(src, slot):
        return [
            mail.send(src.at[pl.ds(192, 64)], before.at[slot], right_peer),
            mail.send(src.at[pl.ds(0, 64)], after.at[slot], left_peer),
        ]

    def take_rims(copies, slot, dst):
        receive(copies)
        dst[pl.ds(0, 64), :] = jnp.where(me > 0, before[slot].astype(F32), 0.0)
        dst[pl.ds(320, 64), :] = jnp.where(me < 63, after[slot].astype(F32), 0.0)

    rims = swap_rims(glu, 0)
    four_later(glu_even, glu_odd, 8, 39)

    def tiles(blocks, body):
        def step(i):
            cols = aligned((i // len(blocks)) * 128, 128)
            which = lax.rem(i, len(blocks))
            block = blocks[0] + which * (blocks[1] - blocks[0])
            body(pl.multiple_of(block * 64, 64), cols)

        loop(8 * len(blocks), step)

    def convolve(base, cols):
        acc = jnp.zeros((64, 128), F32)
        for side in range(2):
            window = (glu_even, glu_odd)[side][pl.ds(base, 192), cols]
            for j in range(1 - side, 31, 2):
                start = (j + 1 - side) * 4
                acc = acc + taps[j : j + 1, cols] * window[start : start + 64]
        conv[pl.ds(base, 64), cols] = acc

    tiles((1, 2), convolve)
    take_rims(rims, 0, glu_even)
    four_later(glu_even, glu_odd, 0, 8)
    four_later(glu_even, glu_odd, 39, 47)
    tiles((0, 3), convolve)
    sums[...] = jnp.zeros_like(sums)

    def second_norm(i):
        rows = aligned(i * 32, 32)
        normed, inverse = moments(conv[rows, :])
        pre = normed * gain_two[...]
        s = sigmoid(pre)
        activated[rows, :] = (pre * s).astype(BF16)
        back = act_grad[rows, :] * s * (1.0 + pre * (1.0 - s))
        weighted = back * normed
        sums[0] += jnp.sum(weighted.reshape(4, 8, 1024), axis=0)
        q = back * gain_two[...]
        mean_q = jnp.mean(q, axis=-1, keepdims=True)
        mean_qn = jnp.mean(q * normed, axis=-1, keepdims=True)
        result = (inverse * (q - mean_q - normed * mean_qn)).astype(BF16)
        conv_grad[rows, :] = result
        grad_even[pl.ds(rows.start + 64, 32), :] = result.astype(F32)

    loop(8, second_norm)
    rims = swap_rims(conv_grad, 1)

    upper = lax.broadcasted_iota(jnp.int32, (32, 8, 512), 1) < 4
    down_base = mail.reserve(2)

    def down_tile(hi, side):
        cols = aligned(hi * 512 + side * 256, 256)
        tile = t_dot(cotangent[:, cols], activated[...]).reshape(32, 8, 1024)
        first, second = tile[:, :, :512], tile[:, :, 512:]
        even = jnp.where(upper, first, pltpu.roll(second, 4, 1)).astype(BF16)
        odd = jnp.where(upper, pltpu.roll(first, 4, 1), second).astype(BF16)
        for n in range(32):
            at = (n // 16, (n // 4) % 4, 2 * (n % 4))
            down_grads[hi, side, at[0], at[1], at[2]] = even[n]
            down_grads[hi, side, at[0], at[1], at[2] + 1] = odd[n]

    def down_far(hi):
        down_tile(hi, 1 - core)
        pltpu.make_async_remote_copy(
            src_ref=down_grads.at[hi, 1 - core], dst_ref=down_other.at[hi],
            send_sem=ssem.at[down_base + hi], recv_sem=rsem.at[down_base + hi],
            device_id=place.sibling, device_id_type=MESH,
        ).start()

    loop(2, down_far)
    loop(2, lambda hi: down_tile(hi, core))

    for hi in range(2):
        pltpu.make_async_copy(
            down_other.at[hi], down_other.at[hi], rsem.at[down_base + hi]
        ).wait()

    def down_join(i):
        at = (i // 8, core, lax.rem(i // 4, 2), lax.rem(i, 4))
        both = down_grads[at].astype(F32) + down_other[at[0], at[2], at[3]].astype(F32)
        down_grads[at] = both.astype(BF16)

    loop(16, down_join)
    down_sum = Sum(
        place, mail, down_grads.at[:, core], DOWN_PARTS, sum_scratch[15:30], total_out, 1152
    )
    down_sum.first()

    def tap_step(i):
        cols = aligned(i * 128, 128)
        for block in range(4):
            local = grad_even[pl.ds(64 + block * 64, 64), cols]
            for side in range(2):
                window = (glu_even, glu_odd)[side][pl.ds(block * 64, 192), cols]
                for j in range(1 - side, 31, 2):
                    start = (j + 1 - side) * 4
                    product = local * window[start : start + 64]
                    part = jnp.sum(product.reshape(8, 8, 128), axis=0)
                    if block == 0:
                        tap_sums[j, :, cols] = part
                    else:
                        tap_sums[j, :, cols] += part

    loop(8, tap_step)
    take_rims(rims, 1, grad_even)
    four_later(grad_even, grad_odd, 0, 47)
    down_sum.second()

    def convolve_back(base, cols):
        acc = jnp.zeros((64, 128), F32)
        for side in range(2):
            window = (grad_even, grad_odd)[side][pl.ds(base, 192), cols]
            for j in range(1 - side, 31, 2):
                start = (31 - j - side) * 4
                acc = acc + taps[j : j + 1, cols] * window[start : start + 64]
        rows = pl.ds(base, 64)
        g = gate[rows, cols]
        acc = acc * mask[rows, :] * g
        lifted_grad[rows, cols] = acc.astype(BF16)
        other_cols = pl.ds(pl.multiple_of(cols.start + 1024, 128), 128)
        lifted_grad[rows, other_cols] = (acc * linear[rows, cols] * (1.0 - g)).astype(BF16)

    tiles((0, 1, 2, 3), convolve_back)
    down_sum.third()

    up_base = mail.reserve(4)
    up_sum = Sum(place, mail, up_grads.at[:, core], UP_PARTS, sum_scratch[:15], total_out, 0)

    def up_tile(hi, lo, side):
        cols = aligned(hi * 1024 + side * 512 + lo * 256, 256)
        return t_dot(lifted_grad[:, cols], scaled_one[...]).reshape(4, 8, 8, 1024)

    def up_far(i):
        hi, lo = i // 2, lax.rem(i, 2)
        up_grads[hi, 1 - core, lo] = up_tile(hi, lo, 1 - core).astype(BF16)
        pltpu.make_async_remote_copy(
            src_ref=up_grads.at[hi, 1 - core, lo], dst_ref=up_other.at[hi, lo],
            send_sem=ssem.at[up_base + i], recv_sem=rsem.at[up_base + i],
            device_id=place.sibling, device_id_type=MESH,
        ).start()

    loop(4, up_far)

    for hi in range(2):

        def up_near(lo):
            tile = up_tile(hi, lo, core)
            arrived = up_other.at[hi, lo]
            pltpu.make_async_copy(arrived, arrived, rsem.at[up_base + hi * 2 + lo]).wait()
            up_grads[hi, core, lo] = (tile + arrived[...].astype(F32)).astype(BF16)

        loop(2, up_near)
        up_sum.first_yz(hi)
    up_sum.first_x()

    def input_tile(i):
        cols = aligned(i * 256, 256)
        product = dot_t(lifted_grad[...], up_w[cols, :]) * normed_one[:, cols]
        sums[1, :, cols] = jnp.sum(product.reshape(32, 8, 256), axis=0)

    loop(4, input_tile)

    rows_33 = [jnp.sum(tap_sums[j], axis=0, keepdims=True) for j in range(31)]
    rows_33 += [jnp.sum(sums[1], axis=0, keepdims=True), jnp.sum(sums[0], axis=0, keepdims=True)]
    small = jnp.concatenate(rows_33 + [jnp.zeros((128 - 33, 1024), F32)], axis=0)
    for tile in range(8):
        turned[pl.ds(tile * 128, 128), :] = small[:, tile * 128 : tile * 128 + 128].T

    def scatter(i):
        at = (i // 4, lax.rem(i // 2, 2), lax.rem(i, 2))
        for n in range(16):
            eight = turned[pl.ds(pl.multiple_of(i * 128 + n * 8, 8), 8), :]
            y, z = n // 4, 2 * (n % 4)
            small_grads[(*at, y, z)] = eight.astype(BF16)
            small_grads[(*at, y, z + 1)] = pltpu.roll(eight, 4, 0).astype(BF16)

    loop(8, scatter)
    small_copy = mail.send(small_grads.at[:, 1 - core], small_other, place.sibling)

    def finish_block(i):
        cols = aligned(i * 512, 512)
        block_out[:, cols] = (hidden[:, cols] + dot(activated[...], down_w[:, cols])).astype(BF16)

    loop(2, finish_block)
    small_copy.wait_recv()

    def small_join(i):
        at = i // 2, lax.rem(i, 2)
        both = small_grads[at[0], core, at[1]].astype(F32) + small_other[at].astype(F32)
        small_grads[at[0], core, at[1]] = both.astype(BF16)

    loop(4, small_join)
    small_sum = Sum(
        place, mail, small_grads.at[:, core], SMALL_PARTS, sum_scratch[30:], total_out, 1024
    )
    small_sum.first()
    down_sum.last()
    up_sum.second()
    small_sum.second()
    up_sum.third()
    small_sum.third()
    up_sum.last()
    small_sum.last()

    mail.close()
    for hi in range(2):
        sent = down_grads.at[hi, 1 - core]
        pltpu.make_async_copy(sent, sent, ssem.at[down_base + hi]).wait()
    for i in range(4):
        sent = up_grads.at[i // 2, 1 - core, i % 2]
        pltpu.make_async_copy(sent, sent, ssem.at[up_base + i]).wait()
    for buf, sem in ((kv_send, kv_ssem), (q_send, q_ssem), (o_send, o_ssem)):
        sent = buf.at[pl.ds(0, 63)]
        pltpu.make_async_copy(sent, sent, sem).wait()


def hand_out_kernel(block, total, block_out, up_grad, down_grad, kernel_grad, one_grad, two_grad):
    def body(i):
        eight = block[aligned(i * 16, 16), :].astype(F32)
        for n in range(4):
            block_out[i * 4 + n] = eight[n * 4 : n * 4 + 4].astype(BF16)

    loop(16, body)
    up_grad[...] = total[:, :1024]
    down = total[:, 1152:1664]
    down_grad[:, :512] = down[:4]
    down_grad[:, 512:] = down[4:]
    small = total[:, 1024:1152]
    kernel_grad[...] = small[:4, :31]
    turned = small.T
    one_grad[...] = turned[31:32, :4]
    two_grad[...] = turned[32:33, :4]


def on_device(
    residual, projections, out_weight, gain_one, up_weight, conv_kernel, gain_two, down_weight,
    lengths, out_grad,
):
    dma = pltpu.SemaphoreType.DMA
    vmem_spec = pl.BlockSpec(memory_space=pltpu.VMEM)
    any_spec = pl.BlockSpec(memory_space=pl.ANY)

    def half(*shape):
        return pltpu.VMEM(shape, BF16)

    def full(*shape):
        return pltpu.VMEM(shape, F32)

    block, total = pl.pallas_call(
        whole_kernel,
        out_shape=(
            jax.ShapeDtypeStruct((256, 1024), BF16),
            jax.ShapeDtypeStruct((8, 1664), F32),
        ),
        in_specs=[any_spec] * 3
        + [pl.BlockSpec(memory_space=pltpu.SMEM)]
        + [vmem_spec] * 3
        + [any_spec] * 3,
        out_specs=(vmem_spec, vmem_spec),
        scratch_shapes=[
            half(64, 4, 3072), half(64, 4, 1024), half(64, 4, 1024), full(24, 256, 128),
            half(64, 64, 128), half(64, 32, 128), half(64, 64, 128), half(64, 32, 128),
            half(64, 32, 128), half(64, 32, 128),
            half(4096, 256), half(512, 256), half(512, 128), full(4096, 128), full(4096, 128),
            half(256, 1024),
            dma, dma, dma, dma, dma((8,)), dma((8,)), dma((8,)),
            half(1024, 1024), half(1024, 2048), half(1024, 1024),
            full(256, 128), full(256, 1024), full(256, 1024), half(256, 1024),
            full(256, 1024), full(256, 1024), half(256, 1024),
            full(384, 1024), full(384, 1024), full(384, 1024), full(384, 1024),
            full(256, 1024), half(256, 1024),
            half(256, 1024), full(256, 1024), half(256, 1024), half(256, 2048),
            half(2, 64, 1024), half(2, 64, 1024),
            full(31, 8, 1024), full(2, 8, 1024), full(1024, 128),
            half(2, 2, 2, 4, 8, 8, 1024), half(2, 2, 2, 4, 8, 8, 512),
            half(2, 2, 2, 4, 8, 8, 128),
            half(2, 2, 4, 8, 8, 1024), half(2, 2, 4, 8, 8, 512), half(2, 2, 4, 8, 8, 128),
            dma((6,)), dma((128,)), dma((128,)),
        ]
        + Sum.scratch(UP_PARTS)
        + Sum.scratch(DOWN_PARTS)
        + Sum.scratch(SMALL_PARTS),
        compiler_params=pltpu.CompilerParams(
            collective_id=1, has_side_effects=True, vmem_limit_bytes=63 << 20
        ),
        name="whole_block",
    )(
        projections, residual, out_grad, lengths, gain_one.reshape(1, 1024),
        gain_two.reshape(1, 1024), conv_kernel, out_weight, up_weight, down_weight,
    )
    outs = pl.pallas_call(
        hand_out_kernel,
        out_shape=(
            jax.ShapeDtypeStruct((64, 4, 1024), BF16),
            jax.ShapeDtypeStruct((8, 1024), F32),
            jax.ShapeDtypeStruct((4, 1024), F32),
            jax.ShapeDtypeStruct((4, 31), F32),
            jax.ShapeDtypeStruct((1, 4), F32),
            jax.ShapeDtypeStruct((1, 4), F32),
        ),
        in_specs=[vmem_spec] * 2,
        out_specs=(vmem_spec,) * 6,
        name="hand_out",
    )(block, total)
    return (*outs[:4], outs[4].reshape(4), outs[5].reshape(4))


def solution(mesh):
    in_specs = (
        P("ctx", "dp", None),
        P("ctx", "dp", None),
        P(),
        P(),
        P(),
        P(),
        P(),
        P(),
        P("dp"),
        P("ctx", "dp", None),
    )
    out_specs = (
        P("ctx", "dp", None),
        P(("dp", "ctx"), None),
        P(("dp", "ctx"), None),
        P(("dp", "ctx"), None),
        P(("dp", "ctx")),
        P(("dp", "ctx")),
    )
    return jax.shard_map(
        on_device, mesh=mesh, in_specs=in_specs, out_specs=out_specs, check_vma=False
    )
```

```python
import functools

import jax
import jax.numpy as jnp
from jax import lax
from jax.experimental import pallas as pl
from jax.experimental.pallas import tpu as pltpu
from jax.sharding import PartitionSpec as P

EPSILON = 1e-05
LOG2E = 1.4426950408889634
MESH = pl.DeviceIdType.MESH
BF16 = jnp.bfloat16
F32 = jnp.float32

UP_PARTS = ((0, 256), (256, 384), (640, 384))
SMALL_PARTS = ((0, 0), (0, 0), (0, 128))
DOWN_PARTS = ((0, 128), (128, 128), (256, 256))


def lane_ids(shape):
    return lax.broadcasted_iota(jnp.int32, shape, len(shape) - 1)


def dot(a, b):
    return jnp.dot(a, b, preferred_element_type=F32)


def dot_t(a, b):
    return lax.dot_general(a, b, (((1,), (1,)), ((), ())), preferred_element_type=F32)


def t_dot(a, b):
    return lax.dot_general(a, b, (((0,), (0,)), ((), ())), preferred_element_type=F32)


def sigmoid(x):
    return 1.0 / (1.0 + jnp.exp(-x))


def moments(values):
    center = values - jnp.mean(values, axis=-1, keepdims=True)
    inverse = lax.rsqrt(jnp.mean(center * center, axis=-1, keepdims=True) + EPSILON)
    return center * inverse, inverse


def loop(count, body):
    def step(i, carry):
        body(i)
        return carry

    lax.fori_loop(0, count, step, 0)


def aligned(start, size):
    return pl.ds(pl.multiple_of(start, size), size)


class Place:
    def __init__(self):
        dp, ctx = lax.axis_index("dp"), lax.axis_index("ctx")
        self.dp, self.ctx = dp, ctx
        self.x_hi, self.core = dp // 2, lax.rem(dp, 2)
        self.x_lo, self.y, self.z = ctx // 32, lax.rem(ctx // 8, 4), lax.rem(ctx, 8)
        self.sibling = (self.x_hi * 2 + 1 - self.core, ctx)

    def x_split(self, k):
        to = lax.rem(self.x_hi * 2 + self.x_lo + k, 4)
        return to // 2, lax.rem(to, 2)

    def along_x(self, k):
        hi, lo = self.x_split(k)
        return hi * 2 + self.core, lo * 32 + self.y * 8 + self.z

    def along_y(self, k):
        return self.dp, self.x_lo * 32 + lax.rem(self.y + k, 4) * 8 + self.z

    def along_z(self, k):
        return self.dp, self.x_lo * 32 + self.y * 8 + lax.rem(self.z + k, 8)


class Mail:
    def __init__(self, ssem, rsem):
        self.ssem, self.rsem, self.used, self.sent = ssem, rsem, 0, []

    def send(self, src, dst, peer):
        copy = pltpu.make_async_remote_copy(
            src_ref=src, dst_ref=dst, send_sem=self.ssem.at[self.used],
            recv_sem=self.rsem.at[self.used], device_id=peer, device_id_type=MESH,
        )
        copy.start()
        self.used += 1
        self.sent.append(copy)
        return copy

    def reserve(self, count):
        base = self.used
        self.used += count
        return base

    def close(self):
        for copy in self.sent:
            copy.wait_send()


def receive(copies):
    for copy in copies:
        copy.wait_recv()


class Sum:
    def __init__(self, place, mail, mine, parts, scratch, out, offset):
        self.place, self.mail, self.mine, self.out, self.offset = place, mail, mine, out, offset
        self.parts = parts
        self.one_x, self.one_y, self.one_z = [], [], []
        self.z_lanes, self.y_lanes, self.x_lanes = [pl.ds(a, max(n, 1)) for a, n in parts]
        (self.y_in, self.y_sum, self.yx_in, self.yx_sum, self.yxz_in,
         self.x_in, self.x_sum, self.xy_in, self.xy_sum, self.xyz_in,
         self.z_in, self.z_sum, self.zx_in, self.zx_sum, self.zxy_in) = scratch

    @staticmethod
    def scratch(parts):
        wz, wy, wx = [max(n, 128) for _, n in parts]
        shapes = [
            (3, 2, 2, 8, 8, wy), (2, 2, 8, 8, wy), (3, 8, 8, wy), (8, 8, wy), (7, 8, wy),
            (3, 4, 8, 8, wx), (4, 8, 8, wx), (3, 8, 8, wx), (8, 8, wx), (7, 8, wx),
            (7, 2, 2, 4, 8, wz), (2, 2, 4, 8, wz), (3, 4, 8, wz), (4, 8, wz), (3, 8, wz),
        ]
        return [pltpu.VMEM(shape, BF16) for shape in shapes]

    def first(self, halves=(slice(None),)):
        self.one_x, self.one_y, self.one_z = [], [], []
        for at in halves:
            self.first_yz(at)
        self.first_x()

    def first_yz(self, at):
        p, mine, mail = self.place, self.mine, self.mail
        if self.parts[1][1]:
            for k in (1, 2, 3):
                self.one_y.append(
                    mail.send(
                        mine.at[at, :, lax.rem(p.y + k, 4), :, :, self.y_lanes],
                        self.y_in.at[k - 1, at], p.along_y(k),
                    )
                )
        if self.parts[0][1]:
            for k in range(1, 8):
                self.one_z.append(
                    mail.send(
                        mine.at[at, :, :, lax.rem(p.z + k, 8), :, self.z_lanes],
                        self.z_in.at[k - 1, at], p.along_z(k),
                    )
                )

    def first_x(self):
        p, mine, mail = self.place, self.mine, self.mail
        for k in (1, 2, 3):
            hi, lo = p.x_split(k)
            self.one_x.append(
                mail.send(
                    mine.at[hi, lo, :, :, :, self.x_lanes], self.x_in.at[k - 1], p.along_x(k)
                )
            )

    def second(self):
        if self.parts[1][1]:
            self.second_y()
        self.second_x()
        if self.parts[0][1]:
            self.second_z()

    def second_y(self):
        p, mine, mail = self.place, self.mine, self.mail
        receive(self.one_y)

        def y_body(i):
            a, b = i // 2, lax.rem(i, 2)
            acc = mine[a, b, p.y, :, :, self.y_lanes].astype(F32)
            for k in range(3):
                acc = acc + self.y_in[k, a, b].astype(F32)
            self.y_sum[a, b] = acc.astype(BF16)

        loop(4, y_body)
        self.two_y = []
        for k in (1, 2, 3):
            hi, lo = p.x_split(k)
            self.two_y.append(
                mail.send(self.y_sum.at[hi, lo], self.yx_in.at[k - 1], p.along_x(k))
            )

    def second_x(self):
        p, mine, mail = self.place, self.mine, self.mail
        receive(self.one_x)

        def x_body(i):
            acc = mine[p.x_hi, p.x_lo, i, :, :, self.x_lanes].astype(F32)
            for k in range(3):
                acc = acc + self.x_in[k, i].astype(F32)
            self.x_sum[i] = acc.astype(BF16)

        loop(4, x_body)
        self.two_x = [
            mail.send(self.x_sum.at[lax.rem(p.y + k, 4)], self.xy_in.at[k - 1], p.along_y(k))
            for k in (1, 2, 3)
        ]

    def second_z(self):
        p, mine, mail = self.place, self.mine, self.mail
        receive(self.one_z)

        def z_body(i):
            a, b = i // 2, lax.rem(i, 2)
            acc = mine[a, b, :, p.z, :, self.z_lanes].astype(F32)
            for k in range(7):
                acc = acc + self.z_in[k, a, b].astype(F32)
            self.z_sum[a, b] = acc.astype(BF16)

        loop(4, z_body)
        self.two_z = []
        for k in (1, 2, 3):
            hi, lo = p.x_split(k)
            self.two_z.append(
                mail.send(self.z_sum.at[hi, lo], self.zx_in.at[k - 1], p.along_x(k))
            )

    def third(self):
        p, mail = self.place, self.mail

        def add(copies, own, received, dst):
            receive(copies)
            acc = own[...].astype(F32)
            for k in range(3):
                acc = acc + received[k].astype(F32)
            dst[...] = acc.astype(BF16)

        if self.parts[1][1]:
            add(self.two_y, self.y_sum.at[p.x_hi, p.x_lo], self.yx_in, self.yx_sum)
            self.three_y = [
                mail.send(self.yx_sum.at[lax.rem(p.z + k, 8)], self.yxz_in.at[k - 1], p.along_z(k))
                for k in range(1, 8)
            ]
        add(self.two_x, self.x_sum.at[p.y], self.xy_in, self.xy_sum)
        self.three_x = [
            mail.send(self.xy_sum.at[lax.rem(p.z + k, 8)], self.xyz_in.at[k - 1], p.along_z(k))
            for k in range(1, 8)
        ]
        if self.parts[0][1]:
            add(self.two_z, self.z_sum.at[p.x_hi, p.x_lo], self.zx_in, self.zx_sum)
            self.three_z = [
                mail.send(self.zx_sum.at[lax.rem(p.y + k, 4)], self.zxy_in.at[k - 1], p.along_y(k))
                for k in (1, 2, 3)
            ]

    def last(self):
        p = self.place
        steps = [(self.three_x, self.xy_sum.at[p.z], self.xyz_in, 7, self.parts[2])]
        if self.parts[0][1]:
            steps += [
                (self.three_y, self.yx_sum.at[p.z], self.yxz_in, 7, self.parts[1]),
                (self.three_z, self.zx_sum.at[p.y], self.zxy_in, 3, self.parts[0]),
            ]
        for copies, own, received, count, (start, width) in steps:
            receive(copies)
            acc = own[...].astype(F32)
            for k in range(count):
                acc = acc + received[k].astype(F32)
            self.out[:, pl.ds(self.offset + start, width)] = acc


def four_later(src, dst, start, stop):
    def body(i):
        base = pl.multiple_of((start + i) * 8, 8)
        dst[pl.ds(base, 8), :] = jnp.concatenate(
            [src[pl.ds(base, 8), :][4:], src[pl.ds(base + 8, 8), :][:4]], axis=0
        )

    loop(stop - start, body)


def whole_kernel(
    projections, residual, out_grad, lengths, gain_one, gain_two, taps,
    out_w_hbm, up_w_hbm, down_w_hbm,
    block_out, total_out,
    pbuf, rbuf, gbuf, rows32, kv_send, q_send, kv_recv, q_recv, o_send, o_recv,
    queries, keys, values, running, totals, context,
    load_sem, kv_ssem, q_ssem, o_ssem, kv_rsem, q_rsem, o_rsem,
    out_w, up_w, down_w, mask, hidden, normed_one, scaled_one, linear, gate, glu,
    glu_even, glu_odd, grad_even, grad_odd, conv, activated,
    cotangent, act_grad, conv_grad, lifted_grad, before, after, tap_sums, sums, turned,
    up_grads, down_grads, small_grads, up_other, down_other, small_other, wsem, ssem, rsem,
    *sum_scratch,
):
    place = Place()
    mail = Mail(ssem, rsem)
    dp, me, core = place.dp, place.ctx, place.core
    group = me // 8
    loads = []
    for i, (src, dst) in enumerate(
        (
            (projections, pbuf), (out_grad, gbuf), (down_w_hbm, down_w), (residual, rbuf),
            (out_w_hbm, out_w), (up_w_hbm, up_w),
        )
    ):
        copy = pltpu.make_async_copy(src, dst, wsem.at[i])
        copy.start()
        loads.append(copy)
    barrier = pltpu.get_barrier_semaphore()

    def greet(i):
        peer = (dp, lax.rem(me + i + 1, 64))
        pl.semaphore_signal(barrier, inc=1, device_id=peer, device_id_type=MESH)

    loop(63, greet)
    for peer in [place.sibling] + [place.along_x(k) for k in (1, 2, 3)]:
        pl.semaphore_signal(barrier, inc=1, device_id=peer, device_id_type=MESH)
    loads[0].wait()

    def widen(i):
        both = jnp.concatenate([pbuf[i * 2 + n].astype(F32) for n in range(2)], axis=0)
        for tile in range(24):
            rows32[tile, aligned(i * 8, 8), :] = both[:, tile * 128 : tile * 128 + 128]

    loop(32, widen)
    low = lane_ids((64, 128)) < 64
    low32 = lane_ids((32, 128)) < 64

    pl.semaphore_wait(barrier, 67)

    def push(src, dst, send_sem, recv_sem, target):
        @pl.when(target != me)
        def _():
            pltpu.make_async_remote_copy(
                src_ref=src, dst_ref=dst, send_sem=send_sem, recv_sem=recv_sem,
                device_id=(dp, target), device_id_type=MESH,
            ).start()

        @pl.when(target == me)
        def _():
            pltpu.make_async_copy(src, dst, recv_sem).start()

    def pack_and_push(step):
        i = lax.rem(group + step // 4, 8) * 4 + lax.rem(place.z // 2 + step, 4)
        utt, duo = i // 8, lax.rem(i, 8)
        rows = pl.ds(utt, 64, stride=4)
        first, second, third = [rows32[duo * 3 + n, rows, :] for n in range(3)]
        first_t, second_t = pltpu.roll(first, 64, 1), pltpu.roll(second, 64, 1)
        kv_send[i * 2] = jnp.where(low, first_t, second_t).astype(BF16)
        kv_send[i * 2 + 1] = third.astype(BF16)
        q_send[i * 2] = jnp.where(low32, first[:32], first_t[32:]).astype(BF16)
        q_send[i * 2 + 1] = jnp.where(low32, second_t[:32], second[32:]).astype(BF16)
        for side in range(2):
            target = i * 2 + side
            push(q_send.at[target], q_recv.at[me], q_ssem, q_rsem.at[group], target)

    loop(32, pack_and_push)

    def push_keys(i):
        target = lax.rem(group + i // 8, 8) * 8 + lax.rem(place.z + i, 8)
        push(kv_send.at[target], kv_recv.at[me], kv_ssem, kv_rsem.at[group], target)

    loop(64, push_keys)

    row = lax.broadcasted_iota(jnp.int32, (256, 128), 0)
    utt = lax.rem(row, 4)
    limit = jnp.where(
        utt < 2,
        jnp.where(utt == 0, lengths[0], lengths[1]),
        jnp.where(utt == 2, lengths[2], lengths[3]),
    )
    mask[...] = jnp.where(me * 64 + row // 4 < limit, 1.0, 0.0)
    loads[1].wait()

    def take_cotangent(i):
        four = jnp.concatenate([gbuf[i * 4 + n].astype(F32) for n in range(4)], axis=0)
        rows = aligned(i * 16, 16)
        cotangent[rows, :] = (four * jnp.tile(mask[rows, :], (1, 8))).astype(BF16)

    loop(16, take_cotangent)
    loads[2].wait()

    def lift_back(i):
        cols = aligned(i * 256, 256)
        act_grad[:, cols] = dot_t(cotangent[...], down_w[cols, :])

    loop(4, lift_back)
    loads[3].wait()

    def take_residual(i):
        both = jnp.concatenate([rbuf[i * 2 + n].astype(F32) for n in range(2)], axis=0)
        hidden[aligned(i * 8, 8), :] = both

    loop(32, take_residual)
    loads[4].wait()
    loads[5].wait()

    def clear(i):
        rows = aligned(i * 512, 512)
        running[rows, :] = jnp.full((512, 128), -1e30, F32)
        totals[rows, :] = jnp.zeros((512, 128), F32)

    loop(8, clear)
    half = lane_ids((256, 128))

    def take_queries(i):
        src = lax.rem(group - i + 8, 8)
        eight = aligned(src * 8, 8)
        pltpu.make_async_copy(q_recv.at[eight], q_recv.at[eight], q_rsem.at[src]).wait()
        query = q_recv[eight].reshape(256, 128).astype(F32) * (0.125 * LOG2E)
        high = query.astype(BF16).astype(F32)
        rest = query - high
        one = jnp.where(half == 0, 1.0, 0.0)
        early = jnp.where(half < 64, high, pltpu.roll(rest, 64, 1))
        late = jnp.where(half < 64, pltpu.roll(high, 64, 1), rest)
        queries[aligned(src * 512, 512), :] = jnp.concatenate(
            [jnp.concatenate([early, one], axis=1), jnp.concatenate([late, one], axis=1)], axis=0
        ).astype(BF16)

    loop(8, take_queries)
    length = lengths[me // 16]

    def with_keys(i, finish):
        src = lax.rem(group - i + 8, 8)
        eight = aligned(src * 8, 8)
        pltpu.make_async_copy(kv_recv.at[eight], kv_recv.at[eight], kv_rsem.at[src]).wait()
        kv = kv_recv[eight].reshape(512, 128).astype(F32)
        lane = lane_ids((512, 128))
        frame = src * 512 + lax.broadcasted_iota(jnp.int32, (512, 128), 0)
        keys[:, :128] = jnp.where(lane < 64, kv, pltpu.roll(kv, 64, 1)).astype(BF16)
        keys[:, 128:] = jnp.where((lane == 0) & (frame >= length), -30000.0, 0.0).astype(BF16)
        values[...] = jnp.where(lane < 64, 1.0, kv).astype(BF16)

        def block_of(n):
            return aligned(lax.rem(group - n + 8, 8) * 512, 512)

        now = dot_t(queries[block_of(0), :], keys[...])
        for n in range(8):
            later = dot_t(queries[block_of(n + 1), :], keys[...]) if n < 7 else None
            rows = block_of(n)
            highest = running[rows, :]
            top = jnp.maximum(highest, jnp.max(now, axis=1, keepdims=True))
            probs = jnp.exp2(now - jnp.tile(top, (1, 4))).astype(BF16)
            total = totals[rows, :] * jnp.exp2(highest - top) + dot(probs, values[...])
            if finish is None:
                running[rows, :] = top
                totals[rows, :] = total
            else:
                finish(n, total)
            now = later

    loop(7, lambda i: with_keys(i, None))

    def reply(n, total):
        src = lax.rem(group - n + 8, 8)
        normed = total / pltpu.roll(total, 64, 1)
        result = jnp.where(half < 64, pltpu.roll(normed[:256], 64, 1), normed[256:])
        o_send[aligned(src * 8, 8)] = result.astype(BF16).reshape(8, 32, 128)

        def push_one(item):
            target = src * 8 + lax.rem(place.z + item, 8)
            push(o_send.at[target], o_recv.at[me], o_ssem, o_rsem.at[group], target)

        loop(8, push_one)

    with_keys(7, reply)

    def gather(i):
        src = lax.rem(group + i, 8)
        eight = aligned(src * 8, 8)
        pltpu.make_async_copy(o_recv.at[eight], o_recv.at[eight], o_rsem.at[src]).wait()
        for n in range(4):
            which = src * 4 + n
            utt, duo = which // 8, lax.rem(which, 8)
            left = o_recv[which * 2].astype(F32)
            right = o_recv[which * 2 + 1].astype(F32)
            upper = jnp.where(low32, left, pltpu.roll(right, 64, 1))
            lower = jnp.where(low32, pltpu.roll(left, 64, 1), right)
            rows32[duo, pl.ds(utt, 64, stride=4), :] = jnp.concatenate([upper, lower], axis=0)

    loop(8, gather)
    for tile in range(8):
        context[:, tile * 128 : tile * 128 + 128] = rows32[tile].astype(BF16)

    def project(i):
        cols = aligned(i * 512, 512)
        hidden[:, cols] = hidden[:, cols] + dot(context[...], out_w[:, cols])

    loop(2, project)

    def first_norm(i):
        rows = aligned(i * 32, 32)
        normed, _ = moments(hidden[rows, :])
        normed_one[rows, :] = normed
        scaled_one[rows, :] = (normed * gain_one[...]).astype(BF16)

    loop(8, first_norm)

    def lift(i):
        cols = aligned(i * 512, 512)
        lin = dot(scaled_one[...], up_w[:, cols])
        gated = sigmoid(dot(scaled_one[...], up_w[:, aligned(i * 512 + 1024, 512)]))
        product = (lin * gated * jnp.tile(mask[...], (1, 4))).astype(BF16)
        linear[:, cols] = lin
        gate[:, cols] = gated
        glu[:, cols] = product
        glu_even[pl.ds(64, 256), cols] = product.astype(F32)

    loop(2, lift)
    left_peer, right_peer = (dp, lax.rem(me + 63, 64)), (dp, lax.rem(me + 1, 64))

    def swap_rims(src, slot):
        return [
            mail.send(src.at[pl.ds(192, 64)], before.at[slot], right_peer),
            mail.send(src.at[pl.ds(0, 64)], after.at[slot], left_peer),
        ]

    def take_rims(copies, slot, dst):
        receive(copies)
        dst[pl.ds(0, 64), :] = jnp.where(me > 0, before[slot].astype(F32), 0.0)
        dst[pl.ds(320, 64), :] = jnp.where(me < 63, after[slot].astype(F32), 0.0)

    rims = swap_rims(glu, 0)
    four_later(glu_even, glu_odd, 8, 39)

    def tiles(blocks, body):
        def step(i):
            cols = aligned((i // len(blocks)) * 128, 128)
            which = lax.rem(i, len(blocks))
            block = blocks[0] + which * (blocks[1] - blocks[0])
            body(pl.multiple_of(block * 64, 64), cols)

        loop(8 * len(blocks), step)

    def convolve(base, cols):
        acc = jnp.zeros((64, 128), F32)
        for side in range(2):
            window = (glu_even, glu_odd)[side][pl.ds(base, 192), cols]
            for j in range(1 - side, 31, 2):
                start = (j + 1 - side) * 4
                acc = acc + taps[j : j + 1, cols] * window[start : start + 64]
        conv[pl.ds(base, 64), cols] = acc

    tiles((1, 2), convolve)
    take_rims(rims, 0, glu_even)
    four_later(glu_even, glu_odd, 0, 8)
    four_later(glu_even, glu_odd, 39, 47)
    tiles((0, 3), convolve)
    sums[...] = jnp.zeros_like(sums)

    def second_norm(i):
        rows = aligned(i * 32, 32)
        normed, inverse = moments(conv[rows, :])
        pre = normed * gain_two[...]
        s = sigmoid(pre)
        activated[rows, :] = (pre * s).astype(BF16)
        back = act_grad[rows, :] * s * (1.0 + pre * (1.0 - s))
        weighted = back * normed
        sums[0] += jnp.sum(weighted.reshape(4, 8, 1024), axis=0)
        q = back * gain_two[...]
        mean_q = jnp.mean(q, axis=-1, keepdims=True)
        mean_qn = jnp.mean(q * normed, axis=-1, keepdims=True)
        result = (inverse * (q - mean_q - normed * mean_qn)).astype(BF16)
        conv_grad[rows, :] = result
        grad_even[pl.ds(rows.start + 64, 32), :] = result.astype(F32)

    loop(8, second_norm)
    rims = swap_rims(conv_grad, 1)

    upper = lax.broadcasted_iota(jnp.int32, (32, 8, 512), 1) < 4
    down_base = mail.reserve(2)

    def down_tile(hi, side):
        cols = aligned(hi * 512 + side * 256, 256)
        tile = t_dot(cotangent[:, cols], activated[...]).reshape(32, 8, 1024)
        first, second = tile[:, :, :512], tile[:, :, 512:]
        even = jnp.where(upper, first, pltpu.roll(second, 4, 1)).astype(BF16)
        odd = jnp.where(upper, pltpu.roll(first, 4, 1), second).astype(BF16)
        for n in range(32):
            at = (n // 16, (n // 4) % 4, 2 * (n % 4))
            down_grads[hi, side, at[0], at[1], at[2]] = even[n]
            down_grads[hi, side, at[0], at[1], at[2] + 1] = odd[n]

    def down_far(hi):
        down_tile(hi, 1 - core)
        pltpu.make_async_remote_copy(
            src_ref=down_grads.at[hi, 1 - core], dst_ref=down_other.at[hi],
            send_sem=ssem.at[down_base + hi], recv_sem=rsem.at[down_base + hi],
            device_id=place.sibling, device_id_type=MESH,
        ).start()

    loop(2, down_far)
    loop(2, lambda hi: down_tile(hi, core))

    for hi in range(2):
        pltpu.make_async_copy(
            down_other.at[hi], down_other.at[hi], rsem.at[down_base + hi]
        ).wait()

    def down_join(i):
        at = (i // 8, core, lax.rem(i // 4, 2), lax.rem(i, 4))
        both = down_grads[at].astype(F32) + down_other[at[0], at[2], at[3]].astype(F32)
        down_grads[at] = both.astype(BF16)

    loop(16, down_join)
    down_sum = Sum(
        place, mail, down_grads.at[:, core], DOWN_PARTS, sum_scratch[15:30], total_out, 1152
    )
    down_sum.first()

    def tap_step(i):
        cols = aligned(i * 128, 128)
        for block in range(4):
            local = grad_even[pl.ds(64 + block * 64, 64), cols]
            for side in range(2):
                window = (glu_even, glu_odd)[side][pl.ds(block * 64, 192), cols]
                for j in range(1 - side, 31, 2):
                    start = (j + 1 - side) * 4
                    product = local * window[start : start + 64]
                    part = jnp.sum(product.reshape(8, 8, 128), axis=0)
                    if block == 0:
                        tap_sums[j, :, cols] = part
                    else:
                        tap_sums[j, :, cols] += part

    loop(8, tap_step)
    take_rims(rims, 1, grad_even)
    four_later(grad_even, grad_odd, 0, 47)
    down_sum.second()

    def convolve_back(base, cols):
        acc = jnp.zeros((64, 128), F32)
        for side in range(2):
            window = (grad_even, grad_odd)[side][pl.ds(base, 192), cols]
            for j in range(1 - side, 31, 2):
                start = (31 - j - side) * 4
                acc = acc + taps[j : j + 1, cols] * window[start : start + 64]
        rows = pl.ds(base, 64)
        g = gate[rows, cols]
        acc = acc * mask[rows, :] * g
        lifted_grad[rows, cols] = acc.astype(BF16)
        other_cols = pl.ds(pl.multiple_of(cols.start + 1024, 128), 128)
        lifted_grad[rows, other_cols] = (acc * linear[rows, cols] * (1.0 - g)).astype(BF16)

    tiles((0, 1, 2, 3), convolve_back)
    down_sum.third()

    up_base = mail.reserve(4)
    up_sum = Sum(place, mail, up_grads.at[:, core], UP_PARTS, sum_scratch[:15], total_out, 0)

    def up_tile(hi, lo, side):
        cols = aligned(hi * 1024 + side * 512 + lo * 256, 256)
        return t_dot(lifted_grad[:, cols], scaled_one[...]).reshape(4, 8, 8, 1024)

    def up_far(i):
        hi, lo = i // 2, lax.rem(i, 2)
        up_grads[hi, 1 - core, lo] = up_tile(hi, lo, 1 - core).astype(BF16)
        pltpu.make_async_remote_copy(
            src_ref=up_grads.at[hi, 1 - core, lo], dst_ref=up_other.at[hi, lo],
            send_sem=ssem.at[up_base + i], recv_sem=rsem.at[up_base + i],
            device_id=place.sibling, device_id_type=MESH,
        ).start()

    loop(4, up_far)

    for hi in range(2):

        def up_near(lo):
            tile = up_tile(hi, lo, core)
            arrived = up_other.at[hi, lo]
            pltpu.make_async_copy(arrived, arrived, rsem.at[up_base + hi * 2 + lo]).wait()
            up_grads[hi, core, lo] = (tile + arrived[...].astype(F32)).astype(BF16)

        loop(2, up_near)
        up_sum.first_yz(hi)
    up_sum.first_x()

    def input_tile(i):
        cols = aligned(i * 512, 512)
        product = dot_t(lifted_grad[...], up_w[cols, :]) * normed_one[:, cols]
        sums[1, :, cols] = jnp.sum(product.reshape(32, 8, 512), axis=0)

    loop(2, input_tile)

    rows_33 = [jnp.sum(tap_sums[j], axis=0, keepdims=True) for j in range(31)]
    rows_33 += [jnp.sum(sums[1], axis=0, keepdims=True), jnp.sum(sums[0], axis=0, keepdims=True)]
    small = jnp.concatenate(rows_33 + [jnp.zeros((128 - 33, 1024), F32)], axis=0)
    for tile in range(8):
        turned[pl.ds(tile * 128, 128), :] = small[:, tile * 128 : tile * 128 + 128].T

    def scatter(i):
        at = (i // 4, lax.rem(i // 2, 2), lax.rem(i, 2))
        for n in range(16):
            eight = turned[pl.ds(pl.multiple_of(i * 128 + n * 8, 8), 8), :]
            y, z = n // 4, 2 * (n % 4)
            small_grads[(*at, y, z)] = eight.astype(BF16)
            small_grads[(*at, y, z + 1)] = pltpu.roll(eight, 4, 0).astype(BF16)

    loop(8, scatter)
    small_copy = mail.send(small_grads.at[:, 1 - core], small_other, place.sibling)

    def finish_block(i):
        cols = aligned(i * 512, 512)
        block_out[:, cols] = (hidden[:, cols] + dot(activated[...], down_w[:, cols])).astype(BF16)

    loop(2, finish_block)
    small_copy.wait_recv()

    def small_join(i):
        at = i // 2, lax.rem(i, 2)
        both = small_grads[at[0], core, at[1]].astype(F32) + small_other[at].astype(F32)
        small_grads[at[0], core, at[1]] = both.astype(BF16)

    loop(4, small_join)
    small_sum = Sum(
        place, mail, small_grads.at[:, core], SMALL_PARTS, sum_scratch[30:], total_out, 1024
    )
    small_sum.first()
    down_sum.last()
    up_sum.second()
    small_sum.second()
    up_sum.third()
    small_sum.third()
    up_sum.last()
    small_sum.last()

    mail.close()
    for hi in range(2):
        sent = down_grads.at[hi, 1 - core]
        pltpu.make_async_copy(sent, sent, ssem.at[down_base + hi]).wait()
    for i in range(4):
        sent = up_grads.at[i // 2, 1 - core, i % 2]
        pltpu.make_async_copy(sent, sent, ssem.at[up_base + i]).wait()
    for buf, sem in ((kv_send, kv_ssem), (q_send, q_ssem), (o_send, o_ssem)):
        sent = buf.at[pl.ds(0, 63)]
        pltpu.make_async_copy(sent, sent, sem).wait()


def hand_out_kernel(block, total, block_out, up_grad, down_grad, kernel_grad, one_grad, two_grad):
    def body(i):
        eight = block[aligned(i * 16, 16), :].astype(F32)
        for n in range(4):
            block_out[i * 4 + n] = eight[n * 4 : n * 4 + 4].astype(BF16)

    loop(16, body)
    up_grad[...] = total[:, :1024]
    down = total[:, 1152:1664]
    down_grad[:, :512] = down[:4]
    down_grad[:, 512:] = down[4:]
    small = total[:, 1024:1152]
    kernel_grad[...] = small[:4, :31]
    turned = small.T
    one_grad[...] = turned[31:32, :4]
    two_grad[...] = turned[32:33, :4]


def on_device(
    residual, projections, out_weight, gain_one, up_weight, conv_kernel, gain_two, down_weight,
    lengths, out_grad,
):
    dma = pltpu.SemaphoreType.DMA
    vmem_spec = pl.BlockSpec(memory_space=pltpu.VMEM)
    any_spec = pl.BlockSpec(memory_space=pl.ANY)

    def half(*shape):
        return pltpu.VMEM(shape, BF16)

    def full(*shape):
        return pltpu.VMEM(shape, F32)

    block, total = pl.pallas_call(
        whole_kernel,
        out_shape=(
            jax.ShapeDtypeStruct((256, 1024), BF16),
            jax.ShapeDtypeStruct((8, 1664), F32),
        ),
        in_specs=[any_spec] * 3
        + [pl.BlockSpec(memory_space=pltpu.SMEM)]
        + [vmem_spec] * 3
        + [any_spec] * 3,
        out_specs=(vmem_spec, vmem_spec),
        scratch_shapes=[
            half(64, 4, 3072), half(64, 4, 1024), half(64, 4, 1024), full(24, 256, 128),
            half(64, 64, 128), half(64, 32, 128), half(64, 64, 128), half(64, 32, 128),
            half(64, 32, 128), half(64, 32, 128),
            half(4096, 256), half(512, 256), half(512, 128), full(4096, 128), full(4096, 128),
            half(256, 1024),
            dma, dma, dma, dma, dma((8,)), dma((8,)), dma((8,)),
            half(1024, 1024), half(1024, 2048), half(1024, 1024),
            full(256, 128), full(256, 1024), full(256, 1024), half(256, 1024),
            full(256, 1024), full(256, 1024), half(256, 1024),
            full(384, 1024), full(384, 1024), full(384, 1024), full(384, 1024),
            full(256, 1024), half(256, 1024),
            half(256, 1024), full(256, 1024), half(256, 1024), half(256, 2048),
            half(2, 64, 1024), half(2, 64, 1024),
            full(31, 8, 1024), full(2, 8, 1024), full(1024, 128),
            half(2, 2, 2, 4, 8, 8, 1024), half(2, 2, 2, 4, 8, 8, 512),
            half(2, 2, 2, 4, 8, 8, 128),
            half(2, 2, 4, 8, 8, 1024), half(2, 2, 4, 8, 8, 512), half(2, 2, 4, 8, 8, 128),
            dma((6,)), dma((128,)), dma((128,)),
        ]
        + Sum.scratch(UP_PARTS)
        + Sum.scratch(DOWN_PARTS)
        + Sum.scratch(SMALL_PARTS),
        compiler_params=pltpu.CompilerParams(
            collective_id=1, has_side_effects=True, vmem_limit_bytes=63 << 20
        ),
        name="whole_block",
    )(
        projections, residual, out_grad, lengths, gain_one.reshape(1, 1024),
        gain_two.reshape(1, 1024), conv_kernel, out_weight, up_weight, down_weight,
    )
    outs = pl.pallas_call(
        hand_out_kernel,
        out_shape=(
            jax.ShapeDtypeStruct((64, 4, 1024), BF16),
            jax.ShapeDtypeStruct((8, 1024), F32),
            jax.ShapeDtypeStruct((4, 1024), F32),
            jax.ShapeDtypeStruct((4, 31), F32),
            jax.ShapeDtypeStruct((1, 4), F32),
            jax.ShapeDtypeStruct((1, 4), F32),
        ),
        in_specs=[vmem_spec] * 2,
        out_specs=(vmem_spec,) * 6,
        name="hand_out",
    )(block, total)
    return (*outs[:4], outs[4].reshape(4), outs[5].reshape(4))


def solution(mesh):
    in_specs = (
        P("ctx", "dp", None),
        P("ctx", "dp", None),
        P(),
        P(),
        P(),
        P(),
        P(),
        P(),
        P("dp"),
        P("ctx", "dp", None),
    )
    out_specs = (
        P("ctx", "dp", None),
        P(("dp", "ctx"), None),
        P(("dp", "ctx"), None),
        P(("dp", "ctx"), None),
        P(("dp", "ctx")),
        P(("dp", "ctx")),
    )
    return jax.shard_map(
        on_device, mesh=mesh, in_specs=in_specs, out_specs=out_specs, check_vma=False
    )
```
